256 devices in a mesh: sec: 2 (over z_lo), dev: 64 (over x, z_hi, y), rep: 2 (over core).
Axes of the slice: x: 4, y: 4, z: 8 (z_hi: 4, z_lo: 2; z = z_hi * 2 + z_lo), core: 2. Of those that a mesh axis runs over, the one named last changes fastest.
Arguments:
- resid: bfloat16 [16384, 4096], P(('rep', 'dev')), parts along dimension 0, may hold values from -27 to 27
- queries: bfloat16 [16384, 4096], P(('rep', 'dev'), 'sec'), parts along dimension 0, may hold values from -30 to 30
- keys: bfloat16 [16384, 1024], P(('rep', 'dev'), 'sec'), parts along dimension 0, may hold values from -6 to 6
- values: bfloat16 [16384, 1024], P(('rep', 'dev'), 'sec'), parts along dimension 0, may hold values from -6 to 6
- norm_gain: float32 [4096], replicated, may hold values from 0.1 to 1.9
- expert_ids: int32 [16384, 2], P(('rep', 'dev')), parts along dimension 0, may hold values from 0 to 31, all different within a row; in each aligned block of 128 rows (0 to 127, 128 to 255, ...) at most 10 rows name the same one
- gate_weights: float32 [16384, 2], P(('rep', 'dev')), parts along dimension 0, may hold values from 0.2 to 1
- w_gate: bfloat16 [64, 4096, 768], P('dev', None, 'sec'), may hold values from -0.09375 to 0.09375
- w_up: bfloat16 [64, 4096, 768], P('dev', None, 'sec'), may hold values from -0.09375 to 0.09375
- w_down: bfloat16 [64, 768, 4096], P('dev', 'sec'), may hold values from -0.15625 to 0.15625
Outputs:
- out: bfloat16 [16384, 4096], P(('rep', 'dev'), 'sec'), parts along dimension 0
The draws below stay inside these ranges and needn't reach their ends.
There are 2 independent parts, one for each index of `rep`. The reference program is written for one: setup_inputs(seed, part) draws one part's arguments, and reference() takes and returns one part's arrays. A program takes and returns all parts, laid end to end along the dimension named above; an argument that names none is the same for every part. Nothing has to cross between parts.
Inputs may be any that keep to these rules, and one draw needn't show every extreme that they name: `expert_ids`: each token names 2 different experts; among the tokens of one index of dev no expert is named more than 10 times.
All inputs are finite; a program needn't handle non-finite values.
Results may differ from the reference program's by a relative error of at most 0.008.
Values may be sent and summed in bfloat16 or wider, within the bound.
A program may use at most 128 MiB of HBM per device.

```python
import math
import jax
import jax.numpy as jnp
import numpy as np
from jax import lax

D = 4096
HEADS = 32
KV = 8
HD = 128
FF = 1536
TOPK = 2
TOK_DEV = 128
TOKENS = 8192
EXPERTS = 32
CAP = 10
N_DEV = 64


def draw_keys(key, part):
    noise_key = jax.random.fold_in(key, 23)
    result = jnp.clip(jax.random.normal(noise_key, (TOKENS, KV, HD), jnp.float32), -6.0, 6.0)
    return result.reshape(TOKENS, KV * HD).astype(jnp.bfloat16)


def draw_queries(key, part):
    noise_key = jax.random.fold_in(key, 29)
    group_size = HEADS // KV
    result = jnp.clip(3.0 * jax.random.normal(noise_key, (TOKENS, KV, group_size, HD), jnp.float32), -12.0, 12.0)
    return result.reshape(TOKENS, HEADS * HD).astype(jnp.bfloat16)


def draw_resid(key, part):
    base_key = jax.random.fold_in(key, 31)
    noise_key, row_key, column_key = jax.random.split(base_key, 3)
    low_log = math.log(0.3)
    high_log = math.log(3.0)
    row_scale = jnp.exp(jax.random.uniform(row_key, (TOKENS, 1), jnp.float32, low_log, high_log))
    column_scale = jnp.exp(jax.random.uniform(column_key, (1, D), jnp.float32, low_log, high_log))
    base_draw = jnp.clip(jax.random.normal(noise_key, (TOKENS, D), jnp.float32), -3.0, 3.0)
    return (base_draw * row_scale * column_scale).astype(jnp.bfloat16)


def steps_of(key, shape, cuts, smallest, top_value):
    factor_of = 1.0
    for position, parts in cuts:
        draws = jax.random.uniform(jax.random.fold_in(jax.random.fold_in(key, 6), position), (parts,), jnp.float32, smallest / len(cuts), top_value / len(cuts))
        factor_of = factor_of * jnp.repeat(jnp.exp(draws), shape[position] // parts).reshape((-1,) + (1,) * (len(shape) - 1 - position))
    return factor_of


def deal_out(own_key, own, number, rows, count, top, reach, skew):
    order = jax.random.permutation(own_key, count)
    packed, ordinary = portions_of(count, rows * top, reach, skew, True), portions_of(count, rows * top, reach, skew, False)
    places = jnp.arange(count)

    def named(lengths, turn):
        used = int((lengths > 0).sum())
        fixed = max(1, used // 4)
        moved = fixed + (places - fixed + turn * (used - fixed)) % max(1, count - fixed)
        return jnp.zeros((count,), jnp.int32).at[order[jnp.where(places < fixed, places, moved)]].set(jnp.asarray(lengths, jnp.int32))

    lengths = jnp.where(number % 4 == 0, named(packed, number // 4), named(ordinary, number - number // 4 - 1))
    mixed = jax.random.permutation(jax.random.fold_in(own, 3), count)
    source_of, taker = mixed[0:count // 2 * 2:2], mixed[1:count // 2 * 2:2]
    margin = jnp.minimum(lengths[source_of] - 1, reach - lengths[taker]) // 2
    margin = jnp.where((source_of == order[0]) | (taker == order[0]) | (lengths[taker] == 0), 0, jnp.maximum(margin, 0))
    moved = jax.random.randint(jax.random.fold_in(own, 4), (count // 2,), 0, 1 << 20) % (margin + 1)
    lengths = lengths.at[source_of].add(-moved).at[taker].add(moved)
    labels = jnp.searchsorted(jnp.cumsum(lengths), jnp.arange(rows * top), side="right").astype(jnp.int32)
    listing = labels.reshape(top, rows).T
    listing = listing[jax.random.permutation(jax.random.fold_in(own, 1), rows)]
    turn = jax.random.randint(jax.random.fold_in(own, 2), (rows, 1), 0, top)
    return jnp.take_along_axis(listing, (jnp.arange(top)[None, :] + turn) % top, axis=1)


def portions_of(count, total, most, lean, full):
    loads = [(1 << 20) // math.isqrt(rank ** lean) + 1 for rank in range(1, count + 1)]
    largest = most if full else min(most, max(-(-total // count), total * loads[0] // sum(loads)))
    least = 1 if total - largest >= count - 1 else 0
    holding, rest = [largest] + [least] * (count - 1), total - largest - least * (count - 1)
    while rest > 0:
        movable = [i for i in range(1, count) if holding[i] < largest] or [i for i in range(1, count) if holding[i] < most]
        pool, remaining = sum([loads[i] for i in movable]), rest
        for i in movable:
            extra = min(most - holding[i], max(1, remaining * loads[i] // pool), rest)
            holding[i] = holding[i] + extra
            rest = rest - extra
    return np.array(holding)


def centred(stream_key, dims, scale, limit, cuts=(), kind=jnp.bfloat16):
    values = scale * jax.random.normal(stream_key, dims, jnp.float32)
    if cuts:
        values = values * steps_of(stream_key, dims, cuts, -0.22, 0.18)
    return jnp.clip(values, -limit, limit).astype(kind)


def setup_inputs(seed: int = 0, part: int = 0) -> dict:
    key_of = jax.random.split(jax.random.key(seed), 11)
    part_splits = jax.random.split(jax.random.fold_in(key_of[10], part), 11)
    resid = draw_resid(jax.random.fold_in(jax.random.fold_in(key_of[10], part), 71), part)
    queries = draw_queries(jax.random.fold_in(jax.random.fold_in(key_of[10], part), 71), part)
    keys = draw_keys(jax.random.fold_in(jax.random.fold_in(key_of[10], part), 71), part)
    values = centred(part_splits[3], (TOKENS, KV * HD), 1.0, 6.0, ((0, 64), (1, 2)))
    norm_gain = jnp.clip(1.0 + 0.18 * jax.random.normal(key_of[4], (D,), jnp.float32), 0.1, 1.9)
    expert_ids_keys = jax.random.split(jax.random.fold_in(part_splits[5], 1), TOKENS // TOK_DEV)
    expert_ids_turns = jax.random.permutation(jax.random.fold_in(part_splits[5], 3), TOKENS // TOK_DEV)
    expert_ids = jax.vmap(lambda own, number: deal_out(jax.random.fold_in(part_splits[5], 2), own, number, TOK_DEV, EXPERTS, TOPK, CAP, 2))(expert_ids_keys, expert_ids_turns).reshape((TOKENS, TOPK))
    gate_weights = jnp.clip(0.2 + 0.8 * jax.random.uniform(part_splits[6], (TOKENS, TOPK), jnp.float32) ** steps_of(part_splits[6], (TOKENS, TOPK), ((0, 64),), -0.2, 0.2), 0.2, 1.0)
    w_gate = centred(key_of[7], (2 * EXPERTS, D, FF // 2), D ** -0.5, 0.09375, ((0, 64), (2, 2)))
    w_up = centred(key_of[8], (2 * EXPERTS, D, FF // 2), D ** -0.5, 0.09375, ((0, 64), (2, 2)))
    w_down = centred(key_of[9], (2 * EXPERTS, FF // 2, D), FF ** -0.5, 0.15625, ((0, 64), (1, 2)))
    return {"resid": resid, "queries": queries, "keys": keys, "values": values, "norm_gain": norm_gain, "expert_ids": expert_ids, "gate_weights": gate_weights, "w_gate": w_gate, "w_up": w_up, "w_down": w_down}


def attend_all(queries, keys, values):
    group_size = HEADS // KV
    block_rows = min(TOKENS, 1024)
    score_scale = 1.0 / math.sqrt(HD)
    query_heads = queries.reshape(TOKENS, HEADS, HD)
    key_heads = keys.reshape(TOKENS, KV, HD)
    value_heads = values.reshape(TOKENS, KV, HD)

    def one_head(head_index):
        kv_index = head_index // group_size
        query_one = lax.dynamic_index_in_dim(query_heads, head_index, 1, keepdims=False)
        key_one = lax.dynamic_index_in_dim(key_heads, kv_index, 1, keepdims=False)
        value_one = lax.dynamic_index_in_dim(value_heads, kv_index, 1, keepdims=False)

        def one_block(query_block):
            scores = jnp.dot(query_block, key_one.T, preferred_element_type=jnp.float32) * score_scale
            row_max = lax.optimization_barrier(jnp.max(scores, axis=1, keepdims=True))
            raised = jnp.exp(scores - row_max)
            row_total = lax.optimization_barrier(jnp.sum(raised, axis=1, keepdims=True))
            mixed = jnp.dot(raised.astype(jnp.bfloat16), value_one, preferred_element_type=jnp.float32)
            return mixed / row_total
        blocks = query_one.reshape(TOKENS // block_rows, block_rows, HD)
        return lax.map(one_block, blocks).reshape(TOKENS, HD)
    gathered_heads = lax.map(one_head, jnp.arange(HEADS, dtype=jnp.int32))
    return jnp.transpose(gathered_heads, (1, 0, 2)).reshape(TOKENS, HEADS * HD).astype(jnp.bfloat16)

def experts_all(normed, expert_ids, gate_weights, w_gate, w_up, w_down):
    flat_ids = expert_ids.reshape(-1).astype(jnp.int32)
    sort_order = jnp.argsort(flat_ids, stable=True).astype(jnp.int32)
    sorted_ids = flat_ids[sort_order]
    expert_range = jnp.arange(EXPERTS, dtype=jnp.int32)
    starts = jnp.searchsorted(sorted_ids, expert_range).astype(jnp.int32)
    counts = lax.optimization_barrier(jnp.sum((flat_ids[:, None] == expert_range[None, :]).astype(jnp.int32), axis=0))
    slot_limit = N_DEV * CAP
    tokens_pad = jnp.concatenate([(sort_order // TOPK).astype(jnp.int32), jnp.zeros((slot_limit,), jnp.int32)])
    gates_pad = jnp.concatenate([gate_weights.reshape(-1)[sort_order], jnp.zeros((slot_limit,), jnp.float32)])
    quarter = FF // 4

    def one_expert(running, expert):
        start_at = starts[expert]
        rows_at = lax.dynamic_slice_in_dim(tokens_pad, start_at, slot_limit)
        weight = lax.dynamic_slice_in_dim(gates_pad, start_at, slot_limit)
        live = jnp.arange(slot_limit, dtype=jnp.int32) < counts[expert]
        weight = jnp.where(live, weight, 0.0)
        picked = normed[rows_at]
        result = jnp.zeros((slot_limit, D), jnp.float32)
        for half_index in range(2):
            shard = 2 * expert + half_index
            gate_shard = lax.dynamic_index_in_dim(w_gate, shard, 0, keepdims=False)
            up_shard = lax.dynamic_index_in_dim(w_up, shard, 0, keepdims=False)
            down_shard = lax.dynamic_index_in_dim(w_down, shard, 0, keepdims=False)
            for section in range(2):
                low = section * quarter
                gate_out = jnp.dot(picked, gate_shard[:, low:low + quarter], preferred_element_type=jnp.float32)
                up_out = jnp.dot(picked, up_shard[:, low:low + quarter], preferred_element_type=jnp.float32)
                activation = (jax.nn.silu(gate_out) * up_out).astype(jnp.bfloat16)
                partial_out = jnp.dot(activation, down_shard[low:low + quarter, :], preferred_element_type=jnp.float32).astype(jnp.bfloat16)
                result = result + partial_out.astype(jnp.float32)
        return (running.at[rows_at].add(result * weight[:, None]), None)
    moe_sum, _ = lax.scan(one_expert, jnp.zeros((TOKENS, D), jnp.float32), expert_range)
    return moe_sum

def reference(resid, queries, keys, values, norm_gain, expert_ids, gate_weights, w_gate, w_up, w_down):
    attended = attend_all(queries, keys, values)
    stream = resid.astype(jnp.float32) + attended.astype(jnp.float32)
    normed = (stream * lax.rsqrt(lax.optimization_barrier(jnp.mean(stream * stream, axis=-1, keepdims=True)) + 1e-06) * norm_gain).astype(jnp.bfloat16)
    moe_sum = experts_all(normed, expert_ids, gate_weights, w_gate, w_up, w_down)
    return (stream + moe_sum).astype(jnp.bfloat16)
```

```python
import math

import jax
import jax.numpy as jnp
from jax import lax
from jax.experimental import pallas as pl
from jax.experimental.pallas import tpu as pltpu
from jax.sharding import PartitionSpec as P

HD = 128
MESH = pl.DeviceIdType.MESH
F32 = jnp.float32
BF16 = jnp.bfloat16
VMEM_BYTES = 58 * 1024 * 1024
ANY = pl.BlockSpec(memory_space=pl.ANY)
VMEM = pl.BlockSpec(memory_space=pltpu.VMEM)


def rcopy(src, dst, send_sem, recv_sem, device_id):
    return pltpu.make_async_remote_copy(
        src_ref=src,
        dst_ref=dst,
        send_sem=send_sem,
        recv_sem=recv_sem,
        device_id=device_id,
        device_id_type=MESH,
    )


def coords():
    me = lax.axis_index("dev")
    return me, me // 16, (me // 4) % 4, me % 4


def gather_kernel(q_ref, k_ref, v_ref, qo_ref, kv_ref, s1, r1, sq, rq, sa1, ra1, sb1, rb1, sa2, ra2, sb2, rb2, lsem):
    me, x, zh, y = coords()
    pos = x * 4 + y

    def at(xx, zz, yy):
        return {"dev": xx * 16 + zz * 4 + yy}

    barrier = pltpu.get_barrier_semaphore()
    for d in range(1, 4):
        for peer in (at((x + d) % 4, zh, y), at(x, (zh + d) % 4, y), at(x, zh, (y + d) % 4)):
            pl.semaphore_signal(barrier, inc=1, device_id=peer, device_id_type=MESH)
    pl.semaphore_wait(barrier, 9)

    def cols(j, w):
        return pl.ds(pl.multiple_of(j * w, w), w)

    first = []
    for d in range(1, 4):
        j = (zh + d) % 4
        first.append(rcopy(k_ref.at[:, cols(j, HD)], kv_ref.at[pos, zh, 0], s1.at[d - 1, 0], r1.at[d - 1, 0], at(x, j, y)))
        first.append(rcopy(v_ref.at[:, cols(j, HD)], kv_ref.at[pos, zh, 1], s1.at[d - 1, 1], r1.at[d - 1, 1], at(x, j, y)))
    for c in first:
        c.start()
    own = [
        pltpu.make_async_copy(k_ref.at[:, cols(zh, HD)], kv_ref.at[pos, zh, 0], lsem.at[0]),
        pltpu.make_async_copy(v_ref.at[:, cols(zh, HD)], kv_ref.at[pos, zh, 1], lsem.at[1]),
        pltpu.make_async_copy(q_ref.at[:, cols(zh, 4 * HD)], qo_ref.at[zh], lsem.at[2]),
    ]
    for c in own:
        c.start()
    qs = []
    for d in range(1, 4):
        j = (zh + d) % 4
        qs.append(rcopy(q_ref.at[:, cols(j, 4 * HD)], qo_ref.at[zh], sq.at[d - 1], rq.at[d - 1], at(x, j, y)))
    for c in qs:
        c.start()
    own[0].wait()
    own[1].wait()
    for d in range(1, 4):
        src = (zh + 4 - d) % 4
        for w in range(2):
            rcopy(kv_ref.at[pos, src, w], kv_ref.at[pos, src, w], s1.at[d - 1, w], r1.at[d - 1, w], at(x, src, y)).wait_recv()

    def half(p, h):
        return kv_ref.at[p, pl.ds(2 * h, 2)]

    sends = []

    def go(c):
        c.start()
        sends.append(c)

    for d in range(1, 4):
        go(rcopy(half(pos, 0), half(pos, 0), sa1.at[d - 1], ra1.at[d - 1], at((x + d) % 4, zh, y)))
        go(rcopy(half(pos, 1), half(pos, 1), sb1.at[d - 1], rb1.at[d - 1], at(x, zh, (y + d) % 4)))
    for d in range(1, 4):
        go(rcopy(half(pos, 0), half(pos, 0), sa2.at[0, d - 1], ra2.at[0, d - 1], at(x, zh, (y + d) % 4)))
        go(rcopy(half(pos, 1), half(pos, 1), sb2.at[0, d - 1], rb2.at[0, d - 1], at((x + d) % 4, zh, y)))
    for e in (1, 3, 2):
        xs = (x + 4 - e) % 4
        ys = (y + 4 - e) % 4
        pa = xs * 4 + y
        pb = x * 4 + ys
        rcopy(half(pa, 0), half(pa, 0), sa1.at[e - 1], ra1.at[e - 1], at(xs, zh, y)).wait_recv()
        for d in range(1, 4):
            go(rcopy(half(pa, 0), half(pa, 0), sa2.at[e, d - 1], ra2.at[e, d - 1], at(x, zh, (y + d) % 4)))
        rcopy(half(pb, 1), half(pb, 1), sb1.at[e - 1], rb1.at[e - 1], at(x, zh, ys)).wait_recv()
        for d in range(1, 4):
            go(rcopy(half(pb, 1), half(pb, 1), sb2.at[e, d - 1], rb2.at[e, d - 1], at((x + d) % 4, zh, y)))
    for e in (0, 1, 3, 2):
        for d in range(1, 4):
            xs = (x + 4 - e) % 4
            yd = (y + 4 - d) % 4
            pa = xs * 4 + yd
            rcopy(half(pa, 0), half(pa, 0), sa2.at[e, d - 1], ra2.at[e, d - 1], at(x, zh, yd)).wait_recv()
            ys = (y + 4 - e) % 4
            xd = (x + 4 - d) % 4
            pb = xd * 4 + ys
            rcopy(half(pb, 1), half(pb, 1), sb2.at[e, d - 1], rb2.at[e, d - 1], at(xd, zh, y)).wait_recv()
    own[2].wait()
    for d in range(1, 4):
        src = (zh + 4 - d) % 4
        rcopy(qo_ref.at[src], qo_ref.at[src], sq.at[d - 1], rq.at[d - 1], at(x, src, y)).wait_recv()
    for c in first + qs + sends:
        c.wait_send()


def gather_heads(queries, keys, values):
    dma = pltpu.SemaphoreType.DMA
    rows = queries.shape[0]
    return pl.pallas_call(
        gather_kernel,
        out_shape=(
            jax.ShapeDtypeStruct((4, rows, 4 * HD), BF16),
            jax.ShapeDtypeStruct((16, 4, 2, rows, HD), BF16),
        ),
        in_specs=[ANY] * 3,
        out_specs=(ANY, ANY),
        scratch_shapes=[
            dma((3, 2)), dma((3, 2)), dma((3,)), dma((3,)),
            dma((3,)), dma((3,)), dma((3,)), dma((3,)),
            dma((4, 3)), dma((4, 3)), dma((4, 3)), dma((4, 3)), dma((3,)),
        ],
        compiler_params=pltpu.CompilerParams(collective_id=0, has_side_effects=True),
    )(queries, keys, values)


KV_BLOCKS = 8


def flash_kernel(q_ref, kv_ref, o_ref, m_ref, acc_ref):
    step = pl.program_id(0)
    fold = math.log2(math.e) / math.sqrt(HD)

    @pl.when(step == 0)
    def _():
        m_ref[...] = jnp.full(m_ref.shape, -1e30, F32)
        acc_ref[...] = jnp.zeros(acc_ref.shape, F32)

    n = KV_BLOCKS * 128
    k = kv_ref[:, 0].reshape(n, HD)
    v = kv_ref[:, 1].reshape(n, HD)
    v_one = jnp.concatenate([v, jnp.ones((n, HD), BF16)], axis=1)
    for h in range(4):
        q = q_ref[:, :, h * HD:(h + 1) * HD].reshape(512, HD)
        s = lax.dot_general(q, k, (((1,), (1,)), ((), ())), preferred_element_type=F32)
        m_old = m_ref[h]
        m_new = jnp.maximum(m_old, jnp.max(s, axis=1, keepdims=True))
        m_ref[h] = m_new
        alpha = jnp.exp2((m_old - m_new) * fold)
        p = jnp.exp2((s - m_new[:, :1]) * fold)
        added = jnp.dot(p.astype(BF16), v_one, preferred_element_type=F32)
        acc_ref[h] = acc_ref[h] * alpha[:, :1] + added

    @pl.when(step == pl.num_programs(0) - 1)
    def _():
        for h in range(4):
            total = acc_ref[h]
            o_ref[:, :, h * HD:(h + 1) * HD] = (total[:, :HD] / total[:, HD:]).astype(BF16).reshape(4, 128, HD)


def flash(q_heads, kv):
    kv = kv.reshape(64, 2, 128, HD)
    steps = 64 // KV_BLOCKS
    return pl.pallas_call(
        flash_kernel,
        out_shape=jax.ShapeDtypeStruct((4, 128, 4 * HD), BF16),
        grid=(steps,),
        in_specs=[
            pl.BlockSpec((4, 128, 4 * HD), lambda i: (0, 0, 0)),
            pl.BlockSpec((KV_BLOCKS, 2, 128, HD), lambda i: (i, 0, 0, 0)),
        ],
        out_specs=pl.BlockSpec((4, 128, 4 * HD), lambda i: (0, 0, 0)),
        scratch_shapes=[pltpu.VMEM((4, 512, HD), F32), pltpu.VMEM((4, 512, 2 * HD), F32)],
        compiler_params=pltpu.CompilerParams(vmem_limit_bytes=VMEM_BYTES),
    )(q_heads, kv)


def greet(me, sec):
    barrier = pltpu.get_barrier_semaphore()

    def one(i, carry):
        pl.semaphore_signal(barrier, inc=1, device_id={"dev": (me + i) % 64}, device_id_type=MESH)
        return carry

    lax.fori_loop(1, 64, one, 0)
    pl.semaphore_signal(barrier, inc=1, device_id={"sec": 1 - sec}, device_id_type=MESH)
    pl.semaphore_signal(barrier, inc=1, device_id={"sec": 1 - sec, "dev": twin(me)}, device_id_type=MESH)
    pl.semaphore_wait(barrier, 65)


def twin(me):
    return me + 1 - 2 * (me % 2)


def one_hot(ids_ref):
    row = lax.broadcasted_iota(jnp.int32, (256, 128), 0)
    expert = row // 8
    first = expert == ids_ref[0:1, :]
    second = expert == ids_ref[1:2, :]
    named = jnp.where(first | second, 1.0, 0.0)
    before = lax.broadcasted_iota(jnp.int32, (128, 128), 0) < lax.broadcasted_iota(jnp.int32, (128, 128), 1)
    slot = jnp.dot(named.astype(BF16), jnp.where(before, 1.0, 0.0).astype(BF16), preferred_element_type=F32)
    slot = jnp.where(named > 0.5, slot, -1.0).astype(jnp.int32)
    return row % 8, first, slot


def dispatch_kernel(
    ao_ref, resid_ref, gain_ref, ids_ref, x_ref, stream_ref,
    att, rbuf, ssq, ssq_in, sbuf, sa, ra, ss, rs, sd, rd, sf, rf, lsem,
):
    me, x, zh, y = coords()
    sec = lax.axis_index("sec")
    j_me = me % 2
    q_me = 2 * sec + j_me
    half = pl.ds(pl.multiple_of(sec * 2048, 2048), 2048)
    fetch = pltpu.make_async_copy(resid_ref.at[:, half], rbuf, lsem.at[0])
    fetch.start()
    keep = pltpu.make_async_copy(ao_ref.at[zh], att.at[zh], lsem.at[1])
    keep.start()
    greet(me, sec)
    back = []
    for d in range(1, 4):
        j = (zh + d) % 4
        back.append(rcopy(ao_ref.at[j], att.at[zh], sa.at[d - 1], ra.at[d - 1], {"dev": x * 16 + j * 4 + y}))
    for c in back:
        c.start()

    r8, first, slot = one_hot(ids_ref)
    pick = jnp.where(slot == r8, 1.0, 0.0).astype(BF16)
    fold = [jnp.where((slot == 8 + r8 // 4) & (r8 % 4 == p), 1.0, 0.0).astype(BF16) for p in range(4)]

    fetch.wait()
    keep.wait()
    for d in range(1, 4):
        src = (zh + 4 - d) % 4
        rcopy(ao_ref.at[src], att.at[src], sa.at[d - 1], ra.at[d - 1], {"dev": x * 16 + src * 4 + y}).wait_recv()
    total = jnp.zeros((128, 1), F32)
    for g in range(4):
        part = rbuf[:, g * 512:(g + 1) * 512].astype(F32) + att[g].astype(F32)
        stream_ref[:, g * 512:(g + 1) * 512] = part
        total = total + jnp.sum(part * part, axis=1, keepdims=True)
    ssq[...] = jnp.broadcast_to(total, (128, 128))
    cross = rcopy(ssq, ssq_in, ss, rs, {"sec": 1 - sec})
    cross.start()
    cross.wait()
    scale = lax.rsqrt((ssq[:, :1] + ssq_in[:, :1]) * (1.0 / 4096) + 1e-06)
    for j in range(2):
        normed = []
        for p in range(4):
            low = j * 1024 + p * 256
            g = gain_ref[:, pl.ds(pl.multiple_of(sec * 2048 + low, 256), 256)]
            normed.append((stream_ref[:, low:low + 256] * scale * g).astype(BF16))
        extra = jnp.zeros((256, 256), F32)
        for p in range(4):
            main = jnp.dot(pick, normed[p], preferred_element_type=F32)
            sbuf[j, :, :, p * 256:(p + 1) * 256] = main.reshape(32, 8, 256).astype(BF16)
            extra = extra + jnp.dot(fold[p], normed[p], preferred_element_type=F32)
        sbuf[j, :, :, 1024:1280] = extra.reshape(32, 8, 256).astype(BF16)

    mg = me // 4

    def send_to(dest, i):
        j, e = dest % 2, dest // 2
        return rcopy(sbuf.at[j, e], x_ref.at[2 * sec + j, me], sd.at[i], rd.at[i], {"dev": dest})

    for d in range(1, 4):
        send_to(mg * 4 + (y + d) % 4, 0).start()
    mine = pltpu.make_async_copy(sbuf.at[j_me, me // 2], x_ref.at[q_me, me], lsem.at[2])
    mine.start()

    def send_group(i, carry):
        g = (mg + i) % 16
        for t in range(4):
            send_to(g * 4 + t, i).start()
        return carry

    lax.fori_loop(1, 16, send_group, 0)
    partners = ({"dev": twin(me)}, {"sec": 1 - sec}, {"dev": twin(me), "sec": 1 - sec})
    quarters = (2 * sec + 1 - j_me, 2 * (1 - sec) + j_me, 2 * (1 - sec) + 1 - j_me)

    def block(q, g):
        return x_ref.at[q, pl.ds(g * 4, 4)]

    mine.wait()
    for d in range(1, 4):
        src = mg * 4 + (y + 4 - d) % 4
        pass
    three = sbuf.at[0, pl.ds(0, 3)]
    rcopy(three, x_ref.at[q_me, pl.ds(0, 3)], sd.at[0], rd.at[0], partners[0]).wait_recv()

    def forward(g, i):
        for k in range(3):
            rcopy(block(q_me, g), block(q_me, g), sf.at[k, i], rf.at[k, i], partners[k]).start()

    forward(mg, 0)

    def pass_on(i, carry):
        g = (mg + 16 - i) % 16
        rcopy(block(q_me, g), block(q_me, g), sd.at[i], rd.at[i], partners[0]).wait_recv()
        forward(g, i)
        return carry

    lax.fori_loop(1, 16, pass_on, 0)

    def finish(i, carry):
        g = (mg + 16 - i) % 16
        for k in range(3):
            c = rcopy(block(quarters[k], g), block(quarters[k], g), sf.at[k, i], rf.at[k, i], partners[k])
            c.wait_recv()
            c.wait_send()
        return carry

    lax.fori_loop(0, 16, finish, 0)
    rcopy(three, x_ref.at[q_me, pl.ds(0, 3)], sd.at[0], rd.at[0], partners[0]).wait_send()

    def sent(i, carry):
        rcopy(sbuf.at[0, pl.ds(0, 4)], block(q_me, 0), sd.at[i], rd.at[i], partners[0]).wait_send()
        return carry

    lax.fori_loop(1, 16, sent, 0)
    for c in back:
        c.wait_send()


def dispatch(ao, resid, gain, ids):
    dma = pltpu.SemaphoreType.DMA
    return pl.pallas_call(
        dispatch_kernel,
        out_shape=(
            jax.ShapeDtypeStruct((4, 64, 8, 1280), BF16),
            jax.ShapeDtypeStruct((128, 2048), F32),
        ),
        in_specs=[ANY, ANY, VMEM, VMEM],
        out_specs=(ANY, VMEM),
        scratch_shapes=[
            pltpu.VMEM((4, 128, 512), BF16),
            pltpu.VMEM((128, 2048), BF16),
            pltpu.VMEM((128, 128), F32),
            pltpu.VMEM((128, 128), F32),
            pltpu.VMEM((2, 32, 8, 1280), BF16),
            dma((3,)), dma((3,)), dma, dma, dma((16,)), dma((16,)), dma((3, 16)), dma((3, 16)), dma((3,)),
        ],
        compiler_params=pltpu.CompilerParams(
            collective_id=1, has_side_effects=True, vmem_limit_bytes=VMEM_BYTES
        ),
    )(ao, resid, gain, ids)


def unfold(extra, p):
    want = 4 * lax.broadcasted_iota(jnp.int32, (128, 512), 0) + p == lax.broadcasted_iota(jnp.int32, (128, 512), 1)
    return jnp.dot(jnp.where(want, 1.0, 0.0).astype(BF16), extra, preferred_element_type=F32).astype(BF16)


def refold(rows, p):
    want = 4 * lax.broadcasted_iota(jnp.int32, (512, 128), 1) + p == lax.broadcasted_iota(jnp.int32, (512, 128), 0)
    return jnp.dot(jnp.where(want, 1.0, 0.0).astype(BF16), rows, preferred_element_type=F32)


def expert_kernel(x_ref, wg_ref, wu_ref, wd_ref, o_ref, gate, up, act):
    step = pl.program_id(0)

    @pl.when(step < 4)
    def _():
        x = x_ref[0]
        over = jnp.concatenate([unfold(x[:, 1024:], p) for p in range(4)], axis=1)
        rows = jnp.concatenate([x[:, :1024], over], axis=0)
        g = jnp.dot(rows, wg_ref[0], preferred_element_type=F32)
        u = jnp.dot(rows, wu_ref[0], preferred_element_type=F32)

        @pl.when(step == 0)
        def _():
            gate[...] = g
            up[...] = u

        @pl.when(step > 0)
        def _():
            gate[...] += g
            up[...] += u

    @pl.when(step == 3)
    def _():
        g = gate[...]
        act[...] = (g / (1.0 + jnp.exp(-g)) * up[...]).astype(BF16)

    @pl.when(step >= 4)
    def _():
        part = jnp.dot(act[...], wd_ref[0], preferred_element_type=F32).astype(BF16)
        o_ref[0, :, :1024] = part[:512]
        extra = refold(part[512:, 0:256], 0)
        for p in range(1, 4):
            extra = extra + refold(part[512:, p * 256:(p + 1) * 256], p)
        o_ref[0, :, 1024:] = extra.astype(BF16)


def experts(x, w_gate, w_up, w_down):
    x = x.reshape(4, 512, 1280)
    hidden = w_gate.shape[2]
    return pl.pallas_call(
        expert_kernel,
        out_shape=jax.ShapeDtypeStruct((4, 512, 1280), BF16),
        grid=(8,),
        in_specs=[
            pl.BlockSpec((1, 512, 1280), lambda i: (jnp.minimum(i, 3), 0, 0)),
            pl.BlockSpec((1, 1024, hidden), lambda i: (0, jnp.minimum(i, 3), 0)),
            pl.BlockSpec((1, 1024, hidden), lambda i: (0, jnp.minimum(i, 3), 0)),
            pl.BlockSpec((1, hidden, 1024), lambda i: (0, 0, jnp.maximum(i, 4) - 4)),
        ],
        out_specs=pl.BlockSpec((1, 512, 1280), lambda i: (jnp.maximum(i, 4) - 4, 0, 0)),
        scratch_shapes=[
            pltpu.VMEM((640, hidden), F32),
            pltpu.VMEM((640, hidden), F32),
            pltpu.VMEM((640, hidden), BF16),
        ],
        compiler_params=pltpu.CompilerParams(vmem_limit_bytes=VMEM_BYTES),
    )(x, w_gate, w_up, w_down)


def combine_kernel(
    part_ref, stream_ref, ids_ref, gates_ref, out_ref,
    own, part_in, sbuf, back, sp, rp, sd, rd, lsem,
):
    me, x, zh, y = coords()
    sec = lax.axis_index("sec")
    j_me = me % 2
    e_me = me // 2
    q_me = 2 * sec + j_me
    mg = me // 4
    fetch = pltpu.make_async_copy(part_ref.at[q_me], own, lsem.at[0])
    fetch.start()
    greet(me, sec)
    partners = ({"dev": twin(me)}, {"sec": 1 - sec}, {"dev": twin(me), "sec": 1 - sec})
    quarters = (2 * sec + 1 - j_me, 2 * (1 - sec) + j_me, 2 * (1 - sec) + 1 - j_me)

    def give(i, k):
        g = (mg + i) % 16
        rows = pl.ds(g * 4, 4)
        return rcopy(part_ref.at[quarters[k], rows], part_in.at[k, rows], sp.at[k, i], rp.at[k, i], partners[k])

    def give_all(i, carry):
        for k in range(3):
            give(i, k).start()
        return carry

    lax.fori_loop(0, 16, give_all, 0)

    r8, first, slot = one_hot(ids_ref)
    weight = jnp.where(first, gates_ref[0:1, :], gates_ref[1:2, :])

    def split(mask):
        w = jnp.where(mask, weight, 0.0).T
        high = w.astype(BF16)
        return high, (w - high.astype(F32)).astype(BF16)

    pick = split(slot == r8)
    fold = [split((slot == 8 + r8 // 4) & (r8 % 4 == p)) for p in range(4)]
    fetch.wait()

    def send_to(dest, i):
        return rcopy(sbuf.at[dest], back.at[j_me, e_me], sd.at[i], rd.at[i], {"dev": dest})

    def add_up(i):
        g = (mg + i) % 16
        rows = pl.ds(g * 4, 4)
        for k in range(3):
            give(i, k).wait_recv()
        total = own[rows].astype(F32) + part_in[0, rows].astype(F32)
        total = total + part_in[1, rows].astype(F32) + part_in[2, rows].astype(F32)
        sbuf[rows] = total.astype(BF16)
        return g

    add_up(0)
    for d in range(1, 4):
        send_to(mg * 4 + (y + d) % 4, 0).start()
    mine = pltpu.make_async_copy(sbuf.at[me], back.at[j_me, e_me], lsem.at[1])
    mine.start()

    def reduce_group(i, carry):
        g = add_up(i)
        for t in range(4):
            send_to(g * 4 + t, i).start()
        return carry

    lax.fori_loop(1, 16, reduce_group, 0)
    mine.wait()
    three = sbuf.at[pl.ds(0, 3)]
    rcopy(three, back.at[0, pl.ds(0, 3)], sd.at[0], rd.at[0], partners[0]).wait()

    def arrive(i, carry):
        g = (mg + 16 - i) % 16
        for k in range(3):
            give(i, k).wait_send()
        rcopy(sbuf.at[pl.ds(0, 4)], back.at[:, pl.ds(2 * g, 2)], sd.at[i], rd.at[i], partners[0]).wait_recv()
        rcopy(sbuf.at[pl.ds(0, 4)], sbuf.at[pl.ds(0, 4)], sd.at[i], rd.at[i], partners[0]).wait_send()
        return carry

    lax.fori_loop(1, 16, arrive, 0)
    for k in range(3):
        give(0, k).wait_send()

    def weigh(pair, data):
        return jnp.dot(pair[0], data, preferred_element_type=F32) + jnp.dot(pair[1], data, preferred_element_type=F32)

    for j in range(2):
        extra = back[j, :, :, 1024:1280].astype(F32).reshape(256, 256).astype(BF16)
        for p in range(4):
            low = j * 1024 + p * 256
            data = back[j, :, :, p * 256:(p + 1) * 256].astype(F32).reshape(256, 256).astype(BF16)
            moe = weigh(pick, data) + weigh(fold[p], extra)
            out_ref[:, low:low + 256] = (stream_ref[:, low:low + 256] + moe).astype(BF16)


def combine(part, stream, ids, gates):
    dma = pltpu.SemaphoreType.DMA
    return pl.pallas_call(
        combine_kernel,
        out_shape=jax.ShapeDtypeStruct((128, 2048), BF16),
        in_specs=[ANY, VMEM, VMEM, VMEM],
        out_specs=VMEM,
        scratch_shapes=[
            pltpu.VMEM((64, 8, 1280), BF16),
            pltpu.VMEM((3, 64, 8, 1280), BF16),
            pltpu.VMEM((64, 8, 1280), BF16),
            pltpu.VMEM((2, 32, 8, 1280), BF16),
            dma((3, 16)), dma((3, 16)), dma((16,)), dma((16,)), dma((2,)),
        ],
        compiler_params=pltpu.CompilerParams(
            collective_id=2, has_side_effects=True, vmem_limit_bytes=VMEM_BYTES
        ),
    )(part, stream, ids, gates)


def body(resid, queries, keys, values, norm_gain, expert_ids, gate_weights, w_gate, w_up, w_down):
    q_heads, kv = gather_heads(queries, keys, values)
    ao = flash(q_heads, kv)
    ids = expert_ids.T
    gates = gate_weights.T
    x, stream = dispatch(ao, resid, norm_gain.reshape(1, -1), ids)
    part = experts(x, w_gate, w_up, w_down)
    return combine(part.reshape(4, 64, 8, 1280), stream, ids, gates)


def solution(mesh):
    in_specs = (
        P(("rep", "dev"), None),
        P(("rep", "dev"), "sec"),
        P(("rep", "dev"), "sec"),
        P(("rep", "dev"), "sec"),
        P(),
        P(("rep", "dev"), None),
        P(("rep", "dev"), None),
        P("dev", None, "sec"),
        P("dev", None, "sec"),
        P("dev", "sec", None),
    )
    out_specs = P(("rep", "dev"), "sec")
    return jax.shard_map(body, mesh=mesh, in_specs=in_specs, out_specs=out_specs, check_vma=False)
```

```python
import math

import jax
import jax.numpy as jnp
from jax import lax
from jax.experimental import pallas as pl
from jax.experimental.pallas import tpu as pltpu
from jax.sharding import PartitionSpec as P

HD = 128
MESH = pl.DeviceIdType.MESH
F32 = jnp.float32
BF16 = jnp.bfloat16
VMEM_BYTES = 58 * 1024 * 1024
ANY = pl.BlockSpec(memory_space=pl.ANY)
VMEM = pl.BlockSpec(memory_space=pltpu.VMEM)


def rcopy(src, dst, send_sem, recv_sem, device_id):
    return pltpu.make_async_remote_copy(
        src_ref=src,
        dst_ref=dst,
        send_sem=send_sem,
        recv_sem=recv_sem,
        device_id=device_id,
        device_id_type=MESH,
    )


def coords():
    me = lax.axis_index("dev")
    return me, me // 16, (me // 4) % 4, me % 4


def attention_kernel(
    q_ref, k_ref, v_ref, o_ref, q_vm, kv_vm, m_ref, acc_ref, s1, r1, sq, rq, sa, ra, sb, rb, lsem,
):
    me, x, zh, y = coords()
    pos = x * 4 + y
    fold = math.log2(math.e) / math.sqrt(HD)

    def at(xx, zz, yy):
        return {"dev": xx * 16 + zz * 4 + yy}

    def cols(j, w):
        return pl.ds(pl.multiple_of(j * w, w), w)

    own = [
        pltpu.make_async_copy(k_ref.at[:, cols(zh, HD)], kv_vm.at[pos, zh, 0], lsem.at[0]),
        pltpu.make_async_copy(v_ref.at[:, cols(zh, HD)], kv_vm.at[pos, zh, 1], lsem.at[1]),
        pltpu.make_async_copy(q_ref.at[:, cols(zh, 4 * HD)], q_vm.at[zh], lsem.at[2]),
    ]
    for c in own:
        c.start()
    barrier = pltpu.get_barrier_semaphore()
    for d in range(1, 4):
        for peer in (at((x + d) % 4, zh, y), at(x, (zh + d) % 4, y), at(x, zh, (y + d) % 4)):
            pl.semaphore_signal(barrier, inc=1, device_id=peer, device_id_type=MESH)
    pl.semaphore_wait(barrier, 9)

    first = []
    for d in range(1, 4):
        j = (zh + d) % 4
        first.append(rcopy(k_ref.at[:, cols(j, HD)], kv_vm.at[pos, zh, 0], s1.at[d - 1, 0], r1.at[d - 1, 0], at(x, j, y)))
        first.append(rcopy(v_ref.at[:, cols(j, HD)], kv_vm.at[pos, zh, 1], s1.at[d - 1, 1], r1.at[d - 1, 1], at(x, j, y)))
    for d in range(1, 4):
        j = (zh + d) % 4
        first.append(rcopy(q_ref.at[:, cols(j, 4 * HD)], q_vm.at[zh], sq.at[d - 1], rq.at[d - 1], at(x, j, y)))
    for c in first:
        c.start()
    m_ref[...] = jnp.full(m_ref.shape, -1e30, F32)
    acc_ref[...] = jnp.zeros(acc_ref.shape, F32)
    own[0].wait()
    own[1].wait()
    for d in range(1, 4):
        src = (zh + 4 - d) % 4
        for w in range(2):
            rcopy(kv_vm.at[pos, src, w], kv_vm.at[pos, src, w], s1.at[d - 1, w], r1.at[d - 1, w], at(x, src, y)).wait_recv()

    def half(p, h):
        return kv_vm.at[p, pl.ds(2 * h, 2)]

    def lower(ex, ey, p, dest):
        return rcopy(half(p, 0), half(p, 0), sa.at[ex, ey], ra.at[ex, ey], dest)

    def upper(ex, ey, p, dest):
        return rcopy(half(p, 1), half(p, 1), sb.at[ex, ey], rb.at[ex, ey], dest)

    sends = []

    def go(c):
        c.start()
        sends.append(c)

    for d in range(1, 4):
        go(lower(d, 0, pos, at((x + d) % 4, zh, y)))
        go(upper(0, d, pos, at(x, zh, (y + d) % 4)))
    for d in range(1, 4):
        go(lower(0, d, pos, at(x, zh, (y + d) % 4)))
        go(upper(d, 0, pos, at((x + d) % 4, zh, y)))

    def absorb(p0, p1):
        k = jnp.concatenate([kv_vm[p0, :, 0].reshape(512, HD), kv_vm[p1, :, 0].reshape(512, HD)], axis=0)
        v = jnp.concatenate([kv_vm[p0, :, 1].reshape(512, HD), kv_vm[p1, :, 1].reshape(512, HD)], axis=0)
        v_one = jnp.concatenate([v, jnp.ones((1024, HD), BF16)], axis=1)
        for h in range(4):
            for r in range(2):
                rows = slice(r * 256, (r + 1) * 256)
                q = q_vm[2 * r:2 * r + 2, :, h * HD:(h + 1) * HD].reshape(256, HD)
                s = lax.dot_general(q, k, (((1,), (1,)), ((), ())), preferred_element_type=F32)
                m_old = m_ref[h, rows]
                m_new = jnp.maximum(m_old, jnp.max(s, axis=1, keepdims=True))
                m_ref[h, rows] = m_new
                alpha = jnp.exp2((m_old - m_new) * fold)
                p = jnp.exp2((s - m_new[:, :1]) * fold)
                added = jnp.dot(p.astype(BF16), v_one, preferred_element_type=F32)
                acc_ref[h, rows] = acc_ref[h, rows] * alpha[:, :1] + added

    own[2].wait()
    for d in range(1, 4):
        src = (zh + 4 - d) % 4
        rcopy(q_vm.at[src], q_vm.at[src], sq.at[d - 1], rq.at[d - 1], at(x, src, y)).wait_recv()

    for d in (1, 3, 2):
        xs = (x + 4 - d) % 4
        ys = (y + 4 - d) % 4
        pa = xs * 4 + y
        pb = x * 4 + ys
        lower(d, 0, pa, at(xs, zh, y)).wait_recv()
        for t in range(1, 4):
            go(lower(d, t, pa, at(x, zh, (y + t) % 4)))
        upper(0, d, pb, at(x, zh, ys)).wait_recv()
        for t in range(1, 4):
            go(upper(t, d, pb, at((x + t) % 4, zh, y)))

    def step(i, carry):
        ex = i // 2
        ey = (i % 2) * 2
        p0 = ((x + 4 - ex) % 4) * 4 + (y + 4 - ey) % 4
        p1 = ((x + 4 - ex) % 4) * 4 + (y + 3 - ey) % 4

        @pl.when((ey > 0) & (ex > 0))
        def _():
            lower(ex, ey, p0, at(x, zh, y)).wait_recv()
            upper(ex, ey, p0, at(x, zh, y)).wait_recv()

        @pl.when((ey > 0) & (ex == 0))
        def _():
            lower(ex, ey, p0, at(x, zh, y)).wait_recv()

        @pl.when((ey == 0) & (ex > 0))
        def _():
            upper(ex, ey, p0, at(x, zh, y)).wait_recv()

        lower(ex, ey + 1, p1, at(x, zh, y)).wait_recv()

        @pl.when(ex > 0)
        def _():
            upper(ex, ey + 1, p1, at(x, zh, y)).wait_recv()

        absorb(p0, p1)
        return carry

    lax.fori_loop(0, 8, step, 0)
    for h in range(4):
        total = acc_ref[h]
        o_ref[:, :, h * HD:(h + 1) * HD] = (total[:, :HD] / total[:, HD:]).astype(BF16).reshape(4, 128, HD)
    for c in first + sends:
        c.wait_send()


def attention(queries, keys, values):
    dma = pltpu.SemaphoreType.DMA
    rows = queries.shape[0]
    return pl.pallas_call(
        attention_kernel,
        out_shape=jax.ShapeDtypeStruct((4, rows, 4 * HD), BF16),
        in_specs=[ANY] * 3,
        out_specs=VMEM,
        scratch_shapes=[
            pltpu.VMEM((4, rows, 4 * HD), BF16),
            pltpu.VMEM((16, 4, 2, rows, HD), BF16),
            pltpu.VMEM((4, 512, HD), F32),
            pltpu.VMEM((4, 512, 2 * HD), F32),
            dma((3, 2)), dma((3, 2)), dma((3,)), dma((3,)),
            dma((4, 4)), dma((4, 4)), dma((4, 4)), dma((4, 4)), dma((3,)),
        ],
        compiler_params=pltpu.CompilerParams(
            collective_id=0, has_side_effects=True, vmem_limit_bytes=VMEM_BYTES
        ),
    )(queries, keys, values)


def greet(me, sec):
    barrier = pltpu.get_barrier_semaphore()

    def one(i, carry):
        pl.semaphore_signal(barrier, inc=1, device_id={"dev": (me + i) % 64}, device_id_type=MESH)
        return carry

    lax.fori_loop(1, 64, one, 0)
    pl.semaphore_signal(barrier, inc=1, device_id={"sec": 1 - sec}, device_id_type=MESH)
    pl.semaphore_signal(barrier, inc=1, device_id={"sec": 1 - sec, "dev": twin(me)}, device_id_type=MESH)
    pl.semaphore_wait(barrier, 65)


def twin(me):
    return me + 1 - 2 * (me % 2)


def one_hot(ids_ref):
    row = lax.broadcasted_iota(jnp.int32, (256, 128), 0)
    expert = row // 8
    first = expert == ids_ref[0:1, :]
    second = expert == ids_ref[1:2, :]
    named = jnp.where(first | second, 1.0, 0.0)
    before = lax.broadcasted_iota(jnp.int32, (128, 128), 0) < lax.broadcasted_iota(jnp.int32, (128, 128), 1)
    slot = jnp.dot(named.astype(BF16), jnp.where(before, 1.0, 0.0).astype(BF16), preferred_element_type=F32)
    slot = jnp.where(named > 0.5, slot, -1.0).astype(jnp.int32)
    return row % 8, first, slot


def dispatch_kernel(
    ao_ref, resid_ref, gain_ref, ids_ref, x_ref, stream_ref,
    att, rbuf, ssq, ssq_in, sbuf, sa, ra, ss, rs, sd, rd, sf, rf, lsem,
):
    me, x, zh, y = coords()
    sec = lax.axis_index("sec")
    j_me = me % 2
    q_me = 2 * sec + j_me
    half = pl.ds(pl.multiple_of(sec * 2048, 2048), 2048)
    fetch = pltpu.make_async_copy(resid_ref.at[:, half], rbuf, lsem.at[0])
    fetch.start()
    keep = pltpu.make_async_copy(ao_ref.at[zh], att.at[zh], lsem.at[1])
    keep.start()
    greet(me, sec)
    back = []
    for d in range(1, 4):
        j = (zh + d) % 4
        back.append(rcopy(ao_ref.at[j], att.at[zh], sa.at[d - 1], ra.at[d - 1], {"dev": x * 16 + j * 4 + y}))
    for c in back:
        c.start()

    r8, first, slot = one_hot(ids_ref)
    pick = jnp.where(slot == r8, 1.0, 0.0).astype(BF16)
    fold = [jnp.where((slot == 8 + r8 // 4) & (r8 % 4 == p), 1.0, 0.0).astype(BF16) for p in range(4)]

    fetch.wait()
    keep.wait()
    for d in range(1, 4):
        src = (zh + 4 - d) % 4
        rcopy(ao_ref.at[src], att.at[src], sa.at[d - 1], ra.at[d - 1], {"dev": x * 16 + src * 4 + y}).wait_recv()
    total = jnp.zeros((128, 1), F32)
    for g in range(4):
        part = rbuf[:, g * 512:(g + 1) * 512].astype(F32) + att[g].astype(F32)
        stream_ref[:, g * 512:(g + 1) * 512] = part
        total = total + jnp.sum(part * part, axis=1, keepdims=True)
    ssq[...] = jnp.broadcast_to(total, (128, 128))
    cross = rcopy(ssq, ssq_in, ss, rs, {"sec": 1 - sec})
    cross.start()
    cross.wait()
    scale = lax.rsqrt((ssq[:, :1] + ssq_in[:, :1]) * (1.0 / 4096) + 1e-06)
    for j in range(2):
        normed = []
        for p in range(4):
            low = j * 1024 + p * 256
            g = gain_ref[:, pl.ds(pl.multiple_of(sec * 2048 + low, 256), 256)]
            normed.append((stream_ref[:, low:low + 256] * scale * g).astype(BF16))
        extra = jnp.zeros((256, 256), F32)
        for p in range(4):
            main = jnp.dot(pick, normed[p], preferred_element_type=F32)
            sbuf[j, :, :, p * 256:(p + 1) * 256] = main.reshape(32, 8, 256).astype(BF16)
            extra = extra + jnp.dot(fold[p], normed[p], preferred_element_type=F32)
        sbuf[j, :, :, 1024:1280] = extra.reshape(32, 8, 256).astype(BF16)

    mg = me // 4

    def send_to(dest, i):
        j, e = dest % 2, dest // 2
        return rcopy(sbuf.at[j, e], x_ref.at[2 * sec + j, me], sd.at[i], rd.at[i], {"dev": dest})

    for d in range(1, 4):
        send_to(mg * 4 + (y + d) % 4, 0).start()
    mine = pltpu.make_async_copy(sbuf.at[j_me, me // 2], x_ref.at[q_me, me], lsem.at[2])
    mine.start()

    def send_group(i, carry):
        g = (mg + i) % 16
        for t in range(4):
            send_to(g * 4 + t, i).start()
        return carry

    lax.fori_loop(1, 16, send_group, 0)
    partners = ({"dev": twin(me)}, {"sec": 1 - sec}, {"dev": twin(me), "sec": 1 - sec})
    quarters = (2 * sec + 1 - j_me, 2 * (1 - sec) + j_me, 2 * (1 - sec) + 1 - j_me)

    def block(q, g):
        return x_ref.at[q, pl.ds(g * 4, 4)]

    mine.wait()
    three = sbuf.at[0, pl.ds(0, 3)]
    rcopy(three, x_ref.at[q_me, pl.ds(0, 3)], sd.at[0], rd.at[0], partners[0]).wait_recv()

    def pass_on(k, g, i):
        q = quarters[1] if k == 2 else q_me
        return rcopy(block(q, g), block(q, g), sf.at[k, i], rf.at[k, i], partners[1 if k == 1 else 0])

    def came(k, g, i):
        return rcopy(block(quarters[k], g), block(quarters[k], g), sf.at[k, i], rf.at[k, i], partners[0])

    pass_on(1, mg, 0).start()
    pass_on(0, mg, 0).start()

    def relay(i, carry):
        g = (mg + 16 - i) % 16
        before = (mg + 17 - i) % 16
        rcopy(block(q_me, g), block(q_me, g), sd.at[i], rd.at[i], partners[0]).wait_recv()
        pass_on(1, g, i).start()
        pass_on(0, g, i).start()
        came(1, before, i - 1).wait_recv()
        pass_on(2, before, i - 1).start()
        return carry

    lax.fori_loop(1, 16, relay, 0)
    last = (mg + 1) % 16
    came(1, last, 15).wait_recv()
    pass_on(2, last, 15).start()

    def finish(i, carry):
        g = (mg + 16 - i) % 16
        came(0, g, i).wait_recv()
        came(2, g, i).wait_recv()
        for k in range(3):
            pass_on(k, g, i).wait_send()
        return carry

    lax.fori_loop(0, 16, finish, 0)
    rcopy(three, x_ref.at[q_me, pl.ds(0, 3)], sd.at[0], rd.at[0], partners[0]).wait_send()

    def sent(i, carry):
        rcopy(sbuf.at[0, pl.ds(0, 4)], block(q_me, 0), sd.at[i], rd.at[i], partners[0]).wait_send()
        return carry

    lax.fori_loop(1, 16, sent, 0)
    for c in back:
        c.wait_send()


def dispatch(ao, resid, gain, ids):
    dma = pltpu.SemaphoreType.DMA
    return pl.pallas_call(
        dispatch_kernel,
        out_shape=(
            jax.ShapeDtypeStruct((4, 64, 8, 1280), BF16),
            jax.ShapeDtypeStruct((128, 2048), F32),
        ),
        in_specs=[ANY, ANY, VMEM, VMEM],
        out_specs=(ANY, VMEM),
        scratch_shapes=[
            pltpu.VMEM((4, 128, 512), BF16),
            pltpu.VMEM((128, 2048), BF16),
            pltpu.VMEM((128, 128), F32),
            pltpu.VMEM((128, 128), F32),
            pltpu.VMEM((2, 32, 8, 1280), BF16),
            dma((3,)), dma((3,)), dma, dma, dma((16,)), dma((16,)), dma((3, 16)), dma((3, 16)), dma((3,)),
        ],
        compiler_params=pltpu.CompilerParams(
            collective_id=1, has_side_effects=True, vmem_limit_bytes=VMEM_BYTES
        ),
    )(ao, resid, gain, ids)


def unfold(extra, p):
    want = 4 * lax.broadcasted_iota(jnp.int32, (128, 512), 0) + p == lax.broadcasted_iota(jnp.int32, (128, 512), 1)
    return jnp.dot(jnp.where(want, 1.0, 0.0).astype(BF16), extra, preferred_element_type=F32).astype(BF16)


def refold(rows, p):
    want = 4 * lax.broadcasted_iota(jnp.int32, (512, 128), 1) + p == lax.broadcasted_iota(jnp.int32, (512, 128), 0)
    return jnp.dot(jnp.where(want, 1.0, 0.0).astype(BF16), rows, preferred_element_type=F32)


def expert_kernel(x_ref, wg_ref, wu_ref, wd_ref, o_ref, gate, up, act):
    step = pl.program_id(0)

    @pl.when(step < 4)
    def _():
        x = x_ref[0]
        over = jnp.concatenate([unfold(x[:, 1024:], p) for p in range(4)], axis=1)
        rows = jnp.concatenate([x[:, :1024], over], axis=0)
        g = jnp.dot(rows, wg_ref[0], preferred_element_type=F32)
        u = jnp.dot(rows, wu_ref[0], preferred_element_type=F32)

        @pl.when(step == 0)
        def _():
            gate[...] = g
            up[...] = u

        @pl.when(step > 0)
        def _():
            gate[...] += g
            up[...] += u

    @pl.when(step == 3)
    def _():
        g = gate[...]
        act[...] = (g / (1.0 + jnp.exp(-g)) * up[...]).astype(BF16)

    @pl.when(step >= 4)
    def _():
        part = jnp.dot(act[...], wd_ref[0], preferred_element_type=F32).astype(BF16)
        o_ref[0, :, :1024] = part[:512]
        extra = refold(part[512:, 0:256], 0)
        for p in range(1, 4):
            extra = extra + refold(part[512:, p * 256:(p + 1) * 256], p)
        o_ref[0, :, 1024:] = extra.astype(BF16)


def experts(x, w_gate, w_up, w_down):
    x = x.reshape(4, 512, 1280)
    hidden = w_gate.shape[2]
    return pl.pallas_call(
        expert_kernel,
        out_shape=jax.ShapeDtypeStruct((4, 512, 1280), BF16),
        grid=(8,),
        in_specs=[
            pl.BlockSpec((1, 512, 1280), lambda i: (jnp.minimum(i, 3), 0, 0)),
            pl.BlockSpec((1, 1024, hidden), lambda i: (0, jnp.minimum(i, 3), 0)),
            pl.BlockSpec((1, 1024, hidden), lambda i: (0, jnp.minimum(i, 3), 0)),
            pl.BlockSpec((1, hidden, 1024), lambda i: (0, 0, jnp.maximum(i, 4) - 4)),
        ],
        out_specs=pl.BlockSpec((1, 512, 1280), lambda i: (jnp.maximum(i, 4) - 4, 0, 0)),
        scratch_shapes=[
            pltpu.VMEM((640, hidden), F32),
            pltpu.VMEM((640, hidden), F32),
            pltpu.VMEM((640, hidden), BF16),
        ],
        compiler_params=pltpu.CompilerParams(vmem_limit_bytes=VMEM_BYTES),
    )(x, w_gate, w_up, w_down)


def combine_kernel(
    part_ref, stream_ref, ids_ref, gates_ref, out_ref,
    own, part_in, sbuf, back, sp, rp, sd, rd, lsem,
):
    me, x, zh, y = coords()
    sec = lax.axis_index("sec")
    j_me = me % 2
    e_me = me // 2
    q_me = 2 * sec + j_me
    mg = me // 4
    fetch = pltpu.make_async_copy(part_ref.at[q_me], own, lsem.at[0])
    fetch.start()
    greet(me, sec)
    partners = ({"dev": twin(me)}, {"sec": 1 - sec}, {"dev": twin(me), "sec": 1 - sec})
    quarters = (2 * sec + 1 - j_me, 2 * (1 - sec) + j_me, 2 * (1 - sec) + 1 - j_me)

    def give(i, k):
        g = (mg + i) % 16
        rows = pl.ds(g * 4, 4)
        return rcopy(part_ref.at[quarters[k], rows], part_in.at[k, rows], sp.at[k, i], rp.at[k, i], partners[k])

    def give_all(i, carry):
        for k in range(3):
            give(i, k).start()
        return carry

    lax.fori_loop(0, 16, give_all, 0)

    r8, first, slot = one_hot(ids_ref)
    weight = jnp.where(first, gates_ref[0:1, :], gates_ref[1:2, :])

    def split(mask):
        w = jnp.where(mask, weight, 0.0).T
        high = w.astype(BF16)
        return high, (w - high.astype(F32)).astype(BF16)

    pick = split(slot == r8)
    fold = [split((slot == 8 + r8 // 4) & (r8 % 4 == p)) for p in range(4)]
    fetch.wait()

    def send_to(dest, i):
        return rcopy(sbuf.at[dest], back.at[j_me, e_me], sd.at[i], rd.at[i], {"dev": dest})

    def add_up(i):
        g = (mg + i) % 16
        rows = pl.ds(g * 4, 4)
        for k in range(3):
            give(i, k).wait_recv()
        total = own[rows].astype(F32) + part_in[0, rows].astype(F32)
        total = total + part_in[1, rows].astype(F32) + part_in[2, rows].astype(F32)
        sbuf[rows] = total.astype(BF16)
        return g

    add_up(0)
    for d in range(1, 4):
        send_to(mg * 4 + (y + d) % 4, 0).start()
    mine = pltpu.make_async_copy(sbuf.at[me], back.at[j_me, e_me], lsem.at[1])
    mine.start()

    def reduce_group(i, carry):
        g = add_up(i)
        for t in range(4):
            send_to(g * 4 + t, i).start()
        return carry

    lax.fori_loop(1, 16, reduce_group, 0)
    mine.wait()
    three = sbuf.at[pl.ds(0, 3)]
    rcopy(three, back.at[0, pl.ds(0, 3)], sd.at[0], rd.at[0], partners[0]).wait()

    def arrive(i, carry):
        g = (mg + 16 - i) % 16
        for k in range(3):
            give(i, k).wait_send()
        rcopy(sbuf.at[pl.ds(0, 4)], back.at[:, pl.ds(2 * g, 2)], sd.at[i], rd.at[i], partners[0]).wait_recv()
        rcopy(sbuf.at[pl.ds(0, 4)], sbuf.at[pl.ds(0, 4)], sd.at[i], rd.at[i], partners[0]).wait_send()
        return carry

    lax.fori_loop(1, 16, arrive, 0)
    for k in range(3):
        give(0, k).wait_send()

    def weigh(pair, data):
        return jnp.dot(pair[0], data, preferred_element_type=F32) + jnp.dot(pair[1], data, preferred_element_type=F32)

    for j in range(2):
        extra = back[j, :, :, 1024:1280].astype(F32).reshape(256, 256).astype(BF16)
        for p in range(4):
            low = j * 1024 + p * 256
            data = back[j, :, :, p * 256:(p + 1) * 256].astype(F32).reshape(256, 256).astype(BF16)
            moe = weigh(pick, data) + weigh(fold[p], extra)
            out_ref[:, low:low + 256] = (stream_ref[:, low:low + 256] + moe).astype(BF16)


def combine(part, stream, ids, gates):
    dma = pltpu.SemaphoreType.DMA
    return pl.pallas_call(
        combine_kernel,
        out_shape=jax.ShapeDtypeStruct((128, 2048), BF16),
        in_specs=[ANY, VMEM, VMEM, VMEM],
        out_specs=VMEM,
        scratch_shapes=[
            pltpu.VMEM((64, 8, 1280), BF16),
            pltpu.VMEM((3, 64, 8, 1280), BF16),
            pltpu.VMEM((64, 8, 1280), BF16),
            pltpu.VMEM((2, 32, 8, 1280), BF16),
            dma((3, 16)), dma((3, 16)), dma((16,)), dma((16,)), dma((2,)),
        ],
        compiler_params=pltpu.CompilerParams(
            collective_id=2, has_side_effects=True, vmem_limit_bytes=VMEM_BYTES
        ),
    )(part, stream, ids, gates)


def body(resid, queries, keys, values, norm_gain, expert_ids, gate_weights, w_gate, w_up, w_down):
    ao = attention(queries, keys, values)
    ids = expert_ids.T
    gates = gate_weights.T
    x, stream = dispatch(ao, resid, norm_gain.reshape(1, -1), ids)
    part = experts(x, w_gate, w_up, w_down)
    return combine(part.reshape(4, 64, 8, 1280), stream, ids, gates)


def solution(mesh):
    in_specs = (
        P(("rep", "dev"), None),
        P(("rep", "dev"), "sec"),
        P(("rep", "dev"), "sec"),
        P(("rep", "dev"), "sec"),
        P(),
        P(("rep", "dev"), None),
        P(("rep", "dev"), None),
        P("dev", None, "sec"),
        P("dev", None, "sec"),
        P("dev", "sec", None),
    )
    out_specs = P(("rep", "dev"), "sec")
    return jax.shard_map(body, mesh=mesh, in_specs=in_specs, out_specs=out_specs, check_vma=False)
```

```python
import math

import jax
import jax.numpy as jnp
from jax import lax
from jax.experimental import pallas as pl
from jax.experimental.pallas import tpu as pltpu
from jax.sharding import PartitionSpec as P

HD = 128
MESH = pl.DeviceIdType.MESH
F32 = jnp.float32
BF16 = jnp.bfloat16
VMEM_BYTES = 58 * 1024 * 1024
ANY = pl.BlockSpec(memory_space=pl.ANY)
VMEM = pl.BlockSpec(memory_space=pltpu.VMEM)


def rcopy(src, dst, send_sem, recv_sem, device_id):
    return pltpu.make_async_remote_copy(
        src_ref=src,
        dst_ref=dst,
        send_sem=send_sem,
        recv_sem=recv_sem,
        device_id=device_id,
        device_id_type=MESH,
    )


def coords():
    me = lax.axis_index("dev")
    return me, me // 16, (me // 4) % 4, me % 4


def attention_kernel(
    q_ref, k_ref, v_ref, wd_ref, o_ref, wd_out, q_vm, kv_vm, m_ref, acc_ref,
    s1, r1, sq, rq, sa, ra, sb, rb, sw, rw, st, rt, lsem,
):
    me, x, zh, y = coords()
    pos = x * 4 + y
    sec = lax.axis_index("sec")
    rep = lax.axis_index("rep")
    partners, quarters, q_me = square(me, sec)
    sibling = {"rep": 1 - rep}
    fold = math.log2(math.e) / math.sqrt(HD)

    def at(xx, zz, yy):
        return {"dev": xx * 16 + zz * 4 + yy}

    def cols(j, w):
        return pl.ds(pl.multiple_of(j * w, w), w)

    own = [
        pltpu.make_async_copy(k_ref.at[:, cols(zh, HD)], kv_vm.at[pos, zh, 0], lsem.at[0]),
        pltpu.make_async_copy(v_ref.at[:, cols(zh, HD)], kv_vm.at[pos, zh, 1], lsem.at[1]),
        pltpu.make_async_copy(q_ref.at[:, cols(zh, 4 * HD)], q_vm.at[zh], lsem.at[2]),
    ]
    for c in own:
        c.start()
    own_down = pltpu.make_async_copy(wd_ref.at[0, :, cols(q_me, 1024)], wd_out.at[q_me], lsem.at[3])
    own_down.start()
    barrier = pltpu.get_barrier_semaphore()
    for d in range(1, 4):
        for peer in (at((x + d) % 4, zh, y), at(x, (zh + d) % 4, y), at(x, zh, (y + d) % 4)):
            pl.semaphore_signal(barrier, inc=1, device_id=peer, device_id_type=MESH)
    for peer in (partners[1], partners[2], sibling):
        pl.semaphore_signal(barrier, inc=1, device_id=peer, device_id_type=MESH)
    pl.semaphore_wait(barrier, 12)

    hid = wd_ref.shape[1] // 2
    mine = pl.ds(pl.multiple_of(rep * hid, hid), hid)
    other = pl.ds(pl.multiple_of((1 - rep) * hid, hid), hid)

    def down(k):
        return rcopy(wd_ref.at[0, mine, cols(quarters[k], 1024)], wd_out.at[q_me, mine], sw.at[k], rw.at[k], partners[k])

    def share(k):
        part = wd_out.at[quarters[k], mine]
        return rcopy(part, part, st.at[k], rt.at[k], sibling)

    first = []
    for d in range(1, 4):
        j = (zh + d) % 4
        first.append(rcopy(k_ref.at[:, cols(j, HD)], kv_vm.at[pos, zh, 0], s1.at[d - 1, 0], r1.at[d - 1, 0], at(x, j, y)))
        first.append(rcopy(v_ref.at[:, cols(j, HD)], kv_vm.at[pos, zh, 1], s1.at[d - 1, 1], r1.at[d - 1, 1], at(x, j, y)))
    for d in range(1, 4):
        j = (zh + d) % 4
        first.append(rcopy(q_ref.at[:, cols(j, 4 * HD)], q_vm.at[zh], sq.at[d - 1], rq.at[d - 1], at(x, j, y)))
    for c in first:
        c.start()
    m_ref[...] = jnp.full(m_ref.shape, -1e30, F32)
    acc_ref[...] = jnp.zeros(acc_ref.shape, F32)
    own[0].wait()
    own[1].wait()
    for d in range(1, 4):
        src = (zh + 4 - d) % 4
        for w in range(2):
            rcopy(kv_vm.at[pos, src, w], kv_vm.at[pos, src, w], s1.at[d - 1, w], r1.at[d - 1, w], at(x, src, y)).wait_recv()

    def half(p, h):
        return kv_vm.at[p, pl.ds(2 * h, 2)]

    def lower(ex, ey, p, dest):
        return rcopy(half(p, 0), half(p, 0), sa.at[ex, ey], ra.at[ex, ey], dest)

    def upper(ex, ey, p, dest):
        return rcopy(half(p, 1), half(p, 1), sb.at[ex, ey], rb.at[ex, ey], dest)

    sends = []

    def go(c):
        c.start()
        sends.append(c)

    for d in range(1, 4):
        go(lower(d, 0, pos, at((x + d) % 4, zh, y)))
        go(upper(0, d, pos, at(x, zh, (y + d) % 4)))
    for d in range(1, 4):
        go(lower(0, d, pos, at(x, zh, (y + d) % 4)))
        go(upper(d, 0, pos, at((x + d) % 4, zh, y)))

    def absorb(p0, p1):
        k = jnp.concatenate([kv_vm[p0, :, 0].reshape(512, HD), kv_vm[p1, :, 0].reshape(512, HD)], axis=0)
        v = jnp.concatenate([kv_vm[p0, :, 1].reshape(512, HD), kv_vm[p1, :, 1].reshape(512, HD)], axis=0)
        v_one = jnp.concatenate([v, jnp.ones((1024, HD), BF16)], axis=1)
        for h in range(4):
            for r in range(2):
                rows = slice(r * 256, (r + 1) * 256)
                q = q_vm[2 * r:2 * r + 2, :, h * HD:(h + 1) * HD].reshape(256, HD)
                s = lax.dot_general(q, k, (((1,), (1,)), ((), ())), preferred_element_type=F32)
                m_old = m_ref[h, rows]
                m_new = jnp.maximum(m_old, jnp.max(s, axis=1, keepdims=True))
                m_ref[h, rows] = m_new
                alpha = jnp.exp2((m_old - m_new) * fold)
                p = jnp.exp2((s - m_new[:, :1]) * fold)
                added = jnp.dot(p.astype(BF16), v_one, preferred_element_type=F32)
                acc_ref[h, rows] = acc_ref[h, rows] * alpha[:, :1] + added

    own[2].wait()
    for d in range(1, 4):
        src = (zh + 4 - d) % 4
        rcopy(q_vm.at[src], q_vm.at[src], sq.at[d - 1], rq.at[d - 1], at(x, src, y)).wait_recv()

    for d in (1, 3, 2):
        xs = (x + 4 - d) % 4
        ys = (y + 4 - d) % 4
        pa = xs * 4 + y
        pb = x * 4 + ys
        lower(d, 0, pa, at(xs, zh, y)).wait_recv()
        for t in range(1, 4):
            go(lower(d, t, pa, at(x, zh, (y + t) % 4)))
        upper(0, d, pb, at(x, zh, ys)).wait_recv()
        for t in range(1, 4):
            go(upper(t, d, pb, at((x + t) % 4, zh, y)))

    def step(i, carry):
        ex = i // 2
        ey = (i % 2) * 2
        p0 = ((x + 4 - ex) % 4) * 4 + (y + 4 - ey) % 4
        p1 = ((x + 4 - ex) % 4) * 4 + (y + 3 - ey) % 4

        @pl.when((ey > 0) & (ex > 0))
        def _():
            lower(ex, ey, p0, at(x, zh, y)).wait_recv()
            upper(ex, ey, p0, at(x, zh, y)).wait_recv()

        @pl.when((ey > 0) & (ex == 0))
        def _():
            lower(ex, ey, p0, at(x, zh, y)).wait_recv()

        @pl.when((ey == 0) & (ex > 0))
        def _():
            upper(ex, ey, p0, at(x, zh, y)).wait_recv()

        lower(ex, ey + 1, p1, at(x, zh, y)).wait_recv()

        @pl.when(ex > 0)
        def _():
            upper(ex, ey + 1, p1, at(x, zh, y)).wait_recv()

        @pl.when(i == 2)
        def _():
            for k in range(3):
                down(k).start()

        absorb(p0, p1)
        return carry

    lax.fori_loop(0, 8, step, 0)
    for k in range(3):
        part = wd_out.at[quarters[k], mine]
        rcopy(part, part, sw.at[k], rw.at[k], partners[k]).wait_recv()
        share(k).start()
    for h in range(4):
        total = acc_ref[h]
        o_ref[:, :, h * HD:(h + 1) * HD] = (total[:, :HD] / total[:, HD:]).astype(BF16).reshape(4, 128, HD)
    for c in first + sends:
        c.wait_send()
    own_down.wait()
    for k in range(3):
        down(k).wait_send()
        part = wd_out.at[quarters[k], other]
        rcopy(part, part, st.at[k], rt.at[k], sibling).wait_recv()
        share(k).wait_send()


def attention(queries, keys, values, w_down):
    dma = pltpu.SemaphoreType.DMA
    rows = queries.shape[0]
    return pl.pallas_call(
        attention_kernel,
        out_shape=(
            jax.ShapeDtypeStruct((4, rows, 4 * HD), BF16),
            jax.ShapeDtypeStruct((4, w_down.shape[1], 1024), BF16),
        ),
        in_specs=[ANY] * 4,
        out_specs=(VMEM, ANY),
        scratch_shapes=[
            pltpu.VMEM((4, rows, 4 * HD), BF16),
            pltpu.VMEM((16, 4, 2, rows, HD), BF16),
            pltpu.VMEM((4, 512, HD), F32),
            pltpu.VMEM((4, 512, 2 * HD), F32),
            dma((3, 2)), dma((3, 2)), dma((3,)), dma((3,)),
            dma((4, 4)), dma((4, 4)), dma((4, 4)), dma((4, 4)),
            dma((3,)), dma((3,)), dma((3,)), dma((3,)), dma((4,)),
        ],
        compiler_params=pltpu.CompilerParams(
            collective_id=0, has_side_effects=True, vmem_limit_bytes=VMEM_BYTES
        ),
    )(queries, keys, values, w_down)


def square(me, sec):
    j = me % 2
    partners = ({"dev": twin(me)}, {"sec": 1 - sec}, {"dev": twin(me), "sec": 1 - sec})
    quarters = (2 * sec + 1 - j, 2 * (1 - sec) + j, 2 * (1 - sec) + 1 - j)
    return partners, quarters, 2 * sec + j


def greet(me, sec):
    barrier = pltpu.get_barrier_semaphore()

    def one(i, carry):
        pl.semaphore_signal(barrier, inc=1, device_id={"dev": (me + i) % 64}, device_id_type=MESH)
        return carry

    lax.fori_loop(1, 64, one, 0)
    pl.semaphore_signal(barrier, inc=1, device_id={"sec": 1 - sec}, device_id_type=MESH)
    pl.semaphore_signal(barrier, inc=1, device_id={"sec": 1 - sec, "dev": twin(me)}, device_id_type=MESH)
    pl.semaphore_wait(barrier, 65)


def twin(me):
    return me + 1 - 2 * (me % 2)


def one_hot(ids_ref):
    row = lax.broadcasted_iota(jnp.int32, (256, 128), 0)
    expert = row // 8
    first = expert == ids_ref[0:1, :]
    second = expert == ids_ref[1:2, :]
    named = jnp.where(first | second, 1.0, 0.0)
    before = lax.broadcasted_iota(jnp.int32, (128, 128), 0) < lax.broadcasted_iota(jnp.int32, (128, 128), 1)
    slot = jnp.dot(named.astype(BF16), jnp.where(before, 1.0, 0.0).astype(BF16), preferred_element_type=F32)
    slot = jnp.where(named > 0.5, slot, -1.0).astype(jnp.int32)
    return row % 8, first, slot


def expert_kernel(
    ao_ref, resid_ref, gain_ref, ids_ref, gates_ref, wg_ref, wu_ref, wd_ref, out_ref,
    att, rbuf, stream_ref, ssq, ssq_in, sbuf, xall, wg, wu, wd, acts, outgoing, back,
    sa, ra, ss, rs, sd, rd, sf, rf, sh, rh, sr, rr, lsem,
):
    me, x, zh, y = coords()
    sec = lax.axis_index("sec")
    j_me = me % 2
    e_me = me // 2
    low = me % 16
    partners, quarters, q_me = square(me, sec)
    half = pl.ds(pl.multiple_of(sec * 2048, 2048), 2048)
    fetch = pltpu.make_async_copy(resid_ref.at[:, half], rbuf, lsem.at[0])
    fetch.start()
    keep = pltpu.make_async_copy(ao_ref.at[zh], att.at[zh], lsem.at[1])
    keep.start()
    weights = [
        pltpu.make_async_copy(wg_ref.at[0], wg, lsem.at[3]),
        pltpu.make_async_copy(wu_ref.at[0], wu, lsem.at[4]),
        pltpu.make_async_copy(wd_ref, wd, lsem.at[5]),
    ]
    for c in weights:
        c.start()
    greet(me, sec)
    heads = []
    for d in range(1, 4):
        j = (zh + d) % 4
        heads.append(rcopy(ao_ref.at[j], att.at[zh], sa.at[d - 1], ra.at[d - 1], {"dev": x * 16 + j * 4 + y}))
    for c in heads:
        c.start()

    r8, first, slot = one_hot(ids_ref)
    pick = jnp.where(slot == r8, 1.0, 0.0).astype(BF16)
    fold = [jnp.where((slot == 8 + r8 // 4) & (r8 % 4 == p), 1.0, 0.0).astype(BF16) for p in range(4)]

    fetch.wait()
    keep.wait()
    for d in range(1, 4):
        src = (zh + 4 - d) % 4
        rcopy(ao_ref.at[src], att.at[src], sa.at[d - 1], ra.at[d - 1], {"dev": x * 16 + src * 4 + y}).wait_recv()
    total = jnp.zeros((128, 1), F32)
    for g in range(4):
        part = rbuf[:, g * 512:(g + 1) * 512].astype(F32) + att[g].astype(F32)
        stream_ref[:, g * 512:(g + 1) * 512] = part
        total = total + jnp.sum(part * part, axis=1, keepdims=True)
    ssq[...] = jnp.broadcast_to(total, (128, 128))
    cross = rcopy(ssq, ssq_in, ss, rs, {"sec": 1 - sec})
    cross.start()
    cross.wait()
    scale = lax.rsqrt((ssq[:, :1] + ssq_in[:, :1]) * (1.0 / 4096) + 1e-06)
    for j in range(2):
        normed = []
        for p in range(4):
            at = j * 1024 + p * 256
            g = gain_ref[:, pl.ds(pl.multiple_of(sec * 2048 + at, 256), 256)]
            normed.append((stream_ref[:, at:at + 256] * scale * g).astype(BF16))
        extra = jnp.zeros((256, 256), F32)
        for p in range(4):
            main = jnp.dot(pick, normed[p], preferred_element_type=F32)
            sbuf[j, :, :, p * 256:(p + 1) * 256] = main.reshape(32, 8, 256).astype(BF16)
            extra = extra + jnp.dot(fold[p], normed[p], preferred_element_type=F32)
        sbuf[j, :, :, 1024:1280] = extra.reshape(32, 8, 256).astype(BF16)

    def ahead(c):
        return ((x + c) % 4) * 16

    def behind(c):
        return ((x + 4 - c) % 4) * 16

    def rows_to(dest, c):
        j, e = dest % 2, dest // 2
        return rcopy(sbuf.at[j, e], xall.at[2 * sec + j, me], sd.at[c], rd.at[c], {"dev": dest})

    def send_rows(c, start):
        def one(t, carry):
            rows_to(ahead(c) + (low + t) % 16, c).start()
            return carry

        lax.fori_loop(start, 16, one, 0)

    def block(q, c):
        return xall.at[q, pl.ds(behind(c), 16)]

    def counted(n, send_sem, recv_sem):
        ref = outgoing.at[pl.ds(0, n)]
        return rcopy(ref, ref, send_sem, recv_sem, partners[0])

    def pass_on(k, c):
        q = quarters[1] if k == 2 else q_me
        return rcopy(block(q, c), block(q, c), sf.at[k, c], rf.at[k, c], partners[1 if k == 1 else 0])

    def came(k, c):
        return rcopy(block(quarters[k], c), block(quarters[k], c), sf.at[k, c], rf.at[k, c], partners[0])

    def act_to(k, c):
        return rcopy(acts.at[q_me, c], acts.at[q_me, c], sh.at[k, c], rh.at[k, c], partners[k])

    def act_from(k, c):
        ref = acts.at[quarters[k], c]
        return rcopy(ref, ref, sh.at[k, c], rh.at[k, c], partners[k])

    def result_to(dest, c):
        return rcopy(outgoing.at[dest], back.at[j_me, e_me], sr.at[c], rr.at[c], {"dev": dest})

    own_rows = pltpu.make_async_copy(sbuf.at[j_me, e_me], xall.at[q_me, me], lsem.at[2])
    own_rows.start()
    own_back = pltpu.make_async_copy(outgoing.at[me], back.at[j_me, e_me], lsem.at[6])
    send_rows(0, 1)
    send_rows(1, 0)
    own_rows.wait()
    for c in weights:
        c.wait()

    def relay(c):
        @pl.when(c == 0)
        def _():
            ref = xall.at[q_me, pl.ds(behind(0), 15)]
            rcopy(ref, ref, sd.at[0], rd.at[0], partners[0]).wait_recv()

        @pl.when(c > 0)
        def _():
            rcopy(block(q_me, c), block(q_me, c), sd.at[c], rd.at[c], partners[0]).wait_recv()

        pass_on(1, c).start()
        pass_on(0, c).start()

        @pl.when(c == 0)
        def _():
            counted(15, sd.at[0], rd.at[0]).wait_send()
            send_rows(2, 0)

        @pl.when(c == 1)
        def _():
            counted(16, sd.at[1], rd.at[1]).wait_send()
            send_rows(3, 0)

        came(1, c).wait_recv()
        pass_on(2, c).start()

    def hidden(c):
        came(0, c).wait_recv()
        came(2, c).wait_recv()
        rows = []
        for q in range(4):
            data = xall[q, pl.ds(behind(c), 16)].astype(F32).reshape(128, 1280).astype(BF16)
            over = jnp.concatenate([unfold(data[:, 1024:], p) for p in range(4)], axis=1)
            rows.append(jnp.concatenate([data[:, :1024], over], axis=0))
        rows = jnp.concatenate(rows, axis=1)
        g = jnp.dot(rows, wg[...], preferred_element_type=F32)
        u = jnp.dot(rows, wu[...], preferred_element_type=F32)
        acts[q_me, c] = (g / (1.0 + jnp.exp(-g)) * u).astype(BF16)
        for k in (2, 1, 0):
            act_to(k, c).start()

    def output(c):
        for k in range(3):
            act_from(k, c).wait_recv()
        part = jnp.dot(acts[0, c], wd[0], preferred_element_type=F32)
        for q in range(1, 4):
            part = part + jnp.dot(acts[q, c], wd[q], preferred_element_type=F32)
        outgoing[pl.ds(behind(c), 16), :, 0:1024] = part[:128].reshape(16, 8, 1024).astype(BF16)
        over = part[128:].astype(BF16)
        extra = refold(over[:, 0:256], 0)
        for p in range(1, 4):
            extra = extra + refold(over[:, p * 256:(p + 1) * 256], p)
        outgoing[pl.ds(behind(c), 16), :, 1024:1280] = extra.reshape(16, 8, 256).astype(BF16)

        @pl.when(c == 0)
        def _():
            own_back.start()

        def one(t, carry):
            result_to(behind(c) + (low + t) % 16, c).start()
            return carry

        lax.fori_loop(jnp.where(c == 0, 1, 0), 16, one, 0)

    def stage(c, carry):
        @pl.when(c < 4)
        def _():
            relay(c)

        @pl.when((c >= 1) & (c < 5))
        def _():
            hidden(c - 1)

        @pl.when(c >= 2)
        def _():
            output(c - 2)

        return carry

    lax.fori_loop(0, 6, stage, 0)
    own_back.wait()
    counted(15, sr.at[0], rr.at[0]).wait_send()
    ref = back.at[0, pl.ds(0, 15)]
    rcopy(ref, ref, sr.at[0], rr.at[0], partners[0]).wait_recv()

    def arrive(c, carry):
        ref = back.at[:, pl.ds(ahead(c) // 2, 8)]
        rcopy(ref, ref, sr.at[c], rr.at[c], partners[0]).wait_recv()
        counted(16, sr.at[c], rr.at[c]).wait_send()
        return carry

    lax.fori_loop(1, 4, arrive, 0)

    r8, first, slot = one_hot(ids_ref)
    weight = jnp.where(first, gates_ref[0:1, :], gates_ref[1:2, :])

    def split(mask):
        w = jnp.where(mask, weight, 0.0).T
        high = w.astype(BF16)
        return high, (w - high.astype(F32)).astype(BF16)

    def weigh(pair, data):
        return jnp.dot(pair[0], data, preferred_element_type=F32) + jnp.dot(pair[1], data, preferred_element_type=F32)

    main_pick = split(slot == r8)
    fold_pick = [split((slot == 8 + r8 // 4) & (r8 % 4 == p)) for p in range(4)]
    for j in range(2):
        extra = back[j, :, :, 1024:1280].astype(F32).reshape(256, 256).astype(BF16)
        for p in range(4):
            at = j * 1024 + p * 256
            data = back[j, :, :, p * 256:(p + 1) * 256].astype(F32).reshape(256, 256).astype(BF16)
            moe = weigh(main_pick, data) + weigh(fold_pick[p], extra)
            out_ref[:, at:at + 256] = (stream_ref[:, at:at + 256] + moe).astype(BF16)

    for c in heads:
        c.wait_send()
    for c in (2, 3):
        counted(16, sd.at[c], rd.at[c]).wait_send()

    def drain(c, carry):
        for k in range(3):
            pass_on(k, c).wait_send()
            act_to(k, c).wait_send()
        return carry

    lax.fori_loop(0, 4, drain, 0)


def unfold(extra, p):
    want = 4 * lax.broadcasted_iota(jnp.int32, (32, 128), 0) + p == lax.broadcasted_iota(jnp.int32, (32, 128), 1)
    return jnp.dot(jnp.where(want, 1.0, 0.0).astype(BF16), extra, preferred_element_type=F32).astype(BF16)


def refold(rows, p):
    want = 4 * lax.broadcasted_iota(jnp.int32, (128, 32), 1) + p == lax.broadcasted_iota(jnp.int32, (128, 32), 0)
    return jnp.dot(jnp.where(want, 1.0, 0.0).astype(BF16), rows, preferred_element_type=F32)


def experts(ao, resid, gain, ids, gates, w_gate, w_up, down):
    dma = pltpu.SemaphoreType.DMA
    hidden = w_gate.shape[2]
    return pl.pallas_call(
        expert_kernel,
        out_shape=jax.ShapeDtypeStruct((128, 2048), BF16),
        in_specs=[ANY, ANY, VMEM, VMEM, VMEM, ANY, ANY, ANY],
        out_specs=VMEM,
        scratch_shapes=[
            pltpu.VMEM((4, 128, 512), BF16),
            pltpu.VMEM((128, 2048), BF16),
            pltpu.VMEM((128, 2048), F32),
            pltpu.VMEM((128, 128), F32),
            pltpu.VMEM((128, 128), F32),
            pltpu.VMEM((2, 32, 8, 1280), BF16),
            pltpu.VMEM((4, 64, 8, 1280), BF16),
            pltpu.VMEM((4096, hidden), BF16),
            pltpu.VMEM((4096, hidden), BF16),
            pltpu.VMEM((4, hidden, 1024), BF16),
            pltpu.VMEM((4, 4, 160, hidden), BF16),
            pltpu.VMEM((64, 8, 1280), BF16),
            pltpu.VMEM((2, 32, 8, 1280), BF16),
            dma((3,)), dma((3,)), dma, dma, dma((4,)), dma((4,)), dma((3, 4)), dma((3, 4)),
            dma((3, 4)), dma((3, 4)), dma((4,)), dma((4,)), dma((7,)),
        ],
        compiler_params=pltpu.CompilerParams(
            collective_id=1, has_side_effects=True, vmem_limit_bytes=VMEM_BYTES
        ),
    )(ao, resid, gain, ids, gates, w_gate, w_up, down)


def body(resid, queries, keys, values, norm_gain, expert_ids, gate_weights, w_gate, w_up, w_down):
    ao, down = attention(queries, keys, values, w_down)
    return experts(
        ao, resid, norm_gain.reshape(1, -1), expert_ids.T, gate_weights.T, w_gate, w_up, down
    )


def solution(mesh):
    in_specs = (
        P(("rep", "dev"), None),
        P(("rep", "dev"), "sec"),
        P(("rep", "dev"), "sec"),
        P(("rep", "dev"), "sec"),
        P(),
        P(("rep", "dev"), None),
        P(("rep", "dev"), None),
        P("dev", None, "sec"),
        P("dev", None, "sec"),
        P("dev", "sec", None),
    )
    out_specs = P(("rep", "dev"), "sec")
    return jax.shard_map(body, mesh=mesh, in_specs=in_specs, out_specs=out_specs, check_vma=False)
```

```python
import math

import jax
import jax.numpy as jnp
from jax import lax
from jax.experimental import pallas as pl
from jax.experimental.pallas import tpu as pltpu
from jax.sharding import PartitionSpec as P

HD = 128
MESH = pl.DeviceIdType.MESH
F32 = jnp.float32
BF16 = jnp.bfloat16
VMEM_BYTES = 58 * 1024 * 1024
ANY = pl.BlockSpec(memory_space=pl.ANY)
VMEM = pl.BlockSpec(memory_space=pltpu.VMEM)


def rcopy(src, dst, send_sem, recv_sem, device_id):
    return pltpu.make_async_remote_copy(
        src_ref=src,
        dst_ref=dst,
        send_sem=send_sem,
        recv_sem=recv_sem,
        device_id=device_id,
        device_id_type=MESH,
    )


def coords():
    me = lax.axis_index("dev")
    return me, me // 16, (me // 4) % 4, me % 4


def twin(me):
    return me + 1 - 2 * (me % 2)


def square(me, sec):
    j = me % 2
    partners = ({"dev": twin(me)}, {"sec": 1 - sec}, {"dev": twin(me), "sec": 1 - sec})
    quarters = (2 * sec + 1 - j, 2 * (1 - sec) + j, 2 * (1 - sec) + 1 - j)
    return partners, quarters, 2 * sec + j


def greet(me, sec, rep):
    barrier = pltpu.get_barrier_semaphore()

    def one(i, carry):
        pl.semaphore_signal(barrier, inc=1, device_id={"dev": (me + i) % 64}, device_id_type=MESH)
        return carry

    lax.fori_loop(1, 64, one, 0)
    for peer in ({"sec": 1 - sec}, {"sec": 1 - sec, "dev": twin(me)}, {"rep": 1 - rep}):
        pl.semaphore_signal(barrier, inc=1, device_id=peer, device_id_type=MESH)
    pl.semaphore_wait(barrier, 66)


def one_hot(ids_ref):
    row = lax.broadcasted_iota(jnp.int32, (256, 128), 0)
    expert = row // 8
    first = expert == ids_ref[0:1, :]
    second = expert == ids_ref[1:2, :]
    named = jnp.where(first | second, 1.0, 0.0)
    before = lax.broadcasted_iota(jnp.int32, (128, 128), 0) < lax.broadcasted_iota(jnp.int32, (128, 128), 1)
    slot = jnp.dot(named.astype(BF16), jnp.where(before, 1.0, 0.0).astype(BF16), preferred_element_type=F32)
    slot = jnp.where(named > 0.5, slot, -1.0).astype(jnp.int32)
    return row % 8, first, slot


def attend(
    q_ref, k_ref, v_ref, wd_ref, ao, wd, q_vm, kv_vm, m_ref, acc_ref,
    s1, r1, sq, rq, sa, ra, sb, rb, sap, rap, sbp, rbp, sw, rw, st, rt, lsem,
):
    me, x, zh, y = coords()
    pos = x * 4 + y
    sec = lax.axis_index("sec")
    rep = lax.axis_index("rep")
    partners, quarters, q_me = square(me, sec)
    sibling = {"rep": 1 - rep}
    fold = math.log2(math.e) / math.sqrt(HD)

    def at(xx, zz, yy):
        return {"dev": ((xx + 4) % 4) * 16 + zz * 4 + (yy + 4) % 4}

    def cols(j, w):
        return pl.ds(pl.multiple_of(j * w, w), w)

    own = [
        pltpu.make_async_copy(k_ref.at[:, cols(zh, HD)], kv_vm.at[pos, zh, 0], lsem.at[0]),
        pltpu.make_async_copy(v_ref.at[:, cols(zh, HD)], kv_vm.at[pos, zh, 1], lsem.at[1]),
        pltpu.make_async_copy(q_ref.at[:, cols(zh, 4 * HD)], q_vm.at[zh], lsem.at[2]),
        pltpu.make_async_copy(wd_ref.at[0, :, cols(q_me, 1024)], wd.at[q_me], lsem.at[3]),
    ]
    for c in own:
        c.start()
    greet(me, sec, rep)

    hid = wd_ref.shape[1] // 2
    mine = pl.ds(pl.multiple_of(rep * hid, hid), hid)
    other = pl.ds(pl.multiple_of((1 - rep) * hid, hid), hid)

    def down(k):
        return rcopy(wd_ref.at[0, mine, cols(quarters[k], 1024)], wd.at[q_me, mine], sw.at[k], rw.at[k], partners[k])

    def share(k):
        part = wd.at[quarters[k], mine]
        return rcopy(part, part, st.at[k], rt.at[k], sibling)

    first = []
    for d in range(1, 4):
        j = (zh + d) % 4
        first.append(rcopy(k_ref.at[:, cols(j, HD)], kv_vm.at[pos, zh, 0], s1.at[d - 1, 0], r1.at[d - 1, 0], at(x, j, y)))
        first.append(rcopy(v_ref.at[:, cols(j, HD)], kv_vm.at[pos, zh, 1], s1.at[d - 1, 1], r1.at[d - 1, 1], at(x, j, y)))
    for d in range(1, 4):
        j = (zh + d) % 4
        first.append(rcopy(q_ref.at[:, cols(j, 4 * HD)], q_vm.at[zh], sq.at[d - 1], rq.at[d - 1], at(x, j, y)))
    for c in first:
        c.start()
    m_ref[...] = jnp.full(m_ref.shape, -1e30, F32)
    acc_ref[...] = jnp.zeros(acc_ref.shape, F32)
    own[0].wait()
    own[1].wait()
    for d in range(1, 4):
        src = (zh + 4 - d) % 4
        for w in range(2):
            rcopy(kv_vm.at[pos, src, w], kv_vm.at[pos, src, w], s1.at[d - 1, w], r1.at[d - 1, w], at(x, src, y)).wait_recv()

    def place(ex, ey):
        return ((x + 4 - ex) % 4) * 4 + (y + 4 - ey) % 4

    def copy_of(h, ex, ey, p, dest):
        ref = kv_vm.at[p, pl.ds(2 * h, 2)]
        send, recv = (sa, ra) if h == 0 else (sb, rb)
        return rcopy(ref, ref, send.at[ex, ey], recv.at[ex, ey], dest)

    def piece_of(h, ex, ey, part, p, dest):
        ref = kv_vm.at[p, 2 * h + part]
        send, recv = (sap, rap) if h == 0 else (sbp, rbp)
        line = ey if h == 1 else ex
        return rcopy(ref, ref, send.at[line, part], recv.at[line, part], dest)

    def axis_to(h, second, step):
        return at(x + step, zh, y) if (h == 0) != second else at(x, zh, y + step)

    sends = []

    def go(make, *rest):
        make(*rest).start()
        sends.append((make, rest))

    def index(h, a, b):
        return (a, b) if h == 0 else (b, a)

    def arrived(h, a, b):
        ex, ey = index(h, a, b)
        copy_of(h, ex, ey, place(ex, ey), partners[0]).wait_recv()

    def leg_copy(h, a, b, step):
        ex, ey = index(h, a, b)
        return copy_of(h, ex, ey, place(*index(h, a, 0)), axis_to(h, True, step))

    def second_leg(h, a):
        for b, step in ((1, 1), (3, -1)):
            go(leg_copy, h, a, b, step)

    def piece_copy(h, a, b):
        part, step = (0, 1) if b == 1 else (1, -1)
        ex, ey = index(h, a, 2)
        return piece_of(h, ex, ey, part, place(*index(h, a, b)), axis_to(h, True, step))

    def relay_second(h, a, b):
        go(piece_copy, h, a, b)

    def pieces(h, a):
        ex, ey = index(h, a, 2)
        for part in range(2):
            piece_of(h, ex, ey, part, place(ex, ey), partners[0]).wait_recv()

    def first_piece(h, part, p, dest):
        ref = kv_vm.at[p, 2 * h + part]
        send, recv = (sap, rap) if h == 0 else (sbp, rbp)
        return rcopy(ref, ref, send.at[4, part], recv.at[4, part], dest)

    def start_copy(h, a, step):
        ex, ey = index(h, a, 0)
        return copy_of(h, ex, ey, pos, axis_to(h, False, step))

    def turn_copy(h, a, part, step):
        return first_piece(h, part, place(*index(h, a, 0)), axis_to(h, False, step))

    for h in range(2):
        for a, step in ((1, 1), (3, -1)):
            go(start_copy, h, a, step)
    for h in range(2):
        second_leg(h, 0)

    def absorb(p0, p1):
        k = jnp.concatenate([kv_vm[p0, :, 0].reshape(512, HD), kv_vm[p1, :, 0].reshape(512, HD)], axis=0)
        v = jnp.concatenate([kv_vm[p0, :, 1].reshape(512, HD), kv_vm[p1, :, 1].reshape(512, HD)], axis=0)
        v_one = jnp.concatenate([v, jnp.ones((1024, HD), BF16)], axis=1)
        for h in range(4):
            for r in range(2):
                rows = slice(r * 256, (r + 1) * 256)
                q = q_vm[2 * r:2 * r + 2, :, h * HD:(h + 1) * HD].reshape(256, HD)
                s = lax.dot_general(q, k, (((1,), (1,)), ((), ())), preferred_element_type=F32)
                m_old = m_ref[h, rows]
                m_new = jnp.maximum(m_old, jnp.max(s, axis=1, keepdims=True))
                m_ref[h, rows] = m_new
                alpha = jnp.exp2((m_old - m_new) * fold)
                p = jnp.exp2((s - m_new[:, :1]) * fold)
                added = jnp.dot(p.astype(BF16), v_one, preferred_element_type=F32)
                acc_ref[h, rows] = acc_ref[h, rows] * alpha[:, :1] + added

    for h in range(2):
        for a, step, part in ((1, 1, 0), (3, -1, 1)):
            arrived(h, a, 0)
            go(turn_copy, h, a, part, step)
            second_leg(h, a)
    for h in range(2):
        for b in (1, 3):
            arrived(h, 0, b)
            relay_second(h, 0, b)
    own[2].wait()
    for d in range(1, 4):
        src = (zh + 4 - d) % 4
        rcopy(q_vm.at[src], q_vm.at[src], sq.at[d - 1], rq.at[d - 1], at(x, src, y)).wait_recv()

    order = ((0, 0), (0, 1), (0, 3), (1, 0), (3, 0), (1, 1), (1, 3), (3, 1), (3, 3), (2, 0), (0, 2), (2, 1), (2, 3), (1, 2), (3, 2), (2, 2))

    def step(i, carry):
        def look(values):
            out = 0
            for n, value in enumerate(values):
                if value:
                    out = out + jnp.where(i == n, value, 0)
            return out

        @pl.when(i == 1)
        def _():
            for h in range(2):
                for part in range(2):
                    first_piece(h, part, place(*index(h, 2, 0)), partners[0]).wait_recv()
                second_leg(h, 2)
            for h in range(2):
                for a in (1, 3):
                    for b in (1, 3):
                        arrived(h, a, b)
                        relay_second(h, a, b)

        @pl.when(i == 2)
        def _():
            for h in range(2):
                for b in (1, 3):
                    arrived(h, 2, b)
                    relay_second(h, 2, b)

        @pl.when(i == 3)
        def _():
            for k in range(3):
                down(k).start()

        @pl.when(i == 4)
        def _():
            pieces(1, 0)

        @pl.when(i == 5)
        def _():
            pieces(0, 0)
            pieces(1, 1)

        @pl.when(i == 6)
        def _():
            pieces(1, 3)
            pieces(0, 1)

        @pl.when(i == 7)
        def _():
            pieces(0, 3)
            pieces(0, 2)
            pieces(1, 2)

        p0 = place(look([order[2 * n][0] for n in range(8)]), look([order[2 * n][1] for n in range(8)]))
        p1 = place(look([order[2 * n + 1][0] for n in range(8)]), look([order[2 * n + 1][1] for n in range(8)]))
        absorb(p0, p1)
        return carry

    lax.fori_loop(0, 8, step, 0)
    for h in range(4):
        total = acc_ref[h]
        ao[:, :, h * HD:(h + 1) * HD] = (total[:, :HD] / total[:, HD:]).astype(BF16).reshape(4, 128, HD)

    def come_down():
        for k in range(3):
            part = wd.at[quarters[k], mine]
            rcopy(part, part, sw.at[k], rw.at[k], partners[k]).wait_recv()
            share(k).start()

    def finish():
        own[3].wait()
        for k in range(3):
            part = wd.at[quarters[k], other]
            rcopy(part, part, st.at[k], rt.at[k], sibling).wait_recv()

    def drain():
        for c in first:
            c.wait_send()
        for make, rest in sends:
            make(*rest).wait_send()
        for k in range(3):
            down(k).wait_send()
            share(k).wait_send()

    return come_down, finish, drain


CHUNKS = 8


def layer_kernel(
    q_ref, k_ref, v_ref, resid_ref, gain_ref, ids_ref, gates_ref, wg_ref, wu_ref, wd_ref, out_ref,
    q_vm, kv_vm, m_ref, acc_ref, ao,
    att, rbuf, stream_ref, ssq, ssq_in, sbuf, xall, wg, wu, wd, acts, outgoing, back,
    s1, r1, sq, rq, sa, ra, sb, rb, sap, rap, sbp, rbp, sw, rw, st, rt, lsem_a,
    sh_heads, rh_heads, ss, rs, sd, rd, sf, rf, sf2, rf2, sh, rh, sr, rr, lsem,
):
    me, x, zh, y = coords()
    sec = lax.axis_index("sec")
    j_me = me % 2
    e_me = me // 2
    low = me % 8
    partners, quarters, q_me = square(me, sec)
    half = pl.ds(pl.multiple_of(sec * 2048, 2048), 2048)
    fetch = pltpu.make_async_copy(resid_ref.at[:, half], rbuf, lsem.at[0])
    fetch.start()
    weights = [
        pltpu.make_async_copy(wg_ref.at[0], wg, lsem.at[3]),
        pltpu.make_async_copy(wu_ref.at[0], wu, lsem.at[4]),
    ]
    for c in weights:
        c.start()
    come_down, finish_down, drain_attention = attend(
        q_ref, k_ref, v_ref, wd_ref, ao, wd, q_vm, kv_vm, m_ref, acc_ref,
        s1, r1, sq, rq, sa, ra, sb, rb, sap, rap, sbp, rbp, sw, rw, st, rt, lsem_a,
    )
    keep = pltpu.make_async_copy(ao.at[zh], att.at[zh], lsem.at[1])
    keep.start()
    heads = []
    for d in range(1, 4):
        j = (zh + d) % 4
        heads.append(rcopy(ao.at[j], att.at[zh], sh_heads.at[d - 1], rh_heads.at[d - 1], {"dev": x * 16 + j * 4 + y}))
    for c in heads:
        c.start()
    come_down()

    r8, first, slot = one_hot(ids_ref)
    pick = jnp.where(slot == r8, 1.0, 0.0).astype(BF16)
    fold = [jnp.where((slot == 8 + r8 // 4) & (r8 % 4 == p), 1.0, 0.0).astype(BF16) for p in range(4)]

    fetch.wait()
    keep.wait()
    for d in range(1, 4):
        src = (zh + 4 - d) % 4
        rcopy(ao.at[src], att.at[src], sh_heads.at[d - 1], rh_heads.at[d - 1], {"dev": x * 16 + src * 4 + y}).wait_recv()
    total = jnp.zeros((128, 1), F32)
    for g in range(4):
        part = rbuf[:, g * 512:(g + 1) * 512].astype(F32) + att[g].astype(F32)
        stream_ref[:, g * 512:(g + 1) * 512] = part
        total = total + jnp.sum(part * part, axis=1, keepdims=True)
    ssq[...] = jnp.broadcast_to(total, (128, 128))
    cross = rcopy(ssq, ssq_in, ss, rs, {"sec": 1 - sec})
    cross.start()
    cross.wait()
    scale = lax.rsqrt((ssq[:, :1] + ssq_in[:, :1]) * (1.0 / 4096) + 1e-06)
    for j in range(2):
        normed = []
        for p in range(4):
            at = j * 1024 + p * 256
            g = gain_ref[:, pl.ds(pl.multiple_of(sec * 2048 + at, 256), 256)]
            normed.append((stream_ref[:, at:at + 256] * scale * g).astype(BF16))
        extra = jnp.zeros((256, 256), F32)
        for p in range(4):
            main = jnp.dot(pick, normed[p], preferred_element_type=F32)
            sbuf[j, :, :, p * 256:(p + 1) * 256] = main.reshape(32, 8, 256).astype(BF16)
            extra = extra + jnp.dot(fold[p], normed[p], preferred_element_type=F32)
        sbuf[j, :, :, 1024:1280] = extra.reshape(32, 8, 256).astype(BF16)

    def ahead(c):
        return ((x + c // 2) % 4) * 16 + ((zh // 2 + c) % 2) * 8

    def behind(c):
        return ((x + 4 - c // 2) % 4) * 16 + ((zh // 2 + c) % 2) * 8

    def rows_to(dest, c):
        j, e = dest % 2, dest // 2
        return rcopy(sbuf.at[j, e], xall.at[2 * sec + j, me], sd.at[c], rd.at[c], {"dev": dest})

    def send_rows(c, start):
        def one(t, carry):
            rows_to(ahead(c) + (low + t) % 8, c).start()
            return carry

        lax.fori_loop(start, 8, one, 0)

    def block(q, c):
        return xall.at[q, pl.ds(behind(c), 8)]

    def counted(n, send_sem, recv_sem):
        ref = outgoing.at[pl.ds(0, n)]
        return rcopy(ref, ref, send_sem, recv_sem, partners[0])

    def pass_on(k, c):
        return rcopy(block(q_me, c), block(q_me, c), sf.at[k, c], rf.at[k, c], partners[k])

    def came(k, c):
        return rcopy(block(quarters[k], c), block(quarters[k], c), sf.at[k, c], rf.at[k, c], partners[0])

    def second_rows(c, k):
        return pl.ds(behind(c), 5) if k == 0 else pl.ds(behind(c) + 5, 3)

    def second_hop(k, c):
        ref = xall.at[quarters[1 - k], second_rows(c, k)]
        return rcopy(ref, ref, sf2.at[k, c], rf2.at[k, c], partners[k])

    def came_far(k, c):
        ref = xall.at[quarters[2], second_rows(c, k)]
        return rcopy(ref, ref, sf2.at[k, c], rf2.at[k, c], partners[0])

    def act_to(k, c):
        return rcopy(acts.at[q_me, c], acts.at[q_me, c], sh.at[k, c], rh.at[k, c], partners[k])

    def act_from(k, c):
        ref = acts.at[quarters[k], c]
        return rcopy(ref, ref, sh.at[k, c], rh.at[k, c], partners[k])

    def result_to(dest, c):
        return rcopy(outgoing.at[dest], back.at[j_me, e_me], sr.at[c], rr.at[c], {"dev": dest})

    own_rows = pltpu.make_async_copy(sbuf.at[j_me, e_me], xall.at[q_me, me], lsem.at[2])
    own_rows.start()
    own_back = pltpu.make_async_copy(outgoing.at[me], back.at[j_me, e_me], lsem.at[5])
    send_rows(0, 1)
    send_rows(1, 0)
    send_rows(2, 0)
    own_rows.wait()
    for c in weights:
        c.wait()
    finish_down()

    def relay(c):
        @pl.when(c == 0)
        def _():
            ref = xall.at[q_me, pl.ds(behind(0), 7)]
            rcopy(ref, ref, sd.at[0], rd.at[0], partners[0]).wait_recv()

        @pl.when(c > 0)
        def _():
            rcopy(block(q_me, c), block(q_me, c), sd.at[c], rd.at[c], partners[0]).wait_recv()

        pass_on(1, c).start()
        pass_on(0, c).start()

        @pl.when(c == 0)
        def _():
            counted(7, sd.at[0], rd.at[0]).wait_send()
            send_rows(3, 0)

        @pl.when((c > 0) & (c + 3 < CHUNKS))
        def _():
            counted(8, sd.at[c], rd.at[c]).wait_send()
            send_rows(c + 3, 0)

    def relay_far(c):
        came(1, c).wait_recv()
        second_hop(0, c).start()
        came(0, c).wait_recv()
        second_hop(1, c).start()

    def hidden(c):
        came_far(0, c).wait_recv()
        came_far(1, c).wait_recv()
        rows = []
        for q in range(4):
            data = xall[q, pl.ds(behind(c), 8)].astype(F32).reshape(64, 1280).astype(BF16)
            over = jnp.concatenate([unfold(data[:, 1024:], p) for p in range(4)], axis=1)
            rows.append(jnp.concatenate([data[:, :1024], over], axis=0))
        rows = jnp.concatenate(rows, axis=1)
        g = jnp.dot(rows, wg[...], preferred_element_type=F32)
        u = jnp.dot(rows, wu[...], preferred_element_type=F32)
        acts[q_me, c] = (g / (1.0 + jnp.exp(-g)) * u).astype(BF16)
        for k in (2, 1, 0):
            act_to(k, c).start()

    def output(c):
        for k in range(3):
            act_from(k, c).wait_recv()
        part = jnp.dot(acts[0, c], wd[0], preferred_element_type=F32)
        for q in range(1, 4):
            part = part + jnp.dot(acts[q, c], wd[q], preferred_element_type=F32)
        outgoing[pl.ds(behind(c), 8), :, 0:1024] = part[:64].reshape(8, 8, 1024).astype(BF16)
        over = part[64:].astype(BF16)
        extra = refold(over[:, 0:256], 0)
        for p in range(1, 4):
            extra = extra + refold(over[:, p * 256:(p + 1) * 256], p)
        outgoing[pl.ds(behind(c), 8), :, 1024:1280] = extra.reshape(8, 8, 256).astype(BF16)

        @pl.when(c == 0)
        def _():
            own_back.start()

        def one(t, carry):
            result_to(behind(c) + (low + t) % 8, c).start()
            return carry

        lax.fori_loop(jnp.where(c == 0, 1, 0), 8, one, 0)

    def stage(c, carry):
        @pl.when(c < CHUNKS)
        def _():
            relay(c)

        @pl.when((c >= 1) & (c < CHUNKS + 1))
        def _():
            relay_far(c - 1)

        @pl.when((c >= 2) & (c < CHUNKS + 2))
        def _():
            hidden(c - 2)

        @pl.when(c >= 3)
        def _():
            output(c - 3)

        return carry

    lax.fori_loop(0, CHUNKS + 3, stage, 0)
    own_back.wait()
    counted(7, sr.at[0], rr.at[0]).wait_send()
    ref = back.at[0, pl.ds(0, 7)]
    rcopy(ref, ref, sr.at[0], rr.at[0], partners[0]).wait_recv()

    def arrive(c, carry):
        ref = back.at[:, pl.ds(ahead(c) // 2, 4)]
        rcopy(ref, ref, sr.at[c], rr.at[c], partners[0]).wait_recv()
        counted(8, sr.at[c], rr.at[c]).wait_send()
        return carry

    lax.fori_loop(1, CHUNKS, arrive, 0)

    r8, first, slot = one_hot(ids_ref)
    weight = jnp.where(first, gates_ref[0:1, :], gates_ref[1:2, :])

    def split(mask):
        w = jnp.where(mask, weight, 0.0).T
        high = w.astype(BF16)
        return high, (w - high.astype(F32)).astype(BF16)

    def weigh(pair, data):
        return jnp.dot(pair[0], data, preferred_element_type=F32) + jnp.dot(pair[1], data, preferred_element_type=F32)

    main_pick = split(slot == r8)
    fold_pick = [split((slot == 8 + r8 // 4) & (r8 % 4 == p)) for p in range(4)]
    for j in range(2):
        extra = back[j, :, :, 1024:1280].astype(F32).reshape(256, 256).astype(BF16)
        for p in range(4):
            at = j * 1024 + p * 256
            data = back[j, :, :, p * 256:(p + 1) * 256].astype(F32).reshape(256, 256).astype(BF16)
            moe = weigh(main_pick, data) + weigh(fold_pick[p], extra)
            out_ref[:, at:at + 256] = (stream_ref[:, at:at + 256] + moe).astype(BF16)

    drain_attention()
    for c in heads:
        c.wait_send()
    for c in range(CHUNKS - 3, CHUNKS):
        counted(8, sd.at[c], rd.at[c]).wait_send()

    def drain(c, carry):
        for k in range(2):
            pass_on(k, c).wait_send()
            second_hop(k, c).wait_send()
        for k in range(3):
            act_to(k, c).wait_send()
        return carry

    lax.fori_loop(0, CHUNKS, drain, 0)


def unfold(extra, p):
    want = 4 * lax.broadcasted_iota(jnp.int32, (16, 64), 0) + p == lax.broadcasted_iota(jnp.int32, (16, 64), 1)
    return jnp.dot(jnp.where(want, 1.0, 0.0).astype(BF16), extra, preferred_element_type=F32).astype(BF16)


def refold(rows, p):
    want = 4 * lax.broadcasted_iota(jnp.int32, (64, 16), 1) + p == lax.broadcasted_iota(jnp.int32, (64, 16), 0)
    return jnp.dot(jnp.where(want, 1.0, 0.0).astype(BF16), rows, preferred_element_type=F32)


def body(resid, queries, keys, values, norm_gain, expert_ids, gate_weights, w_gate, w_up, w_down):
    dma = pltpu.SemaphoreType.DMA
    hidden = w_gate.shape[2]
    return pl.pallas_call(
        layer_kernel,
        out_shape=jax.ShapeDtypeStruct((128, 2048), BF16),
        in_specs=[ANY, ANY, ANY, ANY, VMEM, VMEM, VMEM, ANY, ANY, ANY],
        out_specs=VMEM,
        scratch_shapes=[
            pltpu.VMEM((4, 128, 4 * HD), BF16),
            pltpu.VMEM((16, 4, 2, 128, HD), BF16),
            pltpu.VMEM((4, 512, HD), F32),
            pltpu.VMEM((4, 512, 2 * HD), F32),
            pltpu.VMEM((4, 128, 512), BF16),
            pltpu.VMEM((4, 128, 512), BF16),
            pltpu.VMEM((128, 2048), BF16),
            pltpu.VMEM((128, 2048), F32),
            pltpu.VMEM((128, 128), F32),
            pltpu.VMEM((128, 128), F32),
            pltpu.VMEM((2, 32, 8, 1280), BF16),
            pltpu.VMEM((4, 64, 8, 1280), BF16),
            pltpu.VMEM((4096, hidden), BF16),
            pltpu.VMEM((4096, hidden), BF16),
            pltpu.VMEM((4, hidden, 1024), BF16),
            pltpu.VMEM((4, CHUNKS, 640 // CHUNKS, hidden), BF16),
            pltpu.VMEM((64, 8, 1280), BF16),
            pltpu.VMEM((2, 32, 8, 1280), BF16),
            dma((3, 2)), dma((3, 2)), dma((3,)), dma((3,)),
            dma((4, 4)), dma((4, 4)), dma((4, 4)), dma((4, 4)),
            dma((5, 2)), dma((5, 2)), dma((5, 2)), dma((5, 2)),
            dma((3,)), dma((3,)), dma((3,)), dma((3,)), dma((4,)),
            dma((3,)), dma((3,)), dma, dma, dma((CHUNKS,)), dma((CHUNKS,)),
            dma((2, CHUNKS)), dma((2, CHUNKS)), dma((2, CHUNKS)), dma((2, CHUNKS)),
            dma((3, CHUNKS)), dma((3, CHUNKS)), dma((CHUNKS,)), dma((CHUNKS,)), dma((6,)),
        ],
        compiler_params=pltpu.CompilerParams(
            collective_id=0, has_side_effects=True, vmem_limit_bytes=VMEM_BYTES
        ),
    )(
        queries, keys, values, resid, norm_gain.reshape(1, -1), expert_ids.T, gate_weights.T, w_gate, w_up, w_down
    )


def solution(mesh):
    in_specs = (
        P(("rep", "dev"), None),
        P(("rep", "dev"), "sec"),
        P(("rep", "dev"), "sec"),
        P(("rep", "dev"), "sec"),
        P(),
        P(("rep", "dev"), None),
        P(("rep", "dev"), None),
        P("dev", None, "sec"),
        P("dev", None, "sec"),
        P("dev", "sec", None),
    )
    out_specs = P(("rep", "dev"), "sec")
    return jax.shard_map(body, mesh=mesh, in_specs=in_specs, out_specs=out_specs, check_vma=False)
```

```python
import math

import jax
import jax.numpy as jnp
from jax import lax
from jax.experimental import pallas as pl
from jax.experimental.pallas import tpu as pltpu
from jax.sharding import PartitionSpec as P

HD = 128
MESH = pl.DeviceIdType.MESH
F32 = jnp.float32
BF16 = jnp.bfloat16
VMEM_BYTES = 58 * 1024 * 1024
ANY = pl.BlockSpec(memory_space=pl.ANY)
VMEM = pl.BlockSpec(memory_space=pltpu.VMEM)


def rcopy(src, dst, send_sem, recv_sem, device_id):
    return pltpu.make_async_remote_copy(
        src_ref=src,
        dst_ref=dst,
        send_sem=send_sem,
        recv_sem=recv_sem,
        device_id=device_id,
        device_id_type=MESH,
    )


def coords():
    me = lax.axis_index("dev")
    return me, me // 16, (me // 4) % 4, me % 4


def twin(me):
    return me + 1 - 2 * (me % 2)


def square(me, sec):
    j = me % 2
    partners = ({"dev": twin(me)}, {"sec": 1 - sec}, {"dev": twin(me), "sec": 1 - sec})
    quarters = (2 * sec + 1 - j, 2 * (1 - sec) + j, 2 * (1 - sec) + 1 - j)
    return partners, quarters, 2 * sec + j


def greet(me, sec, rep):
    barrier = pltpu.get_barrier_semaphore()

    def one(i, carry):
        pl.semaphore_signal(barrier, inc=1, device_id={"dev": (me + i) % 64}, device_id_type=MESH)
        return carry

    lax.fori_loop(1, 64, one, 0)
    for peer in ({"sec": 1 - sec}, {"sec": 1 - sec, "dev": twin(me)}, {"rep": 1 - rep}):
        pl.semaphore_signal(barrier, inc=1, device_id=peer, device_id_type=MESH)
    pl.semaphore_wait(barrier, 66)


def one_hot(ids_ref):
    row = lax.broadcasted_iota(jnp.int32, (256, 128), 0)
    expert = row // 8
    first = expert == ids_ref[0:1, :]
    second = expert == ids_ref[1:2, :]
    named = jnp.where(first | second, 1.0, 0.0)
    before = lax.broadcasted_iota(jnp.int32, (128, 128), 0) < lax.broadcasted_iota(jnp.int32, (128, 128), 1)
    slot = jnp.dot(named.astype(BF16), jnp.where(before, 1.0, 0.0).astype(BF16), preferred_element_type=F32)
    slot = jnp.where(named > 0.5, slot, -1.0).astype(jnp.int32)
    return row % 8, first, slot


def attend(
    q_ref, k_ref, v_ref, wd_ref, ao, wd, q_vm, kv_vm, m_ref, acc_ref,
    s1, r1, sq, rq, sa, ra, sb, rb, sap, rap, sbp, rbp, sw, rw, st, rt, lsem,
):
    me, x, zh, y = coords()
    pos = x * 4 + y
    sec = lax.axis_index("sec")
    rep = lax.axis_index("rep")
    partners, quarters, q_me = square(me, sec)
    sibling = {"rep": 1 - rep}
    fold = math.log2(math.e) / math.sqrt(HD)

    def at(xx, zz, yy):
        return {"dev": ((xx + 4) % 4) * 16 + zz * 4 + (yy + 4) % 4}

    def cols(j, w):
        return pl.ds(pl.multiple_of(j * w, w), w)

    own = [
        pltpu.make_async_copy(k_ref.at[:, cols(zh, HD)], kv_vm.at[pos, zh, 0], lsem.at[0]),
        pltpu.make_async_copy(v_ref.at[:, cols(zh, HD)], kv_vm.at[pos, zh, 1], lsem.at[1]),
        pltpu.make_async_copy(q_ref.at[:, cols(zh, 4 * HD)], q_vm.at[zh], lsem.at[2]),
        pltpu.make_async_copy(wd_ref.at[0, :, cols(q_me, 1024)], wd.at[q_me], lsem.at[3]),
    ]
    for c in own:
        c.start()
    greet(me, sec, rep)

    hid = wd_ref.shape[1] // 2
    mine = pl.ds(pl.multiple_of(rep * hid, hid), hid)
    other = pl.ds(pl.multiple_of((1 - rep) * hid, hid), hid)

    def down(k):
        return rcopy(wd_ref.at[0, mine, cols(quarters[k], 1024)], wd.at[q_me, mine], sw.at[k], rw.at[k], partners[k])

    def share(k):
        part = wd.at[quarters[k], mine]
        return rcopy(part, part, st.at[k], rt.at[k], sibling)

    first = []
    for d in range(1, 4):
        j = (zh + d) % 4
        first.append(rcopy(k_ref.at[:, cols(j, HD)], kv_vm.at[pos, zh, 0], s1.at[d - 1, 0], r1.at[d - 1, 0], at(x, j, y)))
        first.append(rcopy(v_ref.at[:, cols(j, HD)], kv_vm.at[pos, zh, 1], s1.at[d - 1, 1], r1.at[d - 1, 1], at(x, j, y)))
    for d in range(1, 4):
        j = (zh + d) % 4
        first.append(rcopy(q_ref.at[:, cols(j, 4 * HD)], q_vm.at[zh], sq.at[d - 1], rq.at[d - 1], at(x, j, y)))
    for c in first:
        c.start()
    m_ref[...] = jnp.full(m_ref.shape, -1e30, F32)
    acc_ref[...] = jnp.zeros(acc_ref.shape, F32)
    own[0].wait()
    own[1].wait()
    for d in range(1, 4):
        src = (zh + 4 - d) % 4
        for w in range(2):
            rcopy(kv_vm.at[pos, src, w], kv_vm.at[pos, src, w], s1.at[d - 1, w], r1.at[d - 1, w], at(x, src, y)).wait_recv()

    def place(ex, ey):
        return ((x + 4 - ex) % 4) * 4 + (y + 4 - ey) % 4

    def copy_of(h, ex, ey, p, dest):
        ref = kv_vm.at[p, pl.ds(2 * h, 2)]
        send, recv = (sa, ra) if h == 0 else (sb, rb)
        return rcopy(ref, ref, send.at[ex, ey], recv.at[ex, ey], dest)

    def piece_of(h, ex, ey, part, p, dest):
        ref = kv_vm.at[p, 2 * h + part]
        send, recv = (sap, rap) if h == 0 else (sbp, rbp)
        line = ey if h == 1 else ex
        return rcopy(ref, ref, send.at[line, part], recv.at[line, part], dest)

    def axis_to(h, second, step):
        return at(x + step, zh, y) if (h == 0) != second else at(x, zh, y + step)

    sends = []

    def go(make, *rest):
        make(*rest).start()
        sends.append((make, rest))

    def index(h, a, b):
        return (a, b) if h == 0 else (b, a)

    def arrived(h, a, b):
        ex, ey = index(h, a, b)
        copy_of(h, ex, ey, place(ex, ey), partners[0]).wait_recv()

    def leg_copy(h, a, b, step):
        ex, ey = index(h, a, b)
        return copy_of(h, ex, ey, place(*index(h, a, 0)), axis_to(h, True, step))

    def second_leg(h, a):
        for b, step in ((1, 1), (3, -1)):
            go(leg_copy, h, a, b, step)

    def piece_copy(h, a, b):
        part, step = (0, 1) if b == 1 else (1, -1)
        ex, ey = index(h, a, 2)
        return piece_of(h, ex, ey, part, place(*index(h, a, b)), axis_to(h, True, step))

    def relay_second(h, a, b):
        go(piece_copy, h, a, b)

    def pieces(h, a):
        ex, ey = index(h, a, 2)
        for part in range(2):
            piece_of(h, ex, ey, part, place(ex, ey), partners[0]).wait_recv()

    def first_piece(h, part, p, dest):
        ref = kv_vm.at[p, 2 * h + part]
        send, recv = (sap, rap) if h == 0 else (sbp, rbp)
        return rcopy(ref, ref, send.at[4, part], recv.at[4, part], dest)

    def start_copy(h, a, step):
        ex, ey = index(h, a, 0)
        return copy_of(h, ex, ey, pos, axis_to(h, False, step))

    def turn_copy(h, a, part, step):
        return first_piece(h, part, place(*index(h, a, 0)), axis_to(h, False, step))

    for h in range(2):
        for a, step in ((1, 1), (3, -1)):
            go(start_copy, h, a, step)
    for h in range(2):
        second_leg(h, 0)

    def absorb(p0, p1):
        k = jnp.concatenate([kv_vm[p0, :, 0].reshape(512, HD), kv_vm[p1, :, 0].reshape(512, HD)], axis=0)
        v = jnp.concatenate([kv_vm[p0, :, 1].reshape(512, HD), kv_vm[p1, :, 1].reshape(512, HD)], axis=0)
        v_one = jnp.concatenate([v, jnp.ones((1024, HD), BF16)], axis=1)
        for h in range(4):
            for r in range(2):
                rows = slice(r * 256, (r + 1) * 256)
                q = q_vm[2 * r:2 * r + 2, :, h * HD:(h + 1) * HD].reshape(256, HD)
                s = lax.dot_general(q, k, (((1,), (1,)), ((), ())), preferred_element_type=F32)
                m_old = m_ref[h, rows]
                m_new = jnp.maximum(m_old, jnp.max(s, axis=1, keepdims=True))
                m_ref[h, rows] = m_new
                alpha = jnp.exp2((m_old - m_new) * fold)
                p = jnp.exp2((s - m_new[:, :1]) * fold)
                added = jnp.dot(p.astype(BF16), v_one, preferred_element_type=F32)
                acc_ref[h, rows] = acc_ref[h, rows] * alpha[:, :1] + added

    for h in range(2):
        for a, step, part in ((1, 1, 0), (3, -1, 1)):
            arrived(h, a, 0)
            go(turn_copy, h, a, part, step)
            second_leg(h, a)
    for h in range(2):
        for b in (1, 3):
            arrived(h, 0, b)
            relay_second(h, 0, b)
    own[2].wait()
    for d in range(1, 4):
        src = (zh + 4 - d) % 4
        rcopy(q_vm.at[src], q_vm.at[src], sq.at[d - 1], rq.at[d - 1], at(x, src, y)).wait_recv()

    order = ((0, 0), (0, 1), (0, 3), (1, 0), (3, 0), (1, 1), (1, 3), (3, 1), (3, 3), (2, 0), (0, 2), (2, 1), (2, 3), (1, 2), (3, 2), (2, 2))

    def step(i, carry):
        def look(values):
            out = 0
            for n, value in enumerate(values):
                if value:
                    out = out + jnp.where(i == n, value, 0)
            return out

        @pl.when(i == 2)
        def _():
            for h in range(2):
                for part in range(2):
                    first_piece(h, part, place(*index(h, 2, 0)), partners[0]).wait_recv()
                second_leg(h, 2)
            for h in range(2):
                for a in (1, 3):
                    for b in (1, 3):
                        arrived(h, a, b)
                        relay_second(h, a, b)

        @pl.when(i == 3)
        def _():
            for h in range(2):
                for b in (1, 3):
                    arrived(h, 2, b)
                    relay_second(h, 2, b)

        @pl.when(i == 0)
        def _():
            down(1).start()

        @pl.when(i == 4)
        def _():
            down(0).start()
            pieces(1, 0)

        @pl.when(i == 5)
        def _():
            down(2).start()
            pieces(0, 0)
            pieces(1, 1)

        @pl.when(i == 6)
        def _():
            pieces(1, 3)
            pieces(0, 1)

        @pl.when(i == 7)
        def _():
            pieces(0, 3)
            pieces(0, 2)
            pieces(1, 2)

        p0 = place(look([order[2 * n][0] for n in range(8)]), look([order[2 * n][1] for n in range(8)]))
        p1 = place(look([order[2 * n + 1][0] for n in range(8)]), look([order[2 * n + 1][1] for n in range(8)]))
        absorb(p0, p1)
        return carry

    lax.fori_loop(0, 8, step, 0)
    for h in range(4):
        total = acc_ref[h]
        ao[:, :, h * HD:(h + 1) * HD] = (total[:, :HD] / total[:, HD:]).astype(BF16).reshape(4, 128, HD)

    def come_down():
        for k in range(3):
            part = wd.at[quarters[k], mine]
            rcopy(part, part, sw.at[k], rw.at[k], partners[k]).wait_recv()
            share(k).start()

    def finish():
        own[3].wait()
        for k in range(3):
            part = wd.at[quarters[k], other]
            rcopy(part, part, st.at[k], rt.at[k], sibling).wait_recv()

    def drain():
        for c in first:
            c.wait_send()
        for make, rest in sends:
            make(*rest).wait_send()
        for k in range(3):
            down(k).wait_send()
            share(k).wait_send()

    return come_down, finish, drain


CHUNKS = 8


def layer_kernel(
    q_ref, k_ref, v_ref, resid_ref, gain_ref, ids_ref, gates_ref, wg_ref, wu_ref, wd_ref, out_ref,
    q_vm, kv_vm, m_ref, acc_ref, ao,
    att, rbuf, stream_ref, ssq, ssq_in, sbuf, xall, wg, wu, wd, acts, outgoing, back,
    s1, r1, sq, rq, sa, ra, sb, rb, sap, rap, sbp, rbp, sw, rw, st, rt, lsem_a,
    sh_heads, rh_heads, ss, rs, sd, rd, sf, rf, sf2, rf2, sh, rh, sr, rr, lsem,
):
    me, x, zh, y = coords()
    sec = lax.axis_index("sec")
    j_me = me % 2
    e_me = me // 2
    low = me % 8
    partners, quarters, q_me = square(me, sec)
    half = pl.ds(pl.multiple_of(sec * 2048, 2048), 2048)
    fetch = pltpu.make_async_copy(resid_ref.at[:, half], rbuf, lsem.at[0])
    fetch.start()
    weights = [
        pltpu.make_async_copy(wg_ref.at[0], wg, lsem.at[3]),
        pltpu.make_async_copy(wu_ref.at[0], wu, lsem.at[4]),
    ]
    for c in weights:
        c.start()
    come_down, finish_down, drain_attention = attend(
        q_ref, k_ref, v_ref, wd_ref, ao, wd, q_vm, kv_vm, m_ref, acc_ref,
        s1, r1, sq, rq, sa, ra, sb, rb, sap, rap, sbp, rbp, sw, rw, st, rt, lsem_a,
    )
    keep = pltpu.make_async_copy(ao.at[zh], att.at[zh], lsem.at[1])
    keep.start()
    heads = []
    for d in range(1, 4):
        j = (zh + d) % 4
        heads.append(rcopy(ao.at[j], att.at[zh], sh_heads.at[d - 1], rh_heads.at[d - 1], {"dev": x * 16 + j * 4 + y}))
    for c in heads:
        c.start()
    come_down()

    r8, first, slot = one_hot(ids_ref)
    pick = jnp.where(slot == r8, 1.0, 0.0).astype(BF16)
    fold = [jnp.where((slot == 8 + r8 // 4) & (r8 % 4 == p), 1.0, 0.0).astype(BF16) for p in range(4)]

    fetch.wait()
    keep.wait()
    for d in range(1, 4):
        src = (zh + 4 - d) % 4
        rcopy(ao.at[src], att.at[src], sh_heads.at[d - 1], rh_heads.at[d - 1], {"dev": x * 16 + src * 4 + y}).wait_recv()
    total = jnp.zeros((128, 1), F32)
    for g in range(4):
        part = rbuf[:, g * 512:(g + 1) * 512].astype(F32) + att[g].astype(F32)
        stream_ref[:, g * 512:(g + 1) * 512] = part
        total = total + jnp.sum(part * part, axis=1, keepdims=True)
    ssq[...] = jnp.broadcast_to(total, (128, 128))
    cross = rcopy(ssq, ssq_in, ss, rs, {"sec": 1 - sec})
    cross.start()
    cross.wait()
    scale = lax.rsqrt((ssq[:, :1] + ssq_in[:, :1]) * (1.0 / 4096) + 1e-06)
    for j in range(2):
        normed = []
        for p in range(4):
            at = j * 1024 + p * 256
            g = gain_ref[:, pl.ds(pl.multiple_of(sec * 2048 + at, 256), 256)]
            normed.append((stream_ref[:, at:at + 256] * scale * g).astype(BF16))
        extra = jnp.zeros((256, 256), F32)
        for p in range(4):
            main = jnp.dot(pick, normed[p], preferred_element_type=F32)
            sbuf[j, :, :, p * 256:(p + 1) * 256] = main.reshape(32, 8, 256).astype(BF16)
            extra = extra + jnp.dot(fold[p], normed[p], preferred_element_type=F32)
        sbuf[j, :, :, 1024:1280] = extra.reshape(32, 8, 256).astype(BF16)

    def ahead(c):
        return ((x + c // 2) % 4) * 16 + ((zh // 2 + c) % 2) * 8

    def behind(c):
        return ((x + 4 - c // 2) % 4) * 16 + ((zh // 2 + c) % 2) * 8

    def rows_to(dest, c):
        j, e = dest % 2, dest // 2
        return rcopy(sbuf.at[j, e], xall.at[2 * sec + j, me], sd.at[c], rd.at[c], {"dev": dest})

    def send_rows(c, start):
        def one(t, carry):
            rows_to(ahead(c) + (low + t) % 8, c).start()
            return carry

        lax.fori_loop(start, 8, one, 0)

    def block(q, c):
        return xall.at[q, pl.ds(behind(c), 8)]

    def counted(n, send_sem, recv_sem):
        ref = outgoing.at[pl.ds(0, n)]
        return rcopy(ref, ref, send_sem, recv_sem, partners[0])

    def pass_on(k, c):
        return rcopy(block(q_me, c), block(q_me, c), sf.at[k, c], rf.at[k, c], partners[k])

    def came(k, c):
        return rcopy(block(quarters[k], c), block(quarters[k], c), sf.at[k, c], rf.at[k, c], partners[0])

    def second_rows(c, k):
        return pl.ds(behind(c), 5) if k == 0 else pl.ds(behind(c) + 5, 3)

    def second_hop(k, c):
        ref = xall.at[quarters[1 - k], second_rows(c, k)]
        return rcopy(ref, ref, sf2.at[k, c], rf2.at[k, c], partners[k])

    def came_far(k, c):
        ref = xall.at[quarters[2], second_rows(c, k)]
        return rcopy(ref, ref, sf2.at[k, c], rf2.at[k, c], partners[0])

    def act_to(k, c):
        ref = acts.at[quarters[1] if k == 2 else q_me, c]
        return rcopy(ref, ref, sh.at[k, c], rh.at[k, c], partners[1 if k == 1 else 0])

    def act_from(k, c):
        ref = acts.at[quarters[k], c]
        return rcopy(ref, ref, sh.at[k, c], rh.at[k, c], partners[k])

    def result_to(dest, c):
        return rcopy(outgoing.at[dest], back.at[j_me, e_me], sr.at[c], rr.at[c], {"dev": dest})

    own_rows = pltpu.make_async_copy(sbuf.at[j_me, e_me], xall.at[q_me, me], lsem.at[2])
    own_rows.start()
    own_back = pltpu.make_async_copy(outgoing.at[me], back.at[j_me, e_me], lsem.at[5])
    send_rows(0, 1)
    send_rows(1, 0)
    send_rows(2, 0)
    own_rows.wait()
    for c in weights:
        c.wait()
    finish_down()

    def relay(c):
        @pl.when(c == 0)
        def _():
            ref = xall.at[q_me, pl.ds(behind(0), 7)]
            rcopy(ref, ref, sd.at[0], rd.at[0], partners[0]).wait_recv()

        @pl.when(c > 0)
        def _():
            rcopy(block(q_me, c), block(q_me, c), sd.at[c], rd.at[c], partners[0]).wait_recv()

        pass_on(1, c).start()
        pass_on(0, c).start()

        @pl.when(c == 0)
        def _():
            counted(7, sd.at[0], rd.at[0]).wait_send()
            send_rows(3, 0)

        @pl.when((c > 0) & (c + 3 < CHUNKS))
        def _():
            counted(8, sd.at[c], rd.at[c]).wait_send()
            send_rows(c + 3, 0)

    def relay_far(c):
        came(1, c).wait_recv()
        second_hop(0, c).start()
        came(0, c).wait_recv()
        second_hop(1, c).start()

    def hidden(c):
        came_far(0, c).wait_recv()
        came_far(1, c).wait_recv()
        rows = []
        for q in range(4):
            data = xall[q, pl.ds(behind(c), 8)].astype(F32).reshape(64, 1280).astype(BF16)
            over = jnp.concatenate([unfold(data[:, 1024:], p) for p in range(4)], axis=1)
            rows.append(jnp.concatenate([data[:, :1024], over], axis=0))
        rows = jnp.concatenate(rows, axis=1)
        g = jnp.dot(rows, wg[...], preferred_element_type=F32)
        u = jnp.dot(rows, wu[...], preferred_element_type=F32)
        acts[q_me, c] = (g / (1.0 + jnp.exp(-g)) * u).astype(BF16)
        act_to(1, c).start()
        act_to(0, c).start()

    def act_on(c):
        act_from(1, c).wait_recv()
        act_to(2, c).start()

    def output(c):
        act_from(0, c).wait_recv()
        act_from(2, c).wait_recv()
        part = jnp.dot(acts[0, c], wd[0], preferred_element_type=F32)
        for q in range(1, 4):
            part = part + jnp.dot(acts[q, c], wd[q], preferred_element_type=F32)
        outgoing[pl.ds(behind(c), 8), :, 0:1024] = part[:64].reshape(8, 8, 1024).astype(BF16)
        over = part[64:].astype(BF16)
        extra = refold(over[:, 0:256], 0)
        for p in range(1, 4):
            extra = extra + refold(over[:, p * 256:(p + 1) * 256], p)
        outgoing[pl.ds(behind(c), 8), :, 1024:1280] = extra.reshape(8, 8, 256).astype(BF16)

        @pl.when(c == 0)
        def _():
            own_back.start()

        def one(t, carry):
            result_to(behind(c) + (low + t) % 8, c).start()
            return carry

        lax.fori_loop(jnp.where(c == 0, 1, 0), 8, one, 0)

    def stage(c, carry):
        @pl.when(c < CHUNKS)
        def _():
            relay(c)

        @pl.when((c >= 1) & (c < CHUNKS + 1))
        def _():
            relay_far(c - 1)

        @pl.when(c >= 3)
        def _():
            act_on(c - 3)

        @pl.when((c >= 2) & (c < CHUNKS + 2))
        def _():
            hidden(c - 2)

        @pl.when(c >= 3)
        def _():
            output(c - 3)

        return carry

    lax.fori_loop(0, CHUNKS + 3, stage, 0)
    own_back.wait()
    counted(7, sr.at[0], rr.at[0]).wait_send()
    ref = back.at[0, pl.ds(0, 7)]
    rcopy(ref, ref, sr.at[0], rr.at[0], partners[0]).wait_recv()

    def arrive(c, carry):
        ref = back.at[:, pl.ds(ahead(c) // 2, 4)]
        rcopy(ref, ref, sr.at[c], rr.at[c], partners[0]).wait_recv()
        counted(8, sr.at[c], rr.at[c]).wait_send()
        return carry

    lax.fori_loop(1, CHUNKS, arrive, 0)

    r8, first, slot = one_hot(ids_ref)
    weight = jnp.where(first, gates_ref[0:1, :], gates_ref[1:2, :])

    def split(mask):
        w = jnp.where(mask, weight, 0.0).T
        high = w.astype(BF16)
        return high, (w - high.astype(F32)).astype(BF16)

    def weigh(pair, data):
        return jnp.dot(pair[0], data, preferred_element_type=F32) + jnp.dot(pair[1], data, preferred_element_type=F32)

    main_pick = split(slot == r8)
    fold_pick = [split((slot == 8 + r8 // 4) & (r8 % 4 == p)) for p in range(4)]
    for j in range(2):
        extra = back[j, :, :, 1024:1280].astype(F32).reshape(256, 256).astype(BF16)
        for p in range(4):
            at = j * 1024 + p * 256
            data = back[j, :, :, p * 256:(p + 1) * 256].astype(F32).reshape(256, 256).astype(BF16)
            moe = weigh(main_pick, data) + weigh(fold_pick[p], extra)
            out_ref[:, at:at + 256] = (stream_ref[:, at:at + 256] + moe).astype(BF16)

    drain_attention()
    for c in heads:
        c.wait_send()
    for c in range(CHUNKS - 3, CHUNKS):
        counted(8, sd.at[c], rd.at[c]).wait_send()

    def drain(c, carry):
        for k in range(2):
            pass_on(k, c).wait_send()
            second_hop(k, c).wait_send()
        for k in range(3):
            act_to(k, c).wait_send()
        return carry

    lax.fori_loop(0, CHUNKS, drain, 0)


def unfold(extra, p):
    want = 4 * lax.broadcasted_iota(jnp.int32, (16, 64), 0) + p == lax.broadcasted_iota(jnp.int32, (16, 64), 1)
    return jnp.dot(jnp.where(want, 1.0, 0.0).astype(BF16), extra, preferred_element_type=F32).astype(BF16)


def refold(rows, p):
    want = 4 * lax.broadcasted_iota(jnp.int32, (64, 16), 1) + p == lax.broadcasted_iota(jnp.int32, (64, 16), 0)
    return jnp.dot(jnp.where(want, 1.0, 0.0).astype(BF16), rows, preferred_element_type=F32)


def body(resid, queries, keys, values, norm_gain, expert_ids, gate_weights, w_gate, w_up, w_down):
    dma = pltpu.SemaphoreType.DMA
    hidden = w_gate.shape[2]
    return pl.pallas_call(
        layer_kernel,
        out_shape=jax.ShapeDtypeStruct((128, 2048), BF16),
        in_specs=[ANY, ANY, ANY, ANY, VMEM, VMEM, VMEM, ANY, ANY, ANY],
        out_specs=VMEM,
        scratch_shapes=[
            pltpu.VMEM((4, 128, 4 * HD), BF16),
            pltpu.VMEM((16, 4, 2, 128, HD), BF16),
            pltpu.VMEM((4, 512, HD), F32),
            pltpu.VMEM((4, 512, 2 * HD), F32),
            pltpu.VMEM((4, 128, 512), BF16),
            pltpu.VMEM((4, 128, 512), BF16),
            pltpu.VMEM((128, 2048), BF16),
            pltpu.VMEM((128, 2048), F32),
            pltpu.VMEM((128, 128), F32),
            pltpu.VMEM((128, 128), F32),
            pltpu.VMEM((2, 32, 8, 1280), BF16),
            pltpu.VMEM((4, 64, 8, 1280), BF16),
            pltpu.VMEM((4096, hidden), BF16),
            pltpu.VMEM((4096, hidden), BF16),
            pltpu.VMEM((4, hidden, 1024), BF16),
            pltpu.VMEM((4, CHUNKS, 640 // CHUNKS, hidden), BF16),
            pltpu.VMEM((64, 8, 1280), BF16),
            pltpu.VMEM((2, 32, 8, 1280), BF16),
            dma((3, 2)), dma((3, 2)), dma((3,)), dma((3,)),
            dma((4, 4)), dma((4, 4)), dma((4, 4)), dma((4, 4)),
            dma((5, 2)), dma((5, 2)), dma((5, 2)), dma((5, 2)),
            dma((3,)), dma((3,)), dma((3,)), dma((3,)), dma((4,)),
            dma((3,)), dma((3,)), dma, dma, dma((CHUNKS,)), dma((CHUNKS,)),
            dma((2, CHUNKS)), dma((2, CHUNKS)), dma((2, CHUNKS)), dma((2, CHUNKS)),
            dma((3, CHUNKS)), dma((3, CHUNKS)), dma((CHUNKS,)), dma((CHUNKS,)), dma((6,)),
        ],
        compiler_params=pltpu.CompilerParams(
            collective_id=0, has_side_effects=True, vmem_limit_bytes=VMEM_BYTES
        ),
    )(
        queries, keys, values, resid, norm_gain.reshape(1, -1), expert_ids.T, gate_weights.T, w_gate, w_up, w_down
    )


def solution(mesh):
    in_specs = (
        P(("rep", "dev"), None),
        P(("rep", "dev"), "sec"),
        P(("rep", "dev"), "sec"),
        P(("rep", "dev"), "sec"),
        P(),
        P(("rep", "dev"), None),
        P(("rep", "dev"), None),
        P("dev", None, "sec"),
        P("dev", None, "sec"),
        P("dev", "sec", None),
    )
    out_specs = P(("rep", "dev"), "sec")
    return jax.shard_map(body, mesh=mesh, in_specs=in_specs, out_specs=out_specs, check_vma=False)
```

```python
import math

import jax
import jax.numpy as jnp
from jax import lax
from jax.experimental import pallas as pl
from jax.experimental.pallas import tpu as pltpu
from jax.sharding import PartitionSpec as P

HD = 128
MESH = pl.DeviceIdType.MESH
F32 = jnp.float32
BF16 = jnp.bfloat16
VMEM_BYTES = 58 * 1024 * 1024
ANY = pl.BlockSpec(memory_space=pl.ANY)
VMEM = pl.BlockSpec(memory_space=pltpu.VMEM)


def rcopy(src, dst, send_sem, recv_sem, device_id):
    return pltpu.make_async_remote_copy(
        src_ref=src,
        dst_ref=dst,
        send_sem=send_sem,
        recv_sem=recv_sem,
        device_id=device_id,
        device_id_type=MESH,
    )


def coords():
    me = lax.axis_index("dev")
    return me, me // 16, (me // 4) % 4, me % 4


def twin(me):
    return me + 1 - 2 * (me % 2)


def square(me, sec):
    j = me % 2
    partners = ({"dev": twin(me)}, {"sec": 1 - sec}, {"dev": twin(me), "sec": 1 - sec})
    quarters = (2 * sec + 1 - j, 2 * (1 - sec) + j, 2 * (1 - sec) + 1 - j)
    return partners, quarters, 2 * sec + j


def greet(me, sec, rep):
    barrier = pltpu.get_barrier_semaphore()

    def one(i, carry):
        pl.semaphore_signal(barrier, inc=1, device_id={"dev": (me + i) % 64}, device_id_type=MESH)
        return carry

    lax.fori_loop(1, 64, one, 0)
    for peer in ({"sec": 1 - sec}, {"sec": 1 - sec, "dev": twin(me)}, {"rep": 1 - rep}):
        pl.semaphore_signal(barrier, inc=1, device_id=peer, device_id_type=MESH)
    pl.semaphore_wait(barrier, 66)


def one_hot(ids_ref):
    row = lax.broadcasted_iota(jnp.int32, (256, 128), 0)
    expert = row // 8
    first = expert == ids_ref[0:1, :]
    second = expert == ids_ref[1:2, :]
    named = jnp.where(first | second, 1.0, 0.0)
    before = lax.broadcasted_iota(jnp.int32, (128, 128), 0) < lax.broadcasted_iota(jnp.int32, (128, 128), 1)
    slot = jnp.dot(named.astype(BF16), jnp.where(before, 1.0, 0.0).astype(BF16), preferred_element_type=F32)
    slot = jnp.where(named > 0.5, slot, -1.0).astype(jnp.int32)
    return row % 8, first, slot


def attend(
    q_ref, k_ref, v_ref, wd_ref, ao, wd, q_vm, kv_vm, m_ref, acc_ref,
    s1, r1, sq, rq, sa, ra, sb, rb, sap, rap, sbp, rbp, sw, rw, st, rt, lsem,
):
    me, x, zh, y = coords()
    pos = x * 4 + y
    sec = lax.axis_index("sec")
    rep = lax.axis_index("rep")
    partners, quarters, q_me = square(me, sec)
    sibling = {"rep": 1 - rep}
    fold = math.log2(math.e) / math.sqrt(HD)

    def at(xx, zz, yy):
        return {"dev": ((xx + 4) % 4) * 16 + zz * 4 + (yy + 4) % 4}

    def cols(j, w):
        return pl.ds(pl.multiple_of(j * w, w), w)

    own = [
        pltpu.make_async_copy(k_ref.at[:, cols(zh, HD)], kv_vm.at[pos, zh, 0], lsem.at[0]),
        pltpu.make_async_copy(v_ref.at[:, cols(zh, HD)], kv_vm.at[pos, zh, 1], lsem.at[1]),
        pltpu.make_async_copy(q_ref.at[:, cols(zh, 4 * HD)], q_vm.at[zh], lsem.at[2]),
        pltpu.make_async_copy(wd_ref.at[0, :, cols(q_me, 1024)], wd.at[q_me], lsem.at[3]),
    ]
    for c in own:
        c.start()
    greet(me, sec, rep)

    hid = wd_ref.shape[1] // 2
    mine = pl.ds(pl.multiple_of(rep * hid, hid), hid)
    other = pl.ds(pl.multiple_of((1 - rep) * hid, hid), hid)

    def down(k):
        return rcopy(wd_ref.at[0, mine, cols(quarters[k], 1024)], wd.at[q_me, mine], sw.at[k], rw.at[k], partners[k])

    def share(k):
        part = wd.at[quarters[k], mine]
        return rcopy(part, part, st.at[k], rt.at[k], sibling)

    first = []
    for d in range(1, 4):
        j = (zh + d) % 4
        first.append(rcopy(k_ref.at[:, cols(j, HD)], kv_vm.at[pos, zh, 0], s1.at[d - 1, 0], r1.at[d - 1, 0], at(x, j, y)))
        first.append(rcopy(v_ref.at[:, cols(j, HD)], kv_vm.at[pos, zh, 1], s1.at[d - 1, 1], r1.at[d - 1, 1], at(x, j, y)))
    for d in range(1, 4):
        j = (zh + d) % 4
        first.append(rcopy(q_ref.at[:, cols(j, 4 * HD)], q_vm.at[zh], sq.at[d - 1], rq.at[d - 1], at(x, j, y)))
    for c in first:
        c.start()
    m_ref[...] = jnp.full(m_ref.shape, -1e30, F32)
    acc_ref[...] = jnp.zeros(acc_ref.shape, F32)
    own[0].wait()
    own[1].wait()
    for d in range(1, 4):
        src = (zh + 4 - d) % 4
        for w in range(2):
            rcopy(kv_vm.at[pos, src, w], kv_vm.at[pos, src, w], s1.at[d - 1, w], r1.at[d - 1, w], at(x, src, y)).wait_recv()

    def place(ex, ey):
        return ((x + 4 - ex) % 4) * 4 + (y + 4 - ey) % 4

    def copy_of(h, ex, ey, p, dest):
        ref = kv_vm.at[p, pl.ds(2 * h, 2)]
        send, recv = (sa, ra) if h == 0 else (sb, rb)
        return rcopy(ref, ref, send.at[ex, ey], recv.at[ex, ey], dest)

    def piece_of(h, ex, ey, part, p, dest):
        ref = kv_vm.at[p, 2 * h + part]
        send, recv = (sap, rap) if h == 0 else (sbp, rbp)
        line = ey if h == 1 else ex
        return rcopy(ref, ref, send.at[line, part], recv.at[line, part], dest)

    def axis_to(h, second, step):
        return at(x + step, zh, y) if (h == 0) != second else at(x, zh, y + step)

    sends = []

    def go(make, *rest):
        make(*rest).start()
        sends.append((make, rest))

    def index(h, a, b):
        return (a, b) if h == 0 else (b, a)

    def arrived(h, a, b):
        ex, ey = index(h, a, b)
        copy_of(h, ex, ey, place(ex, ey), partners[0]).wait_recv()

    def leg_copy(h, a, b, step):
        ex, ey = index(h, a, b)
        return copy_of(h, ex, ey, place(*index(h, a, 0)), axis_to(h, True, step))

    def second_leg(h, a):
        for b, step in ((1, 1), (3, -1)):
            go(leg_copy, h, a, b, step)

    def piece_copy(h, a, b):
        part, step = (0, 1) if b == 1 else (1, -1)
        ex, ey = index(h, a, 2)
        return piece_of(h, ex, ey, part, place(*index(h, a, b)), axis_to(h, True, step))

    def relay_second(h, a, b):
        go(piece_copy, h, a, b)

    def pieces(h, a):
        ex, ey = index(h, a, 2)
        for part in range(2):
            piece_of(h, ex, ey, part, place(ex, ey), partners[0]).wait_recv()

    def first_piece(h, part, p, dest):
        ref = kv_vm.at[p, 2 * h + part]
        send, recv = (sap, rap) if h == 0 else (sbp, rbp)
        return rcopy(ref, ref, send.at[4, part], recv.at[4, part], dest)

    def start_copy(h, a, step):
        ex, ey = index(h, a, 0)
        return copy_of(h, ex, ey, pos, axis_to(h, False, step))

    def turn_copy(h, a, part, step):
        return first_piece(h, part, place(*index(h, a, 0)), axis_to(h, False, step))

    for h in range(2):
        for a, step in ((1, 1), (3, -1)):
            go(start_copy, h, a, step)
    for h in range(2):
        second_leg(h, 0)

    def absorb(p0, p1):
        k = jnp.concatenate([kv_vm[p0, :, 0].reshape(512, HD), kv_vm[p1, :, 0].reshape(512, HD)], axis=0)
        v = jnp.concatenate([kv_vm[p0, :, 1].reshape(512, HD), kv_vm[p1, :, 1].reshape(512, HD)], axis=0)
        v_one = jnp.concatenate([v, jnp.ones((1024, HD), BF16)], axis=1)
        for h in range(4):
            for r in range(2):
                rows = slice(r * 256, (r + 1) * 256)
                q = q_vm[2 * r:2 * r + 2, :, h * HD:(h + 1) * HD].reshape(256, HD)
                s = lax.dot_general(q, k, (((1,), (1,)), ((), ())), preferred_element_type=F32)
                m_old = m_ref[h, rows]
                m_new = jnp.maximum(m_old, jnp.max(s, axis=1, keepdims=True))
                m_ref[h, rows] = m_new
                alpha = jnp.exp2((m_old - m_new) * fold)
                p = jnp.exp2((s - m_new[:, :1]) * fold)
                added = jnp.dot(p.astype(BF16), v_one, preferred_element_type=F32)
                acc_ref[h, rows] = acc_ref[h, rows] * alpha[:, :1] + added

    for h in range(2):
        for a, step, part in ((1, 1, 0), (3, -1, 1)):
            arrived(h, a, 0)
            go(turn_copy, h, a, part, step)
            second_leg(h, a)
    for h in range(2):
        for b in (1, 3):
            arrived(h, 0, b)
            relay_second(h, 0, b)
    own[2].wait()
    for d in range(1, 4):
        src = (zh + 4 - d) % 4
        rcopy(q_vm.at[src], q_vm.at[src], sq.at[d - 1], rq.at[d - 1], at(x, src, y)).wait_recv()

    order = ((0, 0), (0, 1), (0, 3), (1, 0), (3, 0), (1, 1), (1, 3), (3, 1), (3, 3), (2, 0), (0, 2), (2, 1), (2, 3), (1, 2), (3, 2), (2, 2))

    def step(i, carry):
        def look(values):
            out = 0
            for n, value in enumerate(values):
                if value:
                    out = out + jnp.where(i == n, value, 0)
            return out

        @pl.when(i == 2)
        def _():
            for h in range(2):
                for part in range(2):
                    first_piece(h, part, place(*index(h, 2, 0)), partners[0]).wait_recv()
                second_leg(h, 2)
            for h in range(2):
                for a in (1, 3):
                    for b in (1, 3):
                        arrived(h, a, b)
                        relay_second(h, a, b)

        @pl.when(i == 3)
        def _():
            for h in range(2):
                for b in (1, 3):
                    arrived(h, 2, b)
                    relay_second(h, 2, b)

        @pl.when(i == 0)
        def _():
            down(1).start()

        @pl.when(i == 4)
        def _():
            down(0).start()
            pieces(1, 0)

        @pl.when(i == 5)
        def _():
            down(2).start()
            pieces(0, 0)
            pieces(1, 1)

        @pl.when(i == 6)
        def _():
            pieces(1, 3)
            pieces(0, 1)

        @pl.when(i == 7)
        def _():
            pieces(0, 3)
            pieces(0, 2)
            pieces(1, 2)

        p0 = place(look([order[2 * n][0] for n in range(8)]), look([order[2 * n][1] for n in range(8)]))
        p1 = place(look([order[2 * n + 1][0] for n in range(8)]), look([order[2 * n + 1][1] for n in range(8)]))
        absorb(p0, p1)
        return carry

    lax.fori_loop(0, 8, step, 0)
    for h in range(4):
        total = acc_ref[h]
        ao[:, :, h * HD:(h + 1) * HD] = (total[:, :HD] / total[:, HD:]).astype(BF16).reshape(4, 128, HD)

    def come_down():
        for k in range(3):
            part = wd.at[quarters[k], mine]
            rcopy(part, part, sw.at[k], rw.at[k], partners[k]).wait_recv()
            share(k).start()

    def finish():
        own[3].wait()
        for k in range(3):
            part = wd.at[quarters[k], other]
            rcopy(part, part, st.at[k], rt.at[k], sibling).wait_recv()

    def drain():
        for c in first:
            c.wait_send()
        for make, rest in sends:
            make(*rest).wait_send()
        for k in range(3):
            down(k).wait_send()
            share(k).wait_send()

    return come_down, finish, drain


CHUNKS = 8


def layer_kernel(
    q_ref, k_ref, v_ref, resid_ref, gain_ref, ids_ref, gates_ref, wg_ref, wu_ref, wd_ref, out_ref,
    q_vm, kv_vm, m_ref, acc_ref, ao,
    att, rbuf, stream_ref, ssq, ssq_in, sbuf, xall, wg, wu, wd, acts, outgoing, back,
    s1, r1, sq, rq, sa, ra, sb, rb, sap, rap, sbp, rbp, sw, rw, st, rt, lsem_a,
    sh_heads, rh_heads, ss, rs, sd, rd, sf, rf, sh, rh, sr, rr, lsem,
):
    me, x, zh, y = coords()
    sec = lax.axis_index("sec")
    j_me = me % 2
    e_me = me // 2
    side = jnp.where((y == 0) | (y == 3), 0, 1)
    low = side * 4 + (zh % 2) * 2 + y // 2
    own_slot = (me // 8) * 8 + low
    partners, quarters, q_me = square(me, sec)
    half = pl.ds(pl.multiple_of(sec * 2048, 2048), 2048)
    fetch = pltpu.make_async_copy(resid_ref.at[:, half], rbuf, lsem.at[0])
    fetch.start()
    weights = [
        pltpu.make_async_copy(wg_ref.at[0], wg, lsem.at[3]),
        pltpu.make_async_copy(wu_ref.at[0], wu, lsem.at[4]),
    ]
    for c in weights:
        c.start()
    come_down, finish_down, drain_attention = attend(
        q_ref, k_ref, v_ref, wd_ref, ao, wd, q_vm, kv_vm, m_ref, acc_ref,
        s1, r1, sq, rq, sa, ra, sb, rb, sap, rap, sbp, rbp, sw, rw, st, rt, lsem_a,
    )
    keep = pltpu.make_async_copy(ao.at[zh], att.at[zh], lsem.at[1])
    keep.start()
    heads = []
    for d in range(1, 4):
        j = (zh + d) % 4
        heads.append(rcopy(ao.at[j], att.at[zh], sh_heads.at[d - 1], rh_heads.at[d - 1], {"dev": x * 16 + j * 4 + y}))
    for c in heads:
        c.start()

    r8, first, slot = one_hot(ids_ref)
    pick = jnp.where(slot == r8, 1.0, 0.0).astype(BF16)
    fold = [jnp.where((slot == 8 + r8 // 4) & (r8 % 4 == p), 1.0, 0.0).astype(BF16) for p in range(4)]

    fetch.wait()
    keep.wait()
    for d in range(1, 4):
        src = (zh + 4 - d) % 4
        rcopy(ao.at[src], att.at[src], sh_heads.at[d - 1], rh_heads.at[d - 1], {"dev": x * 16 + src * 4 + y}).wait_recv()
    total = jnp.zeros((128, 1), F32)
    for g in range(4):
        part = rbuf[:, g * 512:(g + 1) * 512].astype(F32) + att[g].astype(F32)
        stream_ref[:, g * 512:(g + 1) * 512] = part
        total = total + jnp.sum(part * part, axis=1, keepdims=True)
    ssq[...] = jnp.broadcast_to(total, (128, 128))
    cross = rcopy(ssq, ssq_in, ss, rs, {"sec": 1 - sec})
    cross.start()
    cross.wait()
    scale = lax.rsqrt((ssq[:, :1] + ssq_in[:, :1]) * (1.0 / 4096) + 1e-06)
    for j in range(2):
        normed = []
        for p in range(4):
            at = j * 1024 + p * 256
            g = gain_ref[:, pl.ds(pl.multiple_of(sec * 2048 + at, 256), 256)]
            normed.append((stream_ref[:, at:at + 256] * scale * g).astype(BF16))
        extra = jnp.zeros((256, 256), F32)
        for p in range(4):
            main = jnp.dot(pick, normed[p], preferred_element_type=F32)
            sbuf[j, :, :, p * 256:(p + 1) * 256] = main.reshape(32, 8, 256).astype(BF16)
            extra = extra + jnp.dot(fold[p], normed[p], preferred_element_type=F32)
        sbuf[j, :, :, 1024:1280] = extra.reshape(32, 8, 256).astype(BF16)

    def ahead(c):
        return ((x + c // 2) % 4) * 16 + ((zh // 2 + c) % 2) * 8

    def behind(c):
        return ((x + 4 - c // 2) % 4) * 16 + ((zh // 2 + c) % 2) * 8

    def slot_device(slot):
        s, zl, w = (slot // 4) % 2, (slot // 2) % 2, slot % 2
        return (slot // 8) * 8 + zl * 4 + s + w * (3 - 2 * s)

    both = pl.ds(2 * sec, 2)
    far = pl.ds(2 * (1 - sec), 2)

    def rows_to(t, c):
        base = ahead(c)
        turn = (zh + t // 2) % 2
        pair = (y // 2 + t) % 2
        entry = jnp.where(pair == y // 2, y, 3 - y)
        return rcopy(
            sbuf.at[:, base // 2 + turn * 2 + pair], xall.at[both, own_slot], sd.at[c], rd.at[c], {"dev": base + turn * 4 + entry}
        )

    def send_rows(c, start):
        for t in range(start, 4):
            rows_to(t, c).start()

    def near(c):
        return pl.ds(behind(c) + side * 4, 4)

    def off_side(c):
        return pl.ds(behind(c) + (1 - side) * 4, 4)

    def counted(n, send_sem, recv_sem):
        ref = outgoing.at[pl.ds(0, n)]
        return rcopy(ref, ref, send_sem, recv_sem, partners[0])

    def pass_on(k, c):
        ref = xall.at[far if k == 2 else both, near(c)]
        return rcopy(ref, ref, sf.at[k, c], rf.at[k, c], partners[1 if k == 1 else 0])

    def came(k, c):
        ref = xall.at[both if k == 0 else far, near(c) if k == 1 else off_side(c)]
        return rcopy(ref, ref, sf.at[k, c], rf.at[k, c], partners[0])

    def act_to(k, c):
        ref = acts.at[quarters[1] if k == 2 else q_me, c]
        return rcopy(ref, ref, sh.at[k, c], rh.at[k, c], partners[1 if k == 1 else 0])

    def act_from(k, c):
        ref = acts.at[quarters[k], c]
        return rcopy(ref, ref, sh.at[k, c], rh.at[k, c], partners[k])

    def result_to(dest, c):
        return rcopy(outgoing.at[dest], back.at[j_me, e_me], sr.at[c], rr.at[c], {"dev": slot_device(dest)})

    own_rows = pltpu.make_async_copy(sbuf.at[:, e_me], xall.at[both, own_slot], lsem.at[2])
    own_rows.start()
    own_back = pltpu.make_async_copy(outgoing.at[own_slot], back.at[j_me, e_me], lsem.at[5])
    send_rows(0, 1)
    send_rows(1, 0)
    send_rows(2, 0)
    own_rows.wait()
    for c in weights:
        c.wait()
    come_down()

    def relay(c):
        @pl.when(c == 0)
        def _():
            ref = xall.at[both, pl.ds(0, 3)]
            rcopy(ref, ref, sd.at[0], rd.at[0], partners[0]).wait_recv()

        @pl.when(c > 0)
        def _():
            ref = xall.at[both, near(c)]
            rcopy(ref, ref, sd.at[c], rd.at[c], partners[0]).wait_recv()

        pass_on(1, c).start()
        pass_on(0, c).start()

        @pl.when(c == 0)
        def _():
            counted(6, sd.at[0], rd.at[0]).wait_send()
            send_rows(3, 0)

        @pl.when((c > 0) & (c + 3 < CHUNKS))
        def _():
            counted(8, sd.at[c], rd.at[c]).wait_send()
            send_rows(c + 3, 0)

    def relay_far(c):
        came(1, c).wait_recv()
        pass_on(2, c).start()

    def hidden(c):
        came(0, c).wait_recv()
        came(2, c).wait_recv()
        rows = []
        for q in range(4):
            data = xall[q, pl.ds(behind(c), 8)].astype(F32).reshape(64, 1280).astype(BF16)
            over = jnp.concatenate([unfold(data[:, 1024:], p) for p in range(4)], axis=1)
            rows.append(jnp.concatenate([data[:, :1024], over], axis=0))
        rows = jnp.concatenate(rows, axis=1)
        g = jnp.dot(rows, wg[...], preferred_element_type=F32)
        u = jnp.dot(rows, wu[...], preferred_element_type=F32)
        acts[q_me, c] = (g / (1.0 + jnp.exp(-g)) * u).astype(BF16)
        act_to(1, c).start()
        act_to(0, c).start()

    def act_on(c):
        act_from(1, c).wait_recv()
        act_to(2, c).start()

    def output(c):
        @pl.when(c == 0)
        def _():
            finish_down()

        act_from(0, c).wait_recv()
        act_from(2, c).wait_recv()
        part = jnp.dot(acts[0, c], wd[0], preferred_element_type=F32)
        for q in range(1, 4):
            part = part + jnp.dot(acts[q, c], wd[q], preferred_element_type=F32)
        outgoing[pl.ds(behind(c), 8), :, 0:1024] = part[:64].reshape(8, 8, 1024).astype(BF16)
        over = part[64:].astype(BF16)
        extra = refold(over[:, 0:256], 0)
        for p in range(1, 4):
            extra = extra + refold(over[:, p * 256:(p + 1) * 256], p)
        outgoing[pl.ds(behind(c), 8), :, 1024:1280] = extra.reshape(8, 8, 256).astype(BF16)

        @pl.when(c == 0)
        def _():
            own_back.start()

        def one(t, carry):
            result_to(behind(c) + (low + t) % 8, c).start()
            return carry

        lax.fori_loop(jnp.where(c == 0, 1, 0), 8, one, 0)

    def stage(c, carry):
        @pl.when(c < CHUNKS)
        def _():
            relay(c)

        @pl.when((c >= 1) & (c < CHUNKS + 1))
        def _():
            relay_far(c - 1)

        @pl.when(c >= 3)
        def _():
            act_on(c - 3)

        @pl.when((c >= 2) & (c < CHUNKS + 2))
        def _():
            hidden(c - 2)

        @pl.when(c >= 3)
        def _():
            output(c - 3)

        return carry

    lax.fori_loop(0, CHUNKS + 3, stage, 0)
    own_back.wait()
    counted(7, sr.at[0], rr.at[0]).wait_send()
    ref = back.at[0, pl.ds(0, 7)]
    rcopy(ref, ref, sr.at[0], rr.at[0], partners[0]).wait_recv()

    def arrive(c, carry):
        ref = back.at[:, pl.ds(ahead(c) // 2, 4)]
        rcopy(ref, ref, sr.at[c], rr.at[c], partners[0]).wait_recv()
        counted(8, sr.at[c], rr.at[c]).wait_send()
        return carry

    lax.fori_loop(1, CHUNKS, arrive, 0)

    r8, first, slot = one_hot(ids_ref)
    weight = jnp.where(first, gates_ref[0:1, :], gates_ref[1:2, :])

    def split(mask):
        w = jnp.where(mask, weight, 0.0).T
        high = w.astype(BF16)
        return high, (w - high.astype(F32)).astype(BF16)

    def weigh(pair, data):
        return jnp.dot(pair[0], data, preferred_element_type=F32) + jnp.dot(pair[1], data, preferred_element_type=F32)

    main_pick = split(slot == r8)
    fold_pick = [split((slot == 8 + r8 // 4) & (r8 % 4 == p)) for p in range(4)]
    for j in range(2):
        extra = back[j, :, :, 1024:1280].astype(F32).reshape(256, 256).astype(BF16)
        for p in range(4):
            at = j * 1024 + p * 256
            data = back[j, :, :, p * 256:(p + 1) * 256].astype(F32).reshape(256, 256).astype(BF16)
            moe = weigh(main_pick, data) + weigh(fold_pick[p], extra)
            out_ref[:, at:at + 256] = (stream_ref[:, at:at + 256] + moe).astype(BF16)

    drain_attention()
    for c in heads:
        c.wait_send()
    for c in range(CHUNKS - 3, CHUNKS):
        counted(8, sd.at[c], rd.at[c]).wait_send()

    def drain(c, carry):
        for k in range(3):
            pass_on(k, c).wait_send()
            act_to(k, c).wait_send()
        return carry

    lax.fori_loop(0, CHUNKS, drain, 0)


def unfold(extra, p):
    want = 4 * lax.broadcasted_iota(jnp.int32, (16, 64), 0) + p == lax.broadcasted_iota(jnp.int32, (16, 64), 1)
    return jnp.dot(jnp.where(want, 1.0, 0.0).astype(BF16), extra, preferred_element_type=F32).astype(BF16)


def refold(rows, p):
    want = 4 * lax.broadcasted_iota(jnp.int32, (64, 16), 1) + p == lax.broadcasted_iota(jnp.int32, (64, 16), 0)
    return jnp.dot(jnp.where(want, 1.0, 0.0).astype(BF16), rows, preferred_element_type=F32)


def body(resid, queries, keys, values, norm_gain, expert_ids, gate_weights, w_gate, w_up, w_down):
    dma = pltpu.SemaphoreType.DMA
    hidden = w_gate.shape[2]
    return pl.pallas_call(
        layer_kernel,
        out_shape=jax.ShapeDtypeStruct((128, 2048), BF16),
        in_specs=[ANY, ANY, ANY, ANY, VMEM, VMEM, VMEM, ANY, ANY, ANY],
        out_specs=VMEM,
        scratch_shapes=[
            pltpu.VMEM((4, 128, 4 * HD), BF16),
            pltpu.VMEM((16, 4, 2, 128, HD), BF16),
            pltpu.VMEM((4, 512, HD), F32),
            pltpu.VMEM((4, 512, 2 * HD), F32),
            pltpu.VMEM((4, 128, 512), BF16),
            pltpu.VMEM((4, 128, 512), BF16),
            pltpu.VMEM((128, 2048), BF16),
            pltpu.VMEM((128, 2048), F32),
            pltpu.VMEM((128, 128), F32),
            pltpu.VMEM((128, 128), F32),
            pltpu.VMEM((2, 32, 8, 1280), BF16),
            pltpu.VMEM((4, 64, 8, 1280), BF16),
            pltpu.VMEM((4096, hidden), BF16),
            pltpu.VMEM((4096, hidden), BF16),
            pltpu.VMEM((4, hidden, 1024), BF16),
            pltpu.VMEM((4, CHUNKS, 640 // CHUNKS, hidden), BF16),
            pltpu.VMEM((64, 8, 1280), BF16),
            pltpu.VMEM((2, 32, 8, 1280), BF16),
            dma((3, 2)), dma((3, 2)), dma((3,)), dma((3,)),
            dma((4, 4)), dma((4, 4)), dma((4, 4)), dma((4, 4)),
            dma((5, 2)), dma((5, 2)), dma((5, 2)), dma((5, 2)),
            dma((3,)), dma((3,)), dma((3,)), dma((3,)), dma((4,)),
            dma((3,)), dma((3,)), dma, dma, dma((CHUNKS,)), dma((CHUNKS,)),
            dma((3, CHUNKS)), dma((3, CHUNKS)),
            dma((3, CHUNKS)), dma((3, CHUNKS)), dma((CHUNKS,)), dma((CHUNKS,)), dma((6,)),
        ],
        compiler_params=pltpu.CompilerParams(
            collective_id=0, has_side_effects=True, vmem_limit_bytes=VMEM_BYTES
        ),
    )(
        queries, keys, values, resid, norm_gain.reshape(1, -1), expert_ids.T, gate_weights.T, w_gate, w_up, w_down
    )


def solution(mesh):
    in_specs = (
        P(("rep", "dev"), None),
        P(("rep", "dev"), "sec"),
        P(("rep", "dev"), "sec"),
        P(("rep", "dev"), "sec"),
        P(),
        P(("rep", "dev"), None),
        P(("rep", "dev"), None),
        P("dev", None, "sec"),
        P("dev", None, "sec"),
        P("dev", "sec", None),
    )
    out_specs = P(("rep", "dev"), "sec")
    return jax.shard_map(body, mesh=mesh, in_specs=in_specs, out_specs=out_specs, check_vma=False)
```

```python
import math

import jax
import jax.numpy as jnp
from jax import lax
from jax.experimental import pallas as pl
from jax.experimental.pallas import tpu as pltpu
from jax.sharding import PartitionSpec as P

HD = 128
MESH = pl.DeviceIdType.MESH
F32 = jnp.float32
BF16 = jnp.bfloat16
VMEM_BYTES = 58 * 1024 * 1024
ANY = pl.BlockSpec(memory_space=pl.ANY)
VMEM = pl.BlockSpec(memory_space=pltpu.VMEM)


def rcopy(src, dst, send_sem, recv_sem, device_id):
    return pltpu.make_async_remote_copy(
        src_ref=src,
        dst_ref=dst,
        send_sem=send_sem,
        recv_sem=recv_sem,
        device_id=device_id,
        device_id_type=MESH,
    )


def coords():
    me = lax.axis_index("dev")
    return me, me // 16, (me // 4) % 4, me % 4


def twin(me):
    return me + 1 - 2 * (me % 2)


def square(me, sec):
    j = me % 2
    partners = ({"dev": twin(me)}, {"sec": 1 - sec}, {"dev": twin(me), "sec": 1 - sec})
    quarters = (2 * sec + 1 - j, 2 * (1 - sec) + j, 2 * (1 - sec) + 1 - j)
    return partners, quarters, 2 * sec + j


def greet(me, sec, rep):
    barrier = pltpu.get_barrier_semaphore()

    def one(i, carry):
        pl.semaphore_signal(barrier, inc=1, device_id={"dev": (me + i) % 64}, device_id_type=MESH)
        return carry

    lax.fori_loop(1, 64, one, 0)
    for peer in ({"sec": 1 - sec}, {"sec": 1 - sec, "dev": twin(me)}, {"rep": 1 - rep}):
        pl.semaphore_signal(barrier, inc=1, device_id=peer, device_id_type=MESH)
    pl.semaphore_wait(barrier, 66)


def one_hot(ids_ref):
    row = lax.broadcasted_iota(jnp.int32, (256, 128), 0)
    expert = row // 8
    first = expert == ids_ref[0:1, :]
    second = expert == ids_ref[1:2, :]
    named = jnp.where(first | second, 1.0, 0.0)
    before = lax.broadcasted_iota(jnp.int32, (128, 128), 0) < lax.broadcasted_iota(jnp.int32, (128, 128), 1)
    slot = jnp.dot(named.astype(BF16), jnp.where(before, 1.0, 0.0).astype(BF16), preferred_element_type=F32)
    slot = jnp.where(named > 0.5, slot, -1.0).astype(jnp.int32)
    return row % 8, first, slot


def attend(
    q_ref, k_ref, v_ref, wd_ref, ao, wd, q_vm, kv_vm, m_ref, acc_ref,
    s1, r1, sq, rq, sa, ra, sb, rb, sap, rap, sbp, rbp, sw, rw, st, rt, lsem,
):
    me, x, zh, y = coords()
    pos = x * 4 + y
    sec = lax.axis_index("sec")
    rep = lax.axis_index("rep")
    partners, quarters, q_me = square(me, sec)
    sibling = {"rep": 1 - rep}
    fold = math.log2(math.e) / math.sqrt(HD)

    def at(xx, zz, yy):
        return {"dev": ((xx + 4) % 4) * 16 + zz * 4 + (yy + 4) % 4}

    def cols(j, w):
        return pl.ds(pl.multiple_of(j * w, w), w)

    own = [
        pltpu.make_async_copy(k_ref.at[:, cols(zh, HD)], kv_vm.at[pos, zh, 0], lsem.at[0]),
        pltpu.make_async_copy(v_ref.at[:, cols(zh, HD)], kv_vm.at[pos, zh, 1], lsem.at[1]),
        pltpu.make_async_copy(q_ref.at[:, cols(zh, 4 * HD)], q_vm.at[zh], lsem.at[2]),
        pltpu.make_async_copy(wd_ref.at[0, :, cols(q_me, 1024)], wd.at[q_me], lsem.at[3]),
    ]
    for c in own:
        c.start()
    greet(me, sec, rep)

    hid = wd_ref.shape[1] // 2
    mine = pl.ds(pl.multiple_of(rep * hid, hid), hid)
    other = pl.ds(pl.multiple_of((1 - rep) * hid, hid), hid)

    def down(k):
        return rcopy(wd_ref.at[0, mine, cols(quarters[k], 1024)], wd.at[q_me, mine], sw.at[k], rw.at[k], partners[k])

    def share(k):
        part = wd.at[quarters[k], mine]
        return rcopy(part, part, st.at[k], rt.at[k], sibling)

    first = []
    for d in range(1, 4):
        j = (zh + d) % 4
        first.append(rcopy(k_ref.at[:, cols(j, HD)], kv_vm.at[pos, zh, 0], s1.at[d - 1, 0], r1.at[d - 1, 0], at(x, j, y)))
        first.append(rcopy(v_ref.at[:, cols(j, HD)], kv_vm.at[pos, zh, 1], s1.at[d - 1, 1], r1.at[d - 1, 1], at(x, j, y)))
    for c in first:
        c.start()
    m_ref[...] = jnp.full(m_ref.shape, -1e30, F32)
    acc_ref[...] = jnp.zeros(acc_ref.shape, F32)
    own[0].wait()
    own[1].wait()
    for d in range(1, 4):
        src = (zh + 4 - d) % 4
        for w in range(2):
            rcopy(kv_vm.at[pos, src, w], kv_vm.at[pos, src, w], s1.at[d - 1, w], r1.at[d - 1, w], at(x, src, y)).wait_recv()
    for d in range(1, 4):
        j = (zh + d) % 4
        turn = rcopy(q_ref.at[:, cols(j, 4 * HD)], q_vm.at[zh], sq.at[d - 1], rq.at[d - 1], at(x, j, y))
        turn.start()
        first.append(turn)

    def place(ex, ey):
        return ((x + 4 - ex) % 4) * 4 + (y + 4 - ey) % 4

    def copy_of(h, ex, ey, p, dest):
        ref = kv_vm.at[p, pl.ds(2 * h, 2)]
        send, recv = (sa, ra) if h == 0 else (sb, rb)
        return rcopy(ref, ref, send.at[ex, ey], recv.at[ex, ey], dest)

    def piece_of(h, ex, ey, part, p, dest):
        ref = kv_vm.at[p, 2 * h + part]
        send, recv = (sap, rap) if h == 0 else (sbp, rbp)
        line = ey if h == 1 else ex
        return rcopy(ref, ref, send.at[line, part], recv.at[line, part], dest)

    def axis_to(h, second, step):
        return at(x + step, zh, y) if (h == 0) != second else at(x, zh, y + step)

    sends = []

    def go(make, *rest):
        make(*rest).start()
        sends.append((make, rest))

    def index(h, a, b):
        return (a, b) if h == 0 else (b, a)

    def arrived(h, a, b):
        ex, ey = index(h, a, b)
        copy_of(h, ex, ey, place(ex, ey), partners[0]).wait_recv()

    def leg_copy(h, a, b, step):
        ex, ey = index(h, a, b)
        return copy_of(h, ex, ey, place(*index(h, a, 0)), axis_to(h, True, step))

    def second_leg(h, a):
        for b, step in ((1, 1), (3, -1)):
            go(leg_copy, h, a, b, step)

    def piece_copy(h, a, b):
        part, step = (0, 1) if b == 1 else (1, -1)
        ex, ey = index(h, a, 2)
        return piece_of(h, ex, ey, part, place(*index(h, a, b)), axis_to(h, True, step))

    def relay_second(h, a, b):
        go(piece_copy, h, a, b)

    def pieces(h, a):
        ex, ey = index(h, a, 2)
        for part in range(2):
            piece_of(h, ex, ey, part, place(ex, ey), partners[0]).wait_recv()

    def first_piece(h, part, p, dest):
        ref = kv_vm.at[p, 2 * h + part]
        send, recv = (sap, rap) if h == 0 else (sbp, rbp)
        return rcopy(ref, ref, send.at[4, part], recv.at[4, part], dest)

    def start_copy(h, a, step):
        ex, ey = index(h, a, 0)
        return copy_of(h, ex, ey, pos, axis_to(h, False, step))

    def turn_copy(h, a, part, step):
        return first_piece(h, part, place(*index(h, a, 0)), axis_to(h, False, step))

    for h in range(2):
        for a, step in ((1, 1), (3, -1)):
            go(start_copy, h, a, step)
    for h in range(2):
        second_leg(h, 0)

    def absorb(p0, p1):
        k = jnp.concatenate([kv_vm[p0, :, 0].reshape(512, HD), kv_vm[p1, :, 0].reshape(512, HD)], axis=0)
        v = jnp.concatenate([kv_vm[p0, :, 1].reshape(512, HD), kv_vm[p1, :, 1].reshape(512, HD)], axis=0)
        v_one = jnp.concatenate([v, jnp.ones((1024, HD), BF16)], axis=1)
        for h in range(4):
            for r in range(2):
                rows = slice(r * 256, (r + 1) * 256)
                q = q_vm[2 * r:2 * r + 2, :, h * HD:(h + 1) * HD].reshape(256, HD)
                s = lax.dot_general(q, k, (((1,), (1,)), ((), ())), preferred_element_type=F32)
                m_old = m_ref[h, rows]
                m_new = jnp.maximum(m_old, jnp.max(s, axis=1, keepdims=True))
                m_ref[h, rows] = m_new
                alpha = jnp.exp2((m_old - m_new) * fold)
                p = jnp.exp2((s - m_new[:, :1]) * fold)
                added = jnp.dot(p.astype(BF16), v_one, preferred_element_type=F32)
                acc_ref[h, rows] = acc_ref[h, rows] * alpha[:, :1] + added

    for h in range(2):
        for a, step, part in ((1, 1, 0), (3, -1, 1)):
            arrived(h, a, 0)
            go(turn_copy, h, a, part, step)
            second_leg(h, a)
    for h in range(2):
        for b in (1, 3):
            arrived(h, 0, b)
            relay_second(h, 0, b)
    own[2].wait()
    for d in range(1, 4):
        src = (zh + 4 - d) % 4
        rcopy(q_vm.at[src], q_vm.at[src], sq.at[d - 1], rq.at[d - 1], at(x, src, y)).wait_recv()

    order = ((0, 0), (0, 1), (0, 3), (1, 0), (3, 0), (1, 1), (1, 3), (3, 1), (3, 3), (2, 0), (0, 2), (2, 1), (2, 3), (1, 2), (3, 2), (2, 2))

    def step(i, carry):
        def look(values):
            out = 0
            for n, value in enumerate(values):
                if value:
                    out = out + jnp.where(i == n, value, 0)
            return out

        @pl.when(i == 1)
        def _():
            for h in range(2):
                for part in range(2):
                    first_piece(h, part, place(*index(h, 2, 0)), partners[0]).wait_recv()
                second_leg(h, 2)
            for h in range(2):
                for a in (1, 3):
                    for b in (1, 3):
                        arrived(h, a, b)
                        relay_second(h, a, b)

        @pl.when(i == 2)
        def _():
            for h in range(2):
                for b in (1, 3):
                    arrived(h, 2, b)
                    relay_second(h, 2, b)

        @pl.when(i == 1)
        def _():
            down(1).start()

        @pl.when(i == 3)
        def _():
            down(0).start()

        @pl.when(i == 4)
        def _():
            down(2).start()
            pieces(1, 0)

        @pl.when(i == 5)
        def _():
            pieces(0, 0)
            pieces(1, 1)

        @pl.when(i == 6)
        def _():
            pieces(1, 3)
            pieces(0, 1)

        @pl.when(i == 7)
        def _():
            pieces(0, 3)
            pieces(0, 2)
            pieces(1, 2)

        p0 = place(look([order[2 * n][0] for n in range(8)]), look([order[2 * n][1] for n in range(8)]))
        p1 = place(look([order[2 * n + 1][0] for n in range(8)]), look([order[2 * n + 1][1] for n in range(8)]))
        absorb(p0, p1)
        return carry

    lax.fori_loop(0, 8, step, 0)
    for h in range(4):
        total = acc_ref[h]
        ao[:, :, h * HD:(h + 1) * HD] = (total[:, :HD] / total[:, HD:]).astype(BF16).reshape(4, 128, HD)

    def come_down():
        for k in range(3):
            part = wd.at[quarters[k], mine]
            rcopy(part, part, sw.at[k], rw.at[k], partners[k]).wait_recv()
            share(k).start()

    def finish():
        own[3].wait()
        for k in range(3):
            part = wd.at[quarters[k], other]
            rcopy(part, part, st.at[k], rt.at[k], sibling).wait_recv()

    def drain():
        for c in first:
            c.wait_send()
        for make, rest in sends:
            make(*rest).wait_send()
        for k in range(3):
            down(k).wait_send()
            share(k).wait_send()

    return come_down, finish, drain


CHUNKS = 8


def layer_kernel(
    q_ref, k_ref, v_ref, resid_ref, gain_ref, ids_ref, gates_ref, wg_ref, wu_ref, wd_ref, out_ref,
    q_vm, kv_vm, m_ref, acc_ref, ao,
    att, rbuf, stream_ref, ssq, ssq_in, sbuf, xall, wg, wu, wd, acts, outgoing, back,
    s1, r1, sq, rq, sa, ra, sb, rb, sap, rap, sbp, rbp, sw, rw, st, rt, lsem_a,
    sh_heads, rh_heads, ss, rs, sd, rd, sf, rf, sf2, rf2, sh, rh, sr, rr, lsem,
):
    me, x, zh, y = coords()
    sec = lax.axis_index("sec")
    j_me = me % 2
    e_me = me // 2
    low = me % 8
    partners, quarters, q_me = square(me, sec)
    half = pl.ds(pl.multiple_of(sec * 2048, 2048), 2048)
    fetch = pltpu.make_async_copy(resid_ref.at[:, half], rbuf, lsem.at[0])
    fetch.start()
    weights = [
        pltpu.make_async_copy(wg_ref.at[0], wg, lsem.at[3]),
        pltpu.make_async_copy(wu_ref.at[0], wu, lsem.at[4]),
    ]
    for c in weights:
        c.start()
    come_down, finish_down, drain_attention = attend(
        q_ref, k_ref, v_ref, wd_ref, ao, wd, q_vm, kv_vm, m_ref, acc_ref,
        s1, r1, sq, rq, sa, ra, sb, rb, sap, rap, sbp, rbp, sw, rw, st, rt, lsem_a,
    )
    keep = pltpu.make_async_copy(ao.at[zh], att.at[zh], lsem.at[1])
    keep.start()
    heads = []
    for d in range(1, 4):
        j = (zh + d) % 4
        heads.append(rcopy(ao.at[j], att.at[zh], sh_heads.at[d - 1], rh_heads.at[d - 1], {"dev": x * 16 + j * 4 + y}))
    for c in heads:
        c.start()

    r8, first, slot = one_hot(ids_ref)
    pick = jnp.where(slot == r8, 1.0, 0.0).astype(BF16)
    fold = [jnp.where((slot == 8 + r8 // 4) & (r8 % 4 == p), 1.0, 0.0).astype(BF16) for p in range(4)]

    fetch.wait()
    keep.wait()
    for d in range(1, 4):
        src = (zh + 4 - d) % 4
        rcopy(ao.at[src], att.at[src], sh_heads.at[d - 1], rh_heads.at[d - 1], {"dev": x * 16 + src * 4 + y}).wait_recv()
    total = jnp.zeros((128, 1), F32)
    for g in range(4):
        part = rbuf[:, g * 512:(g + 1) * 512].astype(F32) + att[g].astype(F32)
        stream_ref[:, g * 512:(g + 1) * 512] = part
        total = total + jnp.sum(part * part, axis=1, keepdims=True)
    ssq[...] = jnp.broadcast_to(total, (128, 128))
    cross = rcopy(ssq, ssq_in, ss, rs, {"sec": 1 - sec})
    cross.start()
    cross.wait()
    scale = lax.rsqrt((ssq[:, :1] + ssq_in[:, :1]) * (1.0 / 4096) + 1e-06)
    for j in range(2):
        normed = []
        for p in range(4):
            at = j * 1024 + p * 256
            g = gain_ref[:, pl.ds(pl.multiple_of(sec * 2048 + at, 256), 256)]
            normed.append((stream_ref[:, at:at + 256] * scale * g).astype(BF16))
        extra = jnp.zeros((256, 256), F32)
        for p in range(4):
            main = jnp.dot(pick, normed[p], preferred_element_type=F32)
            sbuf[j, :, :, p * 256:(p + 1) * 256] = main.reshape(32, 8, 256).astype(BF16)
            extra = extra + jnp.dot(fold[p], normed[p], preferred_element_type=F32)
        sbuf[j, :, :, 1024:1280] = extra.reshape(32, 8, 256).astype(BF16)

    def ahead(c):
        return ((x + c // 2) % 4) * 16 + ((zh // 2 + c) % 2) * 8

    def behind(c):
        return ((x + 4 - c // 2) % 4) * 16 + ((zh // 2 + c) % 2) * 8

    def rows_to(dest, c):
        j, e = dest % 2, dest // 2
        return rcopy(sbuf.at[j, e], xall.at[2 * sec + j, me], sd.at[c], rd.at[c], {"dev": dest})

    def send_rows(c, start):
        def one(t, carry):
            rows_to(ahead(c) + (low + t) % 8, c).start()
            return carry

        lax.fori_loop(start, 8, one, 0)

    def block(q, c):
        return xall.at[q, pl.ds(behind(c), 8)]

    def counted(n, send_sem, recv_sem):
        ref = outgoing.at[pl.ds(0, n)]
        return rcopy(ref, ref, send_sem, recv_sem, partners[0])

    def pass_on(k, c):
        return rcopy(block(q_me, c), block(q_me, c), sf.at[k, c], rf.at[k, c], partners[k])

    def came(k, c):
        return rcopy(block(quarters[k], c), block(quarters[k], c), sf.at[k, c], rf.at[k, c], partners[0])

    def second_rows(c, k):
        return pl.ds(behind(c), 5) if k == 0 else pl.ds(behind(c) + 5, 3)

    def second_hop(k, c):
        ref = xall.at[quarters[1 - k], second_rows(c, k)]
        return rcopy(ref, ref, sf2.at[k, c], rf2.at[k, c], partners[k])

    def came_far(k, c):
        ref = xall.at[quarters[2], second_rows(c, k)]
        return rcopy(ref, ref, sf2.at[k, c], rf2.at[k, c], partners[0])

    def act_to(k, c):
        ref = acts.at[quarters[1] if k == 2 else q_me, c]
        return rcopy(ref, ref, sh.at[k, c], rh.at[k, c], partners[1 if k == 1 else 0])

    def act_from(k, c):
        ref = acts.at[quarters[k], c]
        return rcopy(ref, ref, sh.at[k, c], rh.at[k, c], partners[k])

    def result_to(dest, c):
        return rcopy(outgoing.at[dest], back.at[j_me, e_me], sr.at[c], rr.at[c], {"dev": dest})

    own_rows = pltpu.make_async_copy(sbuf.at[j_me, e_me], xall.at[q_me, me], lsem.at[2])
    own_rows.start()
    own_back = pltpu.make_async_copy(outgoing.at[me], back.at[j_me, e_me], lsem.at[5])
    send_rows(0, 1)
    send_rows(1, 0)
    send_rows(2, 0)
    own_rows.wait()
    for c in weights:
        c.wait()
    come_down()

    def relay(c):
        @pl.when(c == 0)
        def _():
            ref = xall.at[q_me, pl.ds(behind(0), 7)]
            rcopy(ref, ref, sd.at[0], rd.at[0], partners[0]).wait_recv()

        @pl.when(c > 0)
        def _():
            rcopy(block(q_me, c), block(q_me, c), sd.at[c], rd.at[c], partners[0]).wait_recv()

        pass_on(1, c).start()
        pass_on(0, c).start()

        @pl.when(c == 0)
        def _():
            counted(7, sd.at[0], rd.at[0]).wait_send()
            send_rows(3, 0)

        @pl.when((c > 0) & (c + 3 < CHUNKS))
        def _():
            counted(8, sd.at[c], rd.at[c]).wait_send()
            send_rows(c + 3, 0)

    def relay_far(c):
        came(1, c).wait_recv()
        second_hop(0, c).start()
        came(0, c).wait_recv()
        second_hop(1, c).start()

    def hidden(c):
        came_far(0, c).wait_recv()
        came_far(1, c).wait_recv()
        rows = []
        for q in range(4):
            data = xall[q, pl.ds(behind(c), 8)].astype(F32).reshape(64, 1280).astype(BF16)
            over = jnp.concatenate([unfold(data[:, 1024:], p) for p in range(4)], axis=1)
            rows.append(jnp.concatenate([data[:, :1024], over], axis=0))
        rows = jnp.concatenate(rows, axis=1)
        g = jnp.dot(rows, wg[...], preferred_element_type=F32)
        u = jnp.dot(rows, wu[...], preferred_element_type=F32)
        acts[q_me, c] = (g / (1.0 + jnp.exp(-g)) * u).astype(BF16)
        act_to(1, c).start()
        act_to(0, c).start()

    def act_on(c):
        act_from(1, c).wait_recv()
        act_to(2, c).start()

    def output(c):
        @pl.when(c == 0)
        def _():
            finish_down()

        act_from(0, c).wait_recv()
        act_from(2, c).wait_recv()
        part = jnp.dot(acts[0, c], wd[0], preferred_element_type=F32)
        for q in range(1, 4):
            part = part + jnp.dot(acts[q, c], wd[q], preferred_element_type=F32)
        outgoing[pl.ds(behind(c), 8), :, 0:1024] = part[:64].reshape(8, 8, 1024).astype(BF16)
        over = part[64:].astype(BF16)
        extra = refold(over[:, 0:256], 0)
        for p in range(1, 4):
            extra = extra + refold(over[:, p * 256:(p + 1) * 256], p)
        outgoing[pl.ds(behind(c), 8), :, 1024:1280] = extra.reshape(8, 8, 256).astype(BF16)

        @pl.when(c == 0)
        def _():
            own_back.start()

        def one(t, carry):
            result_to(behind(c) + (low + t) % 8, c).start()
            return carry

        lax.fori_loop(jnp.where(c == 0, 1, 0), 8, one, 0)

    def stage(c, carry):
        @pl.when(c < CHUNKS)
        def _():
            relay(c)

        @pl.when((c >= 1) & (c < CHUNKS + 1))
        def _():
            relay_far(c - 1)

        @pl.when(c >= 3)
        def _():
            act_on(c - 3)

        @pl.when((c >= 2) & (c < CHUNKS + 2))
        def _():
            hidden(c - 2)

        @pl.when(c >= 3)
        def _():
            output(c - 3)

        return carry

    lax.fori_loop(0, CHUNKS + 3, stage, 0)
    own_back.wait()
    counted(7, sr.at[0], rr.at[0]).wait_send()
    ref = back.at[0, pl.ds(0, 7)]
    rcopy(ref, ref, sr.at[0], rr.at[0], partners[0]).wait_recv()

    def arrive(c, carry):
        ref = back.at[:, pl.ds(ahead(c) // 2, 4)]
        rcopy(ref, ref, sr.at[c], rr.at[c], partners[0]).wait_recv()
        counted(8, sr.at[c], rr.at[c]).wait_send()
        return carry

    lax.fori_loop(1, CHUNKS, arrive, 0)

    r8, first, slot = one_hot(ids_ref)
    weight = jnp.where(first, gates_ref[0:1, :], gates_ref[1:2, :])

    def split(mask):
        w = jnp.where(mask, weight, 0.0).T
        high = w.astype(BF16)
        return high, (w - high.astype(F32)).astype(BF16)

    def weigh(pair, data):
        return jnp.dot(pair[0], data, preferred_element_type=F32) + jnp.dot(pair[1], data, preferred_element_type=F32)

    main_pick = split(slot == r8)
    fold_pick = [split((slot == 8 + r8 // 4) & (r8 % 4 == p)) for p in range(4)]
    for j in range(2):
        extra = back[j, :, :, 1024:1280].astype(F32).reshape(256, 256).astype(BF16)
        for p in range(4):
            at = j * 1024 + p * 256
            data = back[j, :, :, p * 256:(p + 1) * 256].astype(F32).reshape(256, 256).astype(BF16)
            moe = weigh(main_pick, data) + weigh(fold_pick[p], extra)
            out_ref[:, at:at + 256] = (stream_ref[:, at:at + 256] + moe).astype(BF16)

    drain_attention()
    for c in heads:
        c.wait_send()
    for c in range(CHUNKS - 3, CHUNKS):
        counted(8, sd.at[c], rd.at[c]).wait_send()

    def drain(c, carry):
        for k in range(2):
            pass_on(k, c).wait_send()
            second_hop(k, c).wait_send()
        for k in range(3):
            act_to(k, c).wait_send()
        return carry

    lax.fori_loop(0, CHUNKS, drain, 0)


def unfold(extra, p):
    want = 4 * lax.broadcasted_iota(jnp.int32, (16, 64), 0) + p == lax.broadcasted_iota(jnp.int32, (16, 64), 1)
    return jnp.dot(jnp.where(want, 1.0, 0.0).astype(BF16), extra, preferred_element_type=F32).astype(BF16)


def refold(rows, p):
    want = 4 * lax.broadcasted_iota(jnp.int32, (64, 16), 1) + p == lax.broadcasted_iota(jnp.int32, (64, 16), 0)
    return jnp.dot(jnp.where(want, 1.0, 0.0).astype(BF16), rows, preferred_element_type=F32)


def body(resid, queries, keys, values, norm_gain, expert_ids, gate_weights, w_gate, w_up, w_down):
    dma = pltpu.SemaphoreType.DMA
    hidden = w_gate.shape[2]
    return pl.pallas_call(
        layer_kernel,
        out_shape=jax.ShapeDtypeStruct((128, 2048), BF16),
        in_specs=[ANY, ANY, ANY, ANY, VMEM, VMEM, VMEM, ANY, ANY, ANY],
        out_specs=VMEM,
        scratch_shapes=[
            pltpu.VMEM((4, 128, 4 * HD), BF16),
            pltpu.VMEM((16, 4, 2, 128, HD), BF16),
            pltpu.VMEM((4, 512, HD), F32),
            pltpu.VMEM((4, 512, 2 * HD), F32),
            pltpu.VMEM((4, 128, 512), BF16),
            pltpu.VMEM((4, 128, 512), BF16),
            pltpu.VMEM((128, 2048), BF16),
            pltpu.VMEM((128, 2048), F32),
            pltpu.VMEM((128, 128), F32),
            pltpu.VMEM((128, 128), F32),
            pltpu.VMEM((2, 32, 8, 1280), BF16),
            pltpu.VMEM((4, 64, 8, 1280), BF16),
            pltpu.VMEM((4096, hidden), BF16),
            pltpu.VMEM((4096, hidden), BF16),
            pltpu.VMEM((4, hidden, 1024), BF16),
            pltpu.VMEM((4, CHUNKS, 640 // CHUNKS, hidden), BF16),
            pltpu.VMEM((64, 8, 1280), BF16),
            pltpu.VMEM((2, 32, 8, 1280), BF16),
            dma((3, 2)), dma((3, 2)), dma((3,)), dma((3,)),
            dma((4, 4)), dma((4, 4)), dma((4, 4)), dma((4, 4)),
            dma((5, 2)), dma((5, 2)), dma((5, 2)), dma((5, 2)),
            dma((3,)), dma((3,)), dma((3,)), dma((3,)), dma((4,)),
            dma((3,)), dma((3,)), dma, dma, dma((CHUNKS,)), dma((CHUNKS,)),
            dma((2, CHUNKS)), dma((2, CHUNKS)), dma((2, CHUNKS)), dma((2, CHUNKS)),
            dma((3, CHUNKS)), dma((3, CHUNKS)), dma((CHUNKS,)), dma((CHUNKS,)), dma((6,)),
        ],
        compiler_params=pltpu.CompilerParams(
            collective_id=0, has_side_effects=True, vmem_limit_bytes=VMEM_BYTES
        ),
    )(
        queries, keys, values, resid, norm_gain.reshape(1, -1), expert_ids.T, gate_weights.T, w_gate, w_up, w_down
    )


def solution(mesh):
    in_specs = (
        P(("rep", "dev"), None),
        P(("rep", "dev"), "sec"),
        P(("rep", "dev"), "sec"),
        P(("rep", "dev"), "sec"),
        P(),
        P(("rep", "dev"), None),
        P(("rep", "dev"), None),
        P("dev", None, "sec"),
        P("dev", None, "sec"),
        P("dev", "sec", None),
    )
    out_specs = P(("rep", "dev"), "sec")
    return jax.shard_map(body, mesh=mesh, in_specs=in_specs, out_specs=out_specs, check_vma=False)
```

```python
import math

import jax
import jax.numpy as jnp
from jax import lax
from jax.experimental import pallas as pl
from jax.experimental.pallas import tpu as pltpu
from jax.sharding import PartitionSpec as P

HD = 128
MESH = pl.DeviceIdType.MESH
F32 = jnp.float32
BF16 = jnp.bfloat16
VMEM_BYTES = 58 * 1024 * 1024
ANY = pl.BlockSpec(memory_space=pl.ANY)
VMEM = pl.BlockSpec(memory_space=pltpu.VMEM)


def rcopy(src, dst, send_sem, recv_sem, device_id):
    return pltpu.make_async_remote_copy(
        src_ref=src,
        dst_ref=dst,
        send_sem=send_sem,
        recv_sem=recv_sem,
        device_id=device_id,
        device_id_type=MESH,
    )


def coords():
    me = lax.axis_index("dev")
    return me, me // 16, (me // 4) % 4, me % 4


def twin(me):
    return me + 1 - 2 * (me % 2)


def square(me, sec):
    j = me % 2
    partners = ({"dev": twin(me)}, {"sec": 1 - sec}, {"dev": twin(me), "sec": 1 - sec})
    quarters = (2 * sec + 1 - j, 2 * (1 - sec) + j, 2 * (1 - sec) + 1 - j)
    return partners, quarters, 2 * sec + j


def greet(me, sec, rep):
    barrier = pltpu.get_barrier_semaphore()

    def one(i, carry):
        pl.semaphore_signal(barrier, inc=1, device_id={"dev": (me + i) % 64}, device_id_type=MESH)
        return carry

    lax.fori_loop(1, 64, one, 0)
    for peer in ({"sec": 1 - sec}, {"sec": 1 - sec, "dev": twin(me)}, {"rep": 1 - rep}):
        pl.semaphore_signal(barrier, inc=1, device_id=peer, device_id_type=MESH)
    pl.semaphore_wait(barrier, 66)


def one_hot(ids_ref):
    row = lax.broadcasted_iota(jnp.int32, (256, 128), 0)
    expert = row // 8
    first = expert == ids_ref[0:1, :]
    second = expert == ids_ref[1:2, :]
    named = jnp.where(first | second, 1.0, 0.0)
    before = lax.broadcasted_iota(jnp.int32, (128, 128), 0) < lax.broadcasted_iota(jnp.int32, (128, 128), 1)
    slot = jnp.dot(named.astype(BF16), jnp.where(before, 1.0, 0.0).astype(BF16), preferred_element_type=F32)
    slot = jnp.where(named > 0.5, slot, -1.0).astype(jnp.int32)
    return row % 8, first, slot


def attend(
    q_ref, k_ref, v_ref, wd_ref, ao, wd, q_vm, kv_vm, m_ref, acc_ref,
    s1, r1, sq, rq, sa, ra, sb, rb, sap, rap, sbp, rbp, sw, rw, st, rt, lsem,
):
    me, x, zh, y = coords()
    pos = x * 4 + y
    sec = lax.axis_index("sec")
    rep = lax.axis_index("rep")
    partners, quarters, q_me = square(me, sec)
    sibling = {"rep": 1 - rep}
    fold = math.log2(math.e) / math.sqrt(HD)

    def at(xx, zz, yy):
        return {"dev": ((xx + 4) % 4) * 16 + zz * 4 + (yy + 4) % 4}

    def cols(j, w):
        return pl.ds(pl.multiple_of(j * w, w), w)

    own = [
        pltpu.make_async_copy(k_ref.at[:, cols(zh, HD)], kv_vm.at[pos, zh, 0], lsem.at[0]),
        pltpu.make_async_copy(v_ref.at[:, cols(zh, HD)], kv_vm.at[pos, zh, 1], lsem.at[1]),
        pltpu.make_async_copy(q_ref.at[:, cols(zh, 4 * HD)], q_vm.at[zh], lsem.at[2]),
        pltpu.make_async_copy(wd_ref.at[0, :, cols(q_me, 1024)], wd.at[q_me], lsem.at[3]),
    ]
    for c in own:
        c.start()
    greet(me, sec, rep)

    hid = wd_ref.shape[1] // 2
    mine = pl.ds(pl.multiple_of(rep * hid, hid), hid)
    other = pl.ds(pl.multiple_of((1 - rep) * hid, hid), hid)

    def down(k):
        return rcopy(wd_ref.at[0, mine, cols(quarters[k], 1024)], wd.at[q_me, mine], sw.at[k], rw.at[k], partners[k])

    def share(k):
        part = wd.at[quarters[k], mine]
        return rcopy(part, part, st.at[k], rt.at[k], sibling)

    first = []
    for d in range(1, 4):
        j = (zh + d) % 4
        first.append(rcopy(k_ref.at[:, cols(j, HD)], kv_vm.at[pos, zh, 0], s1.at[d - 1, 0], r1.at[d - 1, 0], at(x, j, y)))
        first.append(rcopy(v_ref.at[:, cols(j, HD)], kv_vm.at[pos, zh, 1], s1.at[d - 1, 1], r1.at[d - 1, 1], at(x, j, y)))
    for d in range(1, 4):
        j = (zh + d) % 4
        first.append(rcopy(q_ref.at[:, cols(j, 4 * HD)], q_vm.at[zh], sq.at[d - 1], rq.at[d - 1], at(x, j, y)))
    for c in first:
        c.start()
    m_ref[...] = jnp.full(m_ref.shape, -1e30, F32)
    acc_ref[...] = jnp.zeros(acc_ref.shape, F32)
    own[0].wait()
    own[1].wait()
    for d in range(1, 4):
        src = (zh + 4 - d) % 4
        for w in range(2):
            rcopy(kv_vm.at[pos, src, w], kv_vm.at[pos, src, w], s1.at[d - 1, w], r1.at[d - 1, w], at(x, src, y)).wait_recv()

    def place(ex, ey):
        return ((x + 4 - ex) % 4) * 4 + (y + 4 - ey) % 4

    def copy_of(h, ex, ey, p, dest):
        ref = kv_vm.at[p, pl.ds(2 * h, 2)]
        send, recv = (sa, ra) if h == 0 else (sb, rb)
        return rcopy(ref, ref, send.at[ex, ey], recv.at[ex, ey], dest)

    def piece_of(h, ex, ey, part, p, dest):
        ref = kv_vm.at[p, 2 * h + part]
        send, recv = (sap, rap) if h == 0 else (sbp, rbp)
        line = ey if h == 1 else ex
        return rcopy(ref, ref, send.at[line, part], recv.at[line, part], dest)

    def axis_to(h, second, step):
        return at(x + step, zh, y) if (h == 0) != second else at(x, zh, y + step)

    sends = []

    def go(make, *rest):
        make(*rest).start()
        sends.append((make, rest))

    def index(h, a, b):
        return (a, b) if h == 0 else (b, a)

    def arrived(h, a, b):
        ex, ey = index(h, a, b)
        copy_of(h, ex, ey, place(ex, ey), partners[0]).wait_recv()

    def leg_copy(h, a, b, step):
        ex, ey = index(h, a, b)
        return copy_of(h, ex, ey, place(*index(h, a, 0)), axis_to(h, True, step))

    def second_leg(h, a):
        for b, step in ((1, 1), (3, -1)):
            go(leg_copy, h, a, b, step)

    def piece_copy(h, a, b):
        part, step = (0, 1) if b == 1 else (1, -1)
        ex, ey = index(h, a, 2)
        return piece_of(h, ex, ey, part, place(*index(h, a, b)), axis_to(h, True, step))

    def relay_second(h, a, b):
        go(piece_copy, h, a, b)

    def pieces(h, a):
        ex, ey = index(h, a, 2)
        for part in range(2):
            piece_of(h, ex, ey, part, place(ex, ey), partners[0]).wait_recv()

    def first_piece(h, part, p, dest):
        ref = kv_vm.at[p, 2 * h + part]
        send, recv = (sap, rap) if h == 0 else (sbp, rbp)
        return rcopy(ref, ref, send.at[4, part], recv.at[4, part], dest)

    def start_copy(h, a, step):
        ex, ey = index(h, a, 0)
        return copy_of(h, ex, ey, pos, axis_to(h, False, step))

    def turn_copy(h, a, part, step):
        return first_piece(h, part, place(*index(h, a, 0)), axis_to(h, False, step))

    for h in range(2):
        for a, step in ((1, 1), (3, -1)):
            go(start_copy, h, a, step)
    for h in range(2):
        second_leg(h, 0)

    def absorb(p0, p1):
        k = jnp.concatenate([kv_vm[p0, :, 0].reshape(512, HD), kv_vm[p1, :, 0].reshape(512, HD)], axis=0)
        v = jnp.concatenate([kv_vm[p0, :, 1].reshape(512, HD), kv_vm[p1, :, 1].reshape(512, HD)], axis=0)
        v_one = jnp.concatenate([v, jnp.ones((1024, HD), BF16)], axis=1)
        for h in range(4):
            for r in range(2):
                rows = slice(r * 256, (r + 1) * 256)
                q = q_vm[2 * r:2 * r + 2, :, h * HD:(h + 1) * HD].reshape(256, HD)
                s = lax.dot_general(q, k, (((1,), (1,)), ((), ())), preferred_element_type=F32)
                m_old = m_ref[h, rows]
                m_new = jnp.maximum(m_old, jnp.max(s, axis=1, keepdims=True))
                m_ref[h, rows] = m_new
                alpha = jnp.exp2((m_old - m_new) * fold)
                p = jnp.exp2((s - m_new[:, :1]) * fold)
                added = jnp.dot(p.astype(BF16), v_one, preferred_element_type=F32)
                acc_ref[h, rows] = acc_ref[h, rows] * alpha[:, :1] + added

    for h in range(2):
        for a, step, part in ((1, 1, 0), (3, -1, 1)):
            arrived(h, a, 0)
            go(turn_copy, h, a, part, step)
            second_leg(h, a)
    for h in range(2):
        for b in (1, 3):
            arrived(h, 0, b)
            relay_second(h, 0, b)
    own[2].wait()
    for d in range(1, 4):
        src = (zh + 4 - d) % 4
        rcopy(q_vm.at[src], q_vm.at[src], sq.at[d - 1], rq.at[d - 1], at(x, src, y)).wait_recv()

    order = ((0, 0), (0, 1), (0, 3), (1, 0), (3, 0), (1, 1), (1, 3), (3, 1), (3, 3), (2, 0), (0, 2), (2, 1), (2, 3), (1, 2), (3, 2), (2, 2))

    def step(i, carry):
        def look(values):
            out = 0
            for n, value in enumerate(values):
                if value:
                    out = out + jnp.where(i == n, value, 0)
            return out

        @pl.when(i == 2)
        def _():
            for h in range(2):
                for part in range(2):
                    first_piece(h, part, place(*index(h, 2, 0)), partners[0]).wait_recv()
                second_leg(h, 2)
            for h in range(2):
                for a in (1, 3):
                    for b in (1, 3):
                        arrived(h, a, b)
                        relay_second(h, a, b)

        @pl.when(i == 3)
        def _():
            for h in range(2):
                for b in (1, 3):
                    arrived(h, 2, b)
                    relay_second(h, 2, b)

        @pl.when(i == 0)
        def _():
            down(1).start()

        @pl.when(i == 4)
        def _():
            down(0).start()
            pieces(1, 0)

        @pl.when(i == 5)
        def _():
            down(2).start()
            pieces(0, 0)
            pieces(1, 1)

        @pl.when(i == 6)
        def _():
            pieces(1, 3)
            pieces(0, 1)

        @pl.when(i == 7)
        def _():
            pieces(0, 3)
            pieces(0, 2)
            pieces(1, 2)

        p0 = place(look([order[2 * n][0] for n in range(8)]), look([order[2 * n][1] for n in range(8)]))
        p1 = place(look([order[2 * n + 1][0] for n in range(8)]), look([order[2 * n + 1][1] for n in range(8)]))
        absorb(p0, p1)
        return carry

    lax.fori_loop(0, 8, step, 0)
    for h in range(4):
        total = acc_ref[h]
        ao[:, :, h * HD:(h + 1) * HD] = (total[:, :HD] / total[:, HD:]).astype(BF16).reshape(4, 128, HD)

    def come_down():
        for k in range(3):
            part = wd.at[quarters[k], mine]
            rcopy(part, part, sw.at[k], rw.at[k], partners[k]).wait_recv()
            share(k).start()

    def finish():
        own[3].wait()
        for k in range(3):
            part = wd.at[quarters[k], other]
            rcopy(part, part, st.at[k], rt.at[k], sibling).wait_recv()

    def drain():
        for c in first:
            c.wait_send()
        for make, rest in sends:
            make(*rest).wait_send()
        for k in range(3):
            down(k).wait_send()
            share(k).wait_send()

    return come_down, finish, drain


CHUNKS = 8


def layer_kernel(
    q_ref, k_ref, v_ref, resid_ref, gain_ref, ids_ref, gates_ref, wg_ref, wu_ref, wd_ref, out_ref,
    q_vm, kv_vm, m_ref, acc_ref, ao,
    att, rbuf, stream_ref, ssq, ssq_in, sbuf, xall, wg, wu, wd, acts, outgoing, back,
    s1, r1, sq, rq, sa, ra, sb, rb, sap, rap, sbp, rbp, sw, rw, st, rt, lsem_a,
    sh_heads, rh_heads, ss, rs, sd, rd, sf, rf, sh, rh, sr, rr, lsem,
):
    me, x, zh, y = coords()
    sec = lax.axis_index("sec")
    j_me = me % 2
    e_me = me // 2
    side = jnp.where((y == 0) | (y == 3), 0, 1)
    low = side * 4 + (zh % 2) * 2 + y // 2
    own_slot = (me // 8) * 8 + low
    partners, quarters, q_me = square(me, sec)
    half = pl.ds(pl.multiple_of(sec * 2048, 2048), 2048)
    fetch = pltpu.make_async_copy(resid_ref.at[:, half], rbuf, lsem.at[0])
    fetch.start()
    weights = [
        pltpu.make_async_copy(wg_ref.at[0], wg, lsem.at[3]),
        pltpu.make_async_copy(wu_ref.at[0], wu, lsem.at[4]),
    ]
    for c in weights:
        c.start()
    come_down, finish_down, drain_attention = attend(
        q_ref, k_ref, v_ref, wd_ref, ao, wd, q_vm, kv_vm, m_ref, acc_ref,
        s1, r1, sq, rq, sa, ra, sb, rb, sap, rap, sbp, rbp, sw, rw, st, rt, lsem_a,
    )
    keep = pltpu.make_async_copy(ao.at[zh], att.at[zh], lsem.at[1])
    keep.start()
    heads = []
    for d in range(1, 4):
        j = (zh + d) % 4
        heads.append(rcopy(ao.at[j], att.at[zh], sh_heads.at[d - 1], rh_heads.at[d - 1], {"dev": x * 16 + j * 4 + y}))
    for c in heads:
        c.start()

    r8, first, slot = one_hot(ids_ref)
    pick = jnp.where(slot == r8, 1.0, 0.0).astype(BF16)
    fold = [jnp.where((slot == 8 + r8 // 4) & (r8 % 4 == p), 1.0, 0.0).astype(BF16) for p in range(4)]

    fetch.wait()
    keep.wait()
    for d in range(1, 4):
        src = (zh + 4 - d) % 4
        rcopy(ao.at[src], att.at[src], sh_heads.at[d - 1], rh_heads.at[d - 1], {"dev": x * 16 + src * 4 + y}).wait_recv()
    total = jnp.zeros((128, 1), F32)
    for g in range(4):
        part = rbuf[:, g * 512:(g + 1) * 512].astype(F32) + att[g].astype(F32)
        stream_ref[:, g * 512:(g + 1) * 512] = part
        total = total + jnp.sum(part * part, axis=1, keepdims=True)
    ssq[...] = jnp.broadcast_to(total, (128, 128))
    cross = rcopy(ssq, ssq_in, ss, rs, {"sec": 1 - sec})
    cross.start()
    cross.wait()
    scale = lax.rsqrt((ssq[:, :1] + ssq_in[:, :1]) * (1.0 / 4096) + 1e-06)
    for j in range(2):
        normed = []
        for p in range(4):
            at = j * 1024 + p * 256
            g = gain_ref[:, pl.ds(pl.multiple_of(sec * 2048 + at, 256), 256)]
            normed.append((stream_ref[:, at:at + 256] * scale * g).astype(BF16))
        extra = jnp.zeros((256, 256), F32)
        for p in range(4):
            main = jnp.dot(pick, normed[p], preferred_element_type=F32)
            sbuf[j, :, :, p * 256:(p + 1) * 256] = main.reshape(32, 8, 256).astype(BF16)
            extra = extra + jnp.dot(fold[p], normed[p], preferred_element_type=F32)
        sbuf[j, :, :, 1024:1280] = extra.reshape(32, 8, 256).astype(BF16)

    def ahead(c):
        return ((x + c // 2) % 4) * 16 + ((zh // 2 + c) % 2) * 8

    def behind(c):
        return ((x + 4 - c // 2) % 4) * 16 + ((zh // 2 + c) % 2) * 8

    def slot_device(slot):
        s, zl, w = (slot // 4) % 2, (slot // 2) % 2, slot % 2
        return (slot // 8) * 8 + zl * 4 + s + w * (3 - 2 * s)

    both = pl.ds(2 * sec, 2)
    far = pl.ds(2 * (1 - sec), 2)

    def rows_to(t, c):
        base = ahead(c)
        turn = (zh + t // 2) % 2
        pair = (y // 2 + t) % 2
        entry = jnp.where(pair == y // 2, y, 3 - y)
        return rcopy(
            sbuf.at[:, base // 2 + turn * 2 + pair], xall.at[both, own_slot], sd.at[c], rd.at[c], {"dev": base + turn * 4 + entry}
        )

    def send_rows(c, start):
        for t in range(start, 4):
            rows_to(t, c).start()

    def near(c):
        return pl.ds(behind(c) + side * 4, 4)

    def off_side(c):
        return pl.ds(behind(c) + (1 - side) * 4, 4)

    def counted(n, send_sem, recv_sem):
        ref = outgoing.at[pl.ds(0, n)]
        return rcopy(ref, ref, send_sem, recv_sem, partners[0])

    def pass_on(k, c):
        ref = xall.at[far if k == 2 else both, near(c)]
        return rcopy(ref, ref, sf.at[k, c], rf.at[k, c], partners[1 if k == 1 else 0])

    def came(k, c):
        ref = xall.at[both if k == 0 else far, near(c) if k == 1 else off_side(c)]
        return rcopy(ref, ref, sf.at[k, c], rf.at[k, c], partners[0])

    def act_to(k, c):
        ref = acts.at[quarters[1] if k == 2 else q_me, c]
        return rcopy(ref, ref, sh.at[k, c], rh.at[k, c], partners[1 if k == 1 else 0])

    def act_from(k, c):
        ref = acts.at[quarters[k], c]
        return rcopy(ref, ref, sh.at[k, c], rh.at[k, c], partners[k])

    def result_to(dest, c):
        return rcopy(outgoing.at[dest], back.at[j_me, e_me], sr.at[c], rr.at[c], {"dev": slot_device(dest)})

    own_rows = pltpu.make_async_copy(sbuf.at[:, e_me], xall.at[both, own_slot], lsem.at[2])
    own_rows.start()
    own_back = pltpu.make_async_copy(outgoing.at[own_slot], back.at[j_me, e_me], lsem.at[5])
    send_rows(0, 1)
    send_rows(1, 0)
    own_rows.wait()
    for c in weights:
        c.wait()
    come_down()

    def relay(c):
        @pl.when(c == 0)
        def _():
            ref = xall.at[both, pl.ds(0, 3)]
            rcopy(ref, ref, sd.at[0], rd.at[0], partners[0]).wait_recv()

        @pl.when(c > 0)
        def _():
            ref = xall.at[both, near(c)]
            rcopy(ref, ref, sd.at[c], rd.at[c], partners[0]).wait_recv()

        pass_on(1, c).start()
        pass_on(0, c).start()

        @pl.when(c == 0)
        def _():
            counted(6, sd.at[0], rd.at[0]).wait_send()
            send_rows(2, 0)

        @pl.when((c > 0) & (c + 2 < CHUNKS))
        def _():
            counted(8, sd.at[c], rd.at[c]).wait_send()
            send_rows(c + 2, 0)

    def relay_far(c):
        came(1, c).wait_recv()
        pass_on(2, c).start()

    def hidden(c):
        came(0, c).wait_recv()
        came(2, c).wait_recv()
        rows = []
        for q in range(4):
            data = xall[q, pl.ds(behind(c), 8)].astype(F32).reshape(64, 1280).astype(BF16)
            over = jnp.concatenate([unfold(data[:, 1024:], p) for p in range(4)], axis=1)
            rows.append(jnp.concatenate([data[:, :1024], over], axis=0))
        rows = jnp.concatenate(rows, axis=1)
        g = jnp.dot(rows, wg[...], preferred_element_type=F32)
        u = jnp.dot(rows, wu[...], preferred_element_type=F32)
        acts[q_me, c] = (g / (1.0 + jnp.exp(-g)) * u).astype(BF16)
        act_to(1, c).start()
        act_to(0, c).start()

    def act_on(c):
        act_from(1, c).wait_recv()
        act_to(2, c).start()

    def output(c):
        @pl.when(c == 0)
        def _():
            finish_down()

        act_from(0, c).wait_recv()
        act_from(2, c).wait_recv()
        part = jnp.dot(acts[0, c], wd[0], preferred_element_type=F32)
        for q in range(1, 4):
            part = part + jnp.dot(acts[q, c], wd[q], preferred_element_type=F32)
        outgoing[pl.ds(behind(c), 8), :, 0:1024] = part[:64].reshape(8, 8, 1024).astype(BF16)
        over = part[64:].astype(BF16)
        extra = refold(over[:, 0:256], 0)
        for p in range(1, 4):
            extra = extra + refold(over[:, p * 256:(p + 1) * 256], p)
        outgoing[pl.ds(behind(c), 8), :, 1024:1280] = extra.reshape(8, 8, 256).astype(BF16)

        @pl.when(c == 0)
        def _():
            own_back.start()

        def one(t, carry):
            result_to(behind(c) + (low + t) % 8, c).start()
            return carry

        lax.fori_loop(jnp.where(c == 0, 1, 0), 8, one, 0)

    def stage(c, carry):
        @pl.when(c < CHUNKS)
        def _():
            relay(c)

        @pl.when((c >= 1) & (c < CHUNKS + 1))
        def _():
            relay_far(c - 1)

        @pl.when((c >= 3) & (c < CHUNKS + 3))
        def _():
            act_on(c - 3)

        @pl.when(c >= 4)
        def _():
            output(c - 4)

        @pl.when((c >= 2) & (c < CHUNKS + 2))
        def _():
            hidden(c - 2)

        return carry

    lax.fori_loop(0, CHUNKS + 4, stage, 0)
    own_back.wait()
    counted(7, sr.at[0], rr.at[0]).wait_send()
    ref = back.at[0, pl.ds(0, 7)]
    rcopy(ref, ref, sr.at[0], rr.at[0], partners[0]).wait_recv()

    def arrive(c, carry):
        ref = back.at[:, pl.ds(ahead(c) // 2, 4)]
        rcopy(ref, ref, sr.at[c], rr.at[c], partners[0]).wait_recv()
        counted(8, sr.at[c], rr.at[c]).wait_send()
        return carry

    lax.fori_loop(1, CHUNKS, arrive, 0)

    r8, first, slot = one_hot(ids_ref)
    weight = jnp.where(first, gates_ref[0:1, :], gates_ref[1:2, :])

    def split(mask):
        w = jnp.where(mask, weight, 0.0).T
        high = w.astype(BF16)
        return high, (w - high.astype(F32)).astype(BF16)

    def weigh(pair, data):
        return jnp.dot(pair[0], data, preferred_element_type=F32) + jnp.dot(pair[1], data, preferred_element_type=F32)

    main_pick = split(slot == r8)
    fold_pick = [split((slot == 8 + r8 // 4) & (r8 % 4 == p)) for p in range(4)]
    for j in range(2):
        extra = back[j, :, :, 1024:1280].astype(F32).reshape(256, 256).astype(BF16)
        for p in range(4):
            at = j * 1024 + p * 256
            data = back[j, :, :, p * 256:(p + 1) * 256].astype(F32).reshape(256, 256).astype(BF16)
            moe = weigh(main_pick, data) + weigh(fold_pick[p], extra)
            out_ref[:, at:at + 256] = (stream_ref[:, at:at + 256] + moe).astype(BF16)

    drain_attention()
    for c in heads:
        c.wait_send()
    for c in range(CHUNKS - 2, CHUNKS):
        counted(8, sd.at[c], rd.at[c]).wait_send()

    def drain(c, carry):
        for k in range(3):
            pass_on(k, c).wait_send()
            act_to(k, c).wait_send()
        return carry

    lax.fori_loop(0, CHUNKS, drain, 0)


def unfold(extra, p):
    want = 4 * lax.broadcasted_iota(jnp.int32, (16, 64), 0) + p == lax.broadcasted_iota(jnp.int32, (16, 64), 1)
    return jnp.dot(jnp.where(want, 1.0, 0.0).astype(BF16), extra, preferred_element_type=F32).astype(BF16)


def refold(rows, p):
    want = 4 * lax.broadcasted_iota(jnp.int32, (64, 16), 1) + p == lax.broadcasted_iota(jnp.int32, (64, 16), 0)
    return jnp.dot(jnp.where(want, 1.0, 0.0).astype(BF16), rows, preferred_element_type=F32)


def body(resid, queries, keys, values, norm_gain, expert_ids, gate_weights, w_gate, w_up, w_down):
    dma = pltpu.SemaphoreType.DMA
    hidden = w_gate.shape[2]
    return pl.pallas_call(
        layer_kernel,
        out_shape=jax.ShapeDtypeStruct((128, 2048), BF16),
        in_specs=[ANY, ANY, ANY, ANY, VMEM, VMEM, VMEM, ANY, ANY, ANY],
        out_specs=VMEM,
        scratch_shapes=[
            pltpu.VMEM((4, 128, 4 * HD), BF16),
            pltpu.VMEM((16, 4, 2, 128, HD), BF16),
            pltpu.VMEM((4, 512, HD), F32),
            pltpu.VMEM((4, 512, 2 * HD), F32),
            pltpu.VMEM((4, 128, 512), BF16),
            pltpu.VMEM((4, 128, 512), BF16),
            pltpu.VMEM((128, 2048), BF16),
            pltpu.VMEM((128, 2048), F32),
            pltpu.VMEM((128, 128), F32),
            pltpu.VMEM((128, 128), F32),
            pltpu.VMEM((2, 32, 8, 1280), BF16),
            pltpu.VMEM((4, 64, 8, 1280), BF16),
            pltpu.VMEM((4096, hidden), BF16),
            pltpu.VMEM((4096, hidden), BF16),
            pltpu.VMEM((4, hidden, 1024), BF16),
            pltpu.VMEM((4, CHUNKS, 640 // CHUNKS, hidden), BF16),
            pltpu.VMEM((64, 8, 1280), BF16),
            pltpu.VMEM((2, 32, 8, 1280), BF16),
            dma((3, 2)), dma((3, 2)), dma((3,)), dma((3,)),
            dma((4, 4)), dma((4, 4)), dma((4, 4)), dma((4, 4)),
            dma((5, 2)), dma((5, 2)), dma((5, 2)), dma((5, 2)),
            dma((3,)), dma((3,)), dma((3,)), dma((3,)), dma((4,)),
            dma((3,)), dma((3,)), dma, dma, dma((CHUNKS,)), dma((CHUNKS,)),
            dma((3, CHUNKS)), dma((3, CHUNKS)),
            dma((3, CHUNKS)), dma((3, CHUNKS)), dma((CHUNKS,)), dma((CHUNKS,)), dma((6,)),
        ],
        compiler_params=pltpu.CompilerParams(
            collective_id=0, has_side_effects=True, vmem_limit_bytes=VMEM_BYTES
        ),
    )(
        queries, keys, values, resid, norm_gain.reshape(1, -1), expert_ids.T, gate_weights.T, w_gate, w_up, w_down
    )


def solution(mesh):
    in_specs = (
        P(("rep", "dev"), None),
        P(("rep", "dev"), "sec"),
        P(("rep", "dev"), "sec"),
        P(("rep", "dev"), "sec"),
        P(),
        P(("rep", "dev"), None),
        P(("rep", "dev"), None),
        P("dev", None, "sec"),
        P("dev", None, "sec"),
        P("dev", "sec", None),
    )
    out_specs = P(("rep", "dev"), "sec")
    return jax.shard_map(body, mesh=mesh, in_specs=in_specs, out_specs=out_specs, check_vma=False)
```
